32 devices in a mesh: seq: 8 (over z, core), head: 4 (over y, x).
Axes of the slice: x: 2, y: 2, z: 4, core: 2. Of those that a mesh axis runs over, the one named last changes fastest.
Arguments:
- inputs: bfloat16 [2, 2048, 2048], P(None, ('seq', 'head')), may hold values from -6 to 6
- doc_lengths: int32 [2, 16], replicated, may hold values from 1 to 1920, 2048 in all within a row
- ln_gain: float32 [2048], P(('seq', 'head')), may hold values from 0.5 to 1.5
- ln_bias: float32 [2048], P(('seq', 'head')), may hold values from -1.25 to 1.25
- w_qkv: float32 [2048, 6144], P(('seq', 'head')), may hold values from -0.125 to 0.125
- b_qkv: float32 [6144], P(('seq', 'head')), may hold values from -0.1875 to 0.1875
- w_out: float32 [2048, 2048], P(('seq', 'head')), may hold values from -0.75 to 0.75
- b_out: float32 [2048], P(('seq', 'head')), may hold values from -1.25 to 1.25
- w_fc1: float32 [2048, 8192], P(('seq', 'head')), may hold values from -0.125 to 0.125
- b_fc1: float32 [8192], P(('seq', 'head')), may hold values from -1.75 to 1.75
- w_fc2: float32 [8192, 2048], P(('seq', 'head')), may hold values from -0.0625 to 0.0625
- b_fc2: float32 [2048], P(('seq', 'head')), may hold values from -1.25 to 1.25
- cotangent: bfloat16 [2, 2048, 2048], P(None, ('seq', 'head')), may hold values from -6 to 6
Outputs:
- output: bfloat16 [2, 2048, 2048], P(None, ('seq', 'head'))
- grad_input: bfloat16 [2, 2048, 2048], P(None, ('seq', 'head'))
- grad_ln_gain: float32 [2048], P(('seq', 'head'))
- grad_ln_bias: float32 [2048], P(('seq', 'head'))
- grad_w_qkv: float32 [2048, 6144], P(('seq', 'head'))
- grad_b_qkv: float32 [6144], P(('seq', 'head'))
- grad_w_out: float32 [2048, 2048], P(('seq', 'head'))
- grad_b_out: float32 [2048], P(('seq', 'head'))
- grad_w_fc1: float32 [2048, 8192], P(('seq', 'head'))
- grad_b_fc1: float32 [8192], P(('seq', 'head'))
- grad_w_fc2: float32 [8192, 2048], P(('seq', 'head'))
- grad_b_fc2: float32 [2048], P(('seq', 'head'))
The draws below stay inside these ranges and needn't reach their ends.
Inputs may be any that keep to these rules, and one draw needn't show every extreme that they name: `doc_lengths`: in each row the lengths sum to 2048, and one document has exactly 1920 tokens.
All inputs are finite; a program needn't handle non-finite values.
Results may differ from the reference program's by a relative error of at most 0.011.
Values may be sent and summed in bfloat16 or wider, within the bound.
No kernel may reach another device: no remote copies, remote signals or barrier semaphores. Data moves between devices by JAX's collectives and lax.ppermute only.
A program may use at most 448 MiB of HBM per device.

```python
import math
import jax
import jax.numpy as jnp
import numpy as np
from jax import lax

D = 2048
H = 32
FF = 8192
HD = 64
ROT = 32
SEQS = 2
DOCS = 16
LEN = 2048
LONGEST = 1920


def steps_of(key, dims, split, smallest, largest):
    level = 1.0
    for dim, shards_of in split:
        steps = jax.random.uniform(jax.random.fold_in(jax.random.fold_in(key, 6), dim), (shards_of,), jnp.float32, smallest / len(split), largest / len(split))
        level = level * jnp.repeat(jnp.exp(steps), dims[dim] // shards_of).reshape((-1,) + (1,) * (len(dims) - 1 - dim))
    return level


def profile(count, total, bound, slope):
    portions = [(1 << 20) // math.isqrt(standing ** slope) + 1 for standing in range(2, count + 1)]
    spare, holding = total - bound - (count - 1), [1] * (count - 1)
    while spare > 0:
        free = [i for i in range(count - 1) if holding[i] < bound]
        whole, remaining = sum([portions[i] for i in free]), spare
        for i in free:
            extra = min(bound - holding[i], max(1, remaining * portions[i] // whole), spare)
            holding[i] = holding[i] + extra
            spare = spare - extra
    return np.array([bound] + holding)


def ragged_sizes(stream_key, count, total, most, slope):
    if count == 2:
        one = jax.random.randint(stream_key, (), max(1, total - most), min(most, total - 1) + 1)
        return jnp.stack([one, total - one])
    tallies = jnp.asarray(profile(count, total, most, slope), jnp.int32)
    pairs = (count - 1) // 2
    donor, taker = tallies[1:1 + 2 * pairs:2], tallies[2:2 + 2 * pairs:2]
    slack = jnp.minimum(donor - 1, most - taker)
    passed = jax.random.randint(jax.random.fold_in(stream_key, 1), (pairs,), 0, 1 << 20) % (slack + 1)
    tallies = tallies.at[1:1 + 2 * pairs:2].set(donor - passed).at[2:2 + 2 * pairs:2].set(taker + passed)
    return tallies[jax.random.permutation(jax.random.fold_in(stream_key, 2), count)]


def bell_draw(own_key, shape, scale, most, cuts=(), kind=jnp.bfloat16):
    entries = scale * jax.random.normal(own_key, shape, jnp.float32)
    if cuts:
        entries = entries * steps_of(own_key, shape, cuts, -0.22, 0.18)
    return jnp.clip(entries, -most, most).astype(kind)


def setup_inputs(seed: int = 0) -> dict:
    streams_of = jax.random.split(jax.random.key(seed), 14)
    return {
        "inputs": bell_draw(streams_of[0], (SEQS, LEN, D), 1.0, 6.0, ((1, 32),)),
        "doc_lengths": jax.vmap(lambda own: ragged_sizes(own, DOCS, LEN, LONGEST, 2))(jax.random.split(streams_of[1], SEQS)).reshape((SEQS, DOCS)).astype(jnp.int32),
        "ln_gain": jnp.clip(1.0 + 0.1 * jax.random.normal(streams_of[2], (D,), jnp.float32), 0.5, 1.5),
        "ln_bias": bell_draw(streams_of[3], (D,), 0.2, 1.25, ((0, 32),), jnp.float32),
        "w_qkv": bell_draw(streams_of[4], (D, 3 * D), D ** -0.5, 0.125, ((0, 32),), jnp.float32),
        "b_qkv": bell_draw(streams_of[5], (3 * D,), 0.03, 0.1875, ((0, 32),), jnp.float32),
        "w_out": bell_draw(streams_of[6], (D, D), (max(1, D * 64 // LEN)) ** -0.5, 0.75, ((0, 32),), jnp.float32),
        "b_out": bell_draw(streams_of[7], (D,), 0.2, 1.25, ((0, 32),), jnp.float32),
        "w_fc1": bell_draw(streams_of[8], (D, FF), D ** -0.5, 0.125, ((0, 32),), jnp.float32),
        "b_fc1": bell_draw(streams_of[9], (FF,), 0.3, 1.75, ((0, 32),), jnp.float32),
        "w_fc2": bell_draw(streams_of[10], (FF, D), FF ** -0.5, 0.0625, ((0, 32),), jnp.float32),
        "b_fc2": bell_draw(streams_of[11], (D,), 0.2, 1.25, ((0, 32),), jnp.float32),
        "cotangent": bell_draw(streams_of[12], (SEQS, LEN, D), 1.0, 6.0, ((1, 32),)),
    }


@jax.custom_vjp
def low(v):
    return lax.optimization_barrier(v.astype(jnp.bfloat16)).astype(jnp.float32)

@jax.custom_vjp
def low_back(v):
    return v

def low_keep(v):
    return (low(v), None)

def low_pass(kept, grad):
    return (grad,)

def back_keep(v):
    return (v, None)

def back_low(kept, grad):
    return (low(grad),)
low.defvjp(low_keep, low_pass)
low_back.defvjp(back_keep, back_low)
NEG_FILL = -1e+30
HIGHEST_PRECISION = lax.Precision.HIGHEST

def rotate(field, cosine, sine):
    half_rot = ROT // 2
    first_part = field[..., :half_rot]
    second_part = field[..., half_rot:ROT]
    return jnp.concatenate([first_part * cosine - second_part * sine, second_part * cosine + first_part * sine, field[..., ROT:]], axis=-1)

def rotation_tables(positions):
    half_rot = ROT // 2
    inverse = jnp.power(10000.0, -2.0 * jnp.arange(half_rot, dtype=jnp.float32) / ROT)
    angles = positions.astype(jnp.float32)[:, None] * inverse[None, :]
    return (jnp.cos(angles)[:, None, :], jnp.sin(angles)[:, None, :])

def layer_norm(values, gain_value, shift_value):
    center = values - lax.optimization_barrier(jnp.mean(values, axis=-1, keepdims=True))
    spread = lax.optimization_barrier(jnp.mean(center * center, axis=-1, keepdims=True))
    return center * lax.rsqrt(spread + 1e-05) * gain_value + shift_value

def segment_ids(doc_ends, positions):
    return lax.optimization_barrier(jnp.sum((doc_ends[:, None, :] <= positions[None, :, None]).astype(jnp.int32), axis=2))

def attend(queries, key_in, values, segment):
    positions = jnp.arange(LEN, dtype=jnp.int32)
    query_block = math.gcd(LEN, 512)

    def one_head(head_in):
        head_query, head_key, head_value = head_in

        def one_block(block_in):
            block_query, block_pos, block_seg = block_in
            scores = low_back(jnp.dot(block_query, head_key.T, precision=HIGHEST_PRECISION) * 0.125)
            allowed = (positions[None, :] <= block_pos[:, None]) & (segment[None, :] == block_seg[:, None])
            masked = jnp.where(allowed, scores, NEG_FILL)
            row_top = lax.optimization_barrier(jnp.max(masked, axis=1, keepdims=True))
            weights = jnp.where(allowed, jnp.exp(masked - row_top), 0.0)
            probs_low = low(weights / lax.optimization_barrier(jnp.sum(weights, axis=1, keepdims=True)))
            return jnp.dot(probs_low, head_value, precision=HIGHEST_PRECISION)
        pieces = (head_query.reshape(-1, query_block, HD), positions.reshape(-1, query_block), segment.reshape(-1, query_block))
        return lax.map(jax.checkpoint(one_block), pieces).reshape(LEN, HD)
    heads_in = (jnp.transpose(queries, (1, 0, 2)), jnp.transpose(key_in, (1, 0, 2)), jnp.transpose(values, (1, 0, 2)))
    return jnp.transpose(lax.map(one_head, heads_in), (1, 0, 2))

def reference(inputs, doc_lengths, ln_gain, ln_bias, w_qkv, b_qkv, w_out, b_out, w_fc1, b_fc1, w_fc2, b_fc2, cotangent):
    positions = jnp.arange(LEN, dtype=jnp.int32)
    doc_ends = jnp.cumsum(doc_lengths, axis=1).astype(jnp.int32)
    segments = segment_ids(doc_ends, positions)
    cosine, sine = rotation_tables(positions)

    def layer_forward(params, values_in):
        gain_low, shift_low, qkv_w, qkv_b, out_w, out_b, up_w, up_b, down_w, down_b = [low(member) for member in params]
        normed = low(layer_norm(values_in, gain_low, shift_low)).reshape(-1, D)
        qkv_all = low_back(jnp.dot(normed, qkv_w, precision=HIGHEST_PRECISION) + qkv_b).reshape(SEQS, LEN, 3, H, HD)
        queries = low_back(low(rotate(qkv_all[:, :, 0], cosine, sine)))
        keys_all = low_back(low(rotate(qkv_all[:, :, 1], cosine, sine)))
        values = low_back(low(qkv_all[:, :, 2]))
        mixed = lax.map(lambda members: attend(members[0], members[1], members[2], members[3]), (queries, keys_all, values, segments))
        attended = low_back(low(mixed.reshape(-1, D)))
        branch = low_back(jnp.dot(attended, out_w, precision=HIGHEST_PRECISION) + out_b)
        hidden = low_back(jnp.dot(normed, up_w, precision=HIGHEST_PRECISION) + up_b)
        active = low(jax.nn.gelu(hidden, approximate=True))
        feed = low_back(jnp.dot(active, down_w, precision=HIGHEST_PRECISION) + down_b)
        return values_in + (branch + feed).reshape(SEQS, LEN, D)
    params = (ln_gain, ln_bias, w_qkv, b_qkv, w_out, b_out, w_fc1, b_fc1, w_fc2, b_fc2)
    output, pullback = jax.vjp(layer_forward, params, inputs.astype(jnp.float32))
    grad_params, grad_values = pullback(cotangent.astype(jnp.float32))
    return (output.astype(jnp.bfloat16), grad_values.astype(jnp.bfloat16), grad_params[0], grad_params[1], grad_params[2], grad_params[3], grad_params[4], grad_params[5], grad_params[6], grad_params[7], grad_params[8], grad_params[9])
```

```python
from functools import partial

import jax
import jax.numpy as jnp
from jax import lax
from jax.experimental import pallas as pl
from jax.experimental.pallas import tpu as pltpu
from jax.sharding import PartitionSpec as P

D = 2048
H = 32
HD = 64
ROT = 32


NEG_FILL = -1e30


def from_behind(block, axis, distance):
    devices = range(lax.axis_size(axis))
    route = [(i - distance, i) for i in devices if i - distance in devices]
    return lax.ppermute(block, axis, route)


def from_behind_2(shard, axis, by):
    length = lax.axis_size(axis)
    return lax.ppermute(shard, axis, [(i, (i + by) % length) for i in range(length)])


def rotate(field, cosine, sine):
    half_rot = ROT // 2
    first_part = field[..., :half_rot]
    second_part = field[..., half_rot:ROT]
    return jnp.concatenate(
        [
            first_part * cosine - second_part * sine,
            second_part * cosine + first_part * sine,
            field[..., ROT:],
        ],
        axis=-1,
    )


def rotation_tables(positions):
    half_rot = ROT // 2
    inverse = jnp.power(10000.0, -2.0 * jnp.arange(half_rot, dtype=jnp.float32) / ROT)
    angles = positions.astype(jnp.float32)[:, None] * inverse[None, :]
    return (jnp.cos(angles)[:, None, :], jnp.sin(angles)[:, None, :])


def layer_norm(values, gain_value, shift_value):
    center = values - jnp.mean(values, axis=-1, keepdims=True)
    spread = jnp.mean(center * center, axis=-1, keepdims=True)
    return center * lax.rsqrt(spread + 1e-05) * gain_value + shift_value


def segment_ids(doc_ends, positions):
    return jnp.sum((doc_ends[:, None, :] <= positions[None, :, None]).astype(jnp.int32), axis=2)


def gelu_tanh(values):
    return jax.nn.gelu(values, approximate=True)


def allowed_pairs(query_pos, query_seg, key_pos, key_seg):
    return (key_pos[None, :] <= query_pos[:, None]) & (key_seg[None, :] == query_seg[:, None])


def masked_scores(query_seq, key_seq, allowed):
    raw_scores = (
        jnp.einsum("qhd,khd->hqk", query_seq, key_seq, preferred_element_type=jnp.float32) * 0.125
    )
    return jnp.where(allowed[None], raw_scores, NEG_FILL)


def forward_step(members, query_pos, key_pos):
    top_val, total_val, accum_val, query_seq, kv_seq, query_seg, key_seg = members
    kv_split = kv_seq.reshape(kv_seq.shape[0], 2, -1, HD)
    allowed = allowed_pairs(query_pos, query_seg, key_pos, key_seg)
    masked = masked_scores(query_seq, kv_split[:, 0], allowed)
    new_top = jnp.maximum(top_val, jnp.max(masked, axis=2))
    weights = jnp.where(allowed[None], jnp.exp(masked - new_top[:, :, None]), 0.0)
    factor = jnp.exp(top_val - new_top)
    new_total = total_val * factor + jnp.sum(weights, axis=2)
    new_accum = accum_val * factor[:, :, None] + jnp.einsum(
        "hqk,khd->hqd",
        weights.astype(jnp.bfloat16),
        kv_split[:, 1],
        preferred_element_type=jnp.float32,
    )
    return (new_top, new_total, new_accum)


def backward_step(members, query_pos, key_pos):
    grad_query, grad_kv, query_seq, kv_seq, grad_att, log_total, row_dot, query_seg, key_seg = (
        members
    )
    key_total = kv_seq.shape[0]
    kv_split = kv_seq.reshape(key_total, 2, -1, HD)
    allowed = allowed_pairs(query_pos, query_seg, key_pos, key_seg)
    masked = masked_scores(query_seq, kv_split[:, 0], allowed)
    prob_full = jnp.where(allowed[None], jnp.exp(masked - log_total[:, :, None]), 0.0)
    grad_value = jnp.einsum(
        "hqk,qhd->khd", prob_full.astype(jnp.bfloat16), grad_att, preferred_element_type=jnp.float32
    )
    grad_probs = jnp.einsum(
        "qhd,khd->hqk", grad_att, kv_split[:, 1], preferred_element_type=jnp.float32
    )
    grad_scores = (prob_full * (grad_probs - row_dot[:, :, None])).astype(jnp.bfloat16)
    grad_query = (
        grad_query
        + jnp.einsum(
            "hqk,khd->hqd", grad_scores, kv_split[:, 0], preferred_element_type=jnp.float32
        )
        * 0.125
    )
    grad_key = (
        jnp.einsum("hqk,qhd->khd", grad_scores, query_seq, preferred_element_type=jnp.float32)
        * 0.125
    )
    grad_kv = grad_kv + jnp.stack([grad_key, grad_value], axis=1).reshape(key_total, 2, -1)
    return (grad_query, grad_kv)


def gathered_step(
    inputs,
    doc_lengths,
    ln_gain,
    ln_bias,
    w_qkv,
    b_qkv,
    w_out,
    b_out,
    w_fc1,
    b_fc1,
    w_fc2,
    b_fc2,
    cotangent,
):
    seq_total = inputs.shape[0]
    row_count = inputs.shape[1]
    head_count = lax.axis_size("head")
    seq_devices = lax.axis_size("seq")
    heads_here = H // head_count
    group_width = heads_here * HD
    block_rows = row_count * head_count
    seq_rank = lax.axis_index("seq")
    head_rank = lax.axis_index("head")
    doc_ends = jnp.cumsum(doc_lengths, axis=1)
    token_pos = (seq_rank * head_count + head_rank) * row_count + jnp.arange(
        row_count, dtype=jnp.int32
    )
    query_start = seq_rank * block_rows
    query_pos = query_start + jnp.arange(block_rows, dtype=jnp.int32)
    query_seg = segment_ids(doc_ends, query_pos)
    gathered = (
        lax.all_gather(ln_gain.astype(jnp.bfloat16), ("seq", "head"), axis=0, tiled=True),
        lax.all_gather(ln_bias.astype(jnp.bfloat16), ("seq", "head"), axis=0, tiled=True),
        lax.all_gather(w_qkv.astype(jnp.bfloat16), ("seq", "head"), axis=0, tiled=True),
        lax.all_gather(b_qkv.astype(jnp.bfloat16), ("seq", "head"), axis=0, tiled=True),
        lax.all_gather(w_out.astype(jnp.bfloat16), ("seq", "head"), axis=0, tiled=True),
        lax.all_gather(b_out.astype(jnp.bfloat16), ("seq", "head"), axis=0, tiled=True),
        lax.all_gather(w_fc1.astype(jnp.bfloat16), ("seq", "head"), axis=0, tiled=True),
        lax.all_gather(b_fc1.astype(jnp.bfloat16), ("seq", "head"), axis=0, tiled=True),
        lax.all_gather(w_fc2.astype(jnp.bfloat16), ("seq", "head"), axis=0, tiled=True),
        lax.all_gather(b_fc2.astype(jnp.bfloat16), ("seq", "head"), axis=0, tiled=True),
    )
    (
        gain_full,
        shift_full,
        qkv_weight,
        qkv_bias,
        out_weight,
        out_bias,
        up_weight,
        up_bias,
        down_weight,
        down_bias,
    ) = gathered
    flat_in = inputs.reshape(seq_total * row_count, D).astype(jnp.float32)
    normed, norm_back = jax.vjp(
        layer_norm, flat_in, gain_full.astype(jnp.float32), shift_full.astype(jnp.float32)
    )
    normed_low = normed.astype(jnp.bfloat16)
    qkv_all = (
        jnp.dot(normed_low, qkv_weight, preferred_element_type=jnp.float32)
        + qkv_bias.astype(jnp.float32)
    ).reshape(seq_total, row_count, 3, H, HD)
    cosine, sine = rotation_tables(token_pos)

    def turn_field(field):
        return rotate(field, cosine, sine)

    query_rot, turn_back = jax.vjp(turn_field, qkv_all[:, :, 0])
    key_rot = turn_field(qkv_all[:, :, 1])
    stacked = (
        jnp.stack([query_rot, key_rot, qkv_all[:, :, 2]], axis=2)
        .reshape(seq_total, row_count, 3, D)
        .astype(jnp.bfloat16)
    )
    by_heads = lax.all_to_all(stacked, "head", split_axis=3, concat_axis=1, tiled=True)
    query_heads = by_heads[:, :, 0].reshape(seq_total, block_rows, heads_here, HD)
    kv_heads = by_heads[:, :, 1:3]
    start_state = (
        jnp.full((seq_total, heads_here, block_rows), NEG_FILL, jnp.float32),
        jnp.zeros((seq_total, heads_here, block_rows), jnp.float32),
        jnp.zeros((seq_total, heads_here, block_rows, HD), jnp.float32),
    )
    shard_piece = lax.all_gather(kv_heads, "seq", axis=1, tiled=True)

    def one_turn(turn_index, current):
        kv_block = lax.dynamic_slice_in_dim(shard_piece, turn_index * block_rows, block_rows, 1)
        key_start = turn_index * block_rows
        key_pos = key_start + jnp.arange(block_rows, dtype=jnp.int32)
        key_seg = segment_ids(doc_ends, key_pos)

        def one_compute(state_in):
            return lax.map(
                partial(forward_step, query_pos=query_pos, key_pos=key_pos),
                (state_in[0], state_in[1], state_in[2], query_heads, kv_block, query_seg, key_seg),
            )

        return lax.cond(
            key_start < query_start + block_rows, one_compute, lambda state_in: state_in, current
        )

    top_all, total_all, accum_all = lax.fori_loop(
        0, shard_piece.shape[1] // block_rows, one_turn, start_state
    )
    attn_full = accum_all / total_all[:, :, :, None]
    log_total = top_all + jnp.log(total_all)
    attn_low = (
        jnp.transpose(attn_full, (0, 2, 1, 3))
        .reshape(seq_total, block_rows, group_width)
        .astype(jnp.bfloat16)
    )
    attended = lax.all_to_all(attn_low, "head", split_axis=1, concat_axis=2, tiled=True).reshape(
        seq_total * row_count, D
    )
    branch = jnp.dot(attended, out_weight, preferred_element_type=jnp.float32) + out_bias.astype(
        jnp.float32
    )
    hidden = jnp.dot(normed_low, up_weight, preferred_element_type=jnp.float32) + up_bias.astype(
        jnp.float32
    )
    active, gelu_back = jax.vjp(gelu_tanh, hidden)
    active_low = active.astype(jnp.bfloat16)
    feed = jnp.dot(active_low, down_weight, preferred_element_type=jnp.float32) + down_bias.astype(
        jnp.float32
    )
    output = (flat_in + branch + feed).astype(jnp.bfloat16).reshape(inputs.shape)
    qkv_weight, out_weight, up_weight, down_weight = (
        lax.all_gather(w_qkv.astype(jnp.bfloat16), ("seq", "head"), axis=0, tiled=True),
        lax.all_gather(w_out.astype(jnp.bfloat16), ("seq", "head"), axis=0, tiled=True),
        lax.all_gather(w_fc1.astype(jnp.bfloat16), ("seq", "head"), axis=0, tiled=True),
        lax.all_gather(w_fc2.astype(jnp.bfloat16), ("seq", "head"), axis=0, tiled=True),
    )
    grad_low = cotangent.reshape(seq_total * row_count, D)
    grad_full = grad_low.astype(jnp.float32)
    cot_sum = jnp.sum(grad_full, axis=0)
    grad_down_w = jnp.einsum("nf,nd->fd", active_low, grad_low, preferred_element_type=jnp.float32)
    grad_active = jnp.einsum("nd,fd->nf", grad_low, down_weight, preferred_element_type=jnp.float32)
    grad_hidden_low = gelu_back(grad_active)[0].astype(jnp.bfloat16)
    grad_up_w = jnp.einsum(
        "nm,nf->mf", normed_low, grad_hidden_low, preferred_element_type=jnp.float32
    )
    grad_up_b = jnp.sum(grad_hidden_low.astype(jnp.float32), axis=0)
    grad_normed = jnp.einsum(
        "nf,mf->nm", grad_hidden_low, up_weight, preferred_element_type=jnp.float32
    )
    grad_out_w = jnp.einsum("nm,nd->md", attended, grad_low, preferred_element_type=jnp.float32)
    grad_att_low = jnp.einsum(
        "nd,md->nm", grad_low, out_weight, preferred_element_type=jnp.float32
    ).astype(jnp.bfloat16)
    grad_heads = lax.all_to_all(
        grad_att_low.reshape(seq_total, row_count, D),
        "head",
        split_axis=2,
        concat_axis=1,
        tiled=True,
    ).reshape(seq_total, block_rows, heads_here, HD)
    row_dot = jnp.sum(
        jnp.transpose(grad_heads.astype(jnp.float32), (0, 2, 1, 3)) * attn_full, axis=3
    )

    def back_turn(turn_index, current):
        grad_query, grad_kv, kv_now = current
        source = (seq_rank - turn_index) % seq_devices
        key_pos = source * block_rows + jnp.arange(block_rows, dtype=jnp.int32)
        key_seg = segment_ids(doc_ends, key_pos)

        def back_compute(grads_in):
            return lax.map(
                partial(backward_step, query_pos=query_pos, key_pos=key_pos),
                (
                    grads_in[0],
                    grads_in[1],
                    query_heads,
                    kv_now,
                    grad_heads,
                    log_total,
                    row_dot,
                    query_seg,
                    key_seg,
                ),
            )

        return lax.cond(
            source <= seq_rank, back_compute, lambda grads_in: grads_in, (grad_query, grad_kv)
        )

    def pass_keys(kv_now):
        return from_behind(kv_now, "seq", 1)

    def pass_grads(grad_kv):
        return from_behind_2(grad_kv.astype(jnp.bfloat16), "seq", 1).astype(grad_kv.dtype)

    def loop_turn(turn_index, current):
        grad_query, grad_kv = back_turn(turn_index, current)
        return (grad_query, pass_grads(grad_kv), pass_keys(current[2]))

    start_grads = (
        jnp.zeros((seq_total, heads_here, block_rows, HD), jnp.float32),
        jnp.zeros((seq_total, block_rows, 2, group_width), jnp.float32),
        kv_heads,
    )
    loop_state = lax.fori_loop(0, seq_devices - 1, loop_turn, start_grads)
    grad_query, grad_kv = back_turn(seq_devices - 1, loop_state)
    grad_kv = pass_grads(grad_kv)
    back_heads = jnp.concatenate(
        [
            jnp.transpose(grad_query, (0, 2, 1, 3)).reshape(seq_total, block_rows, 1, group_width),
            grad_kv,
        ],
        axis=2,
    ).astype(jnp.bfloat16)
    back_tokens = (
        lax.all_to_all(back_heads, "head", split_axis=1, concat_axis=3, tiled=True)
        .astype(jnp.float32)
        .reshape(seq_total, row_count, 3, H, HD)
    )
    grad_qkv_low = (
        jnp.stack(
            [
                turn_back(back_tokens[:, :, 0])[0],
                turn_back(back_tokens[:, :, 1])[0],
                back_tokens[:, :, 2],
            ],
            axis=2,
        )
        .reshape(seq_total * row_count, 3 * D)
        .astype(jnp.bfloat16)
    )
    grad_qkv_w = jnp.einsum(
        "nm,nk->mk", normed_low, grad_qkv_low, preferred_element_type=jnp.float32
    )
    grad_qkv_b = jnp.sum(grad_qkv_low.astype(jnp.float32), axis=0)
    grad_normed = grad_normed + jnp.einsum(
        "nk,mk->nm", grad_qkv_low, qkv_weight, preferred_element_type=jnp.float32
    )
    grad_in, grad_gain, grad_shift = norm_back(grad_normed)
    grad_input = (grad_full + grad_in).astype(jnp.bfloat16).reshape(inputs.shape)
    sums_all = (
        lax.psum_scatter(grad_gain, ("seq", "head"), scatter_dimension=0, tiled=True),
        lax.psum_scatter(grad_shift, ("seq", "head"), scatter_dimension=0, tiled=True),
        lax.psum_scatter(grad_qkv_w, ("seq", "head"), scatter_dimension=0, tiled=True),
        lax.psum_scatter(grad_qkv_b, ("seq", "head"), scatter_dimension=0, tiled=True),
        lax.psum_scatter(grad_out_w, ("seq", "head"), scatter_dimension=0, tiled=True),
        lax.psum_scatter(cot_sum, ("seq", "head"), scatter_dimension=0, tiled=True),
        lax.psum_scatter(grad_up_w, ("seq", "head"), scatter_dimension=0, tiled=True),
        lax.psum_scatter(grad_up_b, ("seq", "head"), scatter_dimension=0, tiled=True),
        lax.psum_scatter(grad_down_w, ("seq", "head"), scatter_dimension=0, tiled=True),
    )
    return (
        output,
        grad_input,
        sums_all[0],
        sums_all[1],
        sums_all[2],
        sums_all[3],
        sums_all[4],
        sums_all[5],
        sums_all[6],
        sums_all[7],
        sums_all[8],
        sums_all[5],
    )


BF = jnp.bfloat16
F32 = jnp.float32
AXES = ("seq", "head")
FF = 8192
BLOCK = 256


def suits(mesh):
    return mesh.shape["seq"] * mesh.shape["head"] == H and mesh.shape["head"] == 4


def coordinates(rank):
    return rank // 8, (rank // 4) % 2, (rank // 2) % 2, rank % 2


def rank_of(z, core, y, x):
    return ((z * 2 + core) * 2 + y) * 2 + x


def route(step):
    return [(rank, rank_of(*step(*coordinates(rank)))) for rank in range(H)]


def ring_place(z, y, length):
    return z if y == 0 else length - 1 - z


def ring_point(place, length):
    place = place % length
    return (place, 0) if place < length // 2 else (length - 1 - place, 1)


def ring_route(by):
    length = H // 4

    def step(z, core, y, x):
        new_z, new_y = ring_point(ring_place(z, y, length) + by, length)
        return new_z, core, new_y, x

    return route(step)


def across_pair(value):
    return lax.ppermute(value, AXES, route(lambda z, core, y, x: (z, core, y, 1 - x)))


def across_cores(value):
    return lax.ppermute(value, AXES, route(lambda z, core, y, x: (z, 1 - core, y, x)))


def up_ring(value):
    return lax.ppermute(value, AXES, ring_route(1))


def down_ring(value):
    return lax.ppermute(value, AXES, ring_route(-1))


def block_index(place, core):
    length = H // 4
    place = place % length
    z = jnp.where(place < length // 2, place, length - 1 - place)
    y = (place >= length // 2).astype(jnp.int32)
    return (z * 2 + core) * 2 + y


def gather_tokens(own, place, core):
    rows, width = own.shape
    half = rows // 2
    length = H // 4
    chunks = [(0, own)]
    up = down = own
    for hop in range(1, length // 2):
        up, down = up_ring(up), down_ring(down)
        chunks += [(-hop, up), (hop, down)]
    far = jnp.concatenate([up_ring(up[:half]), down_ring(down[half:])], axis=0)
    chunks += [(length // 2, far)]
    whole = jnp.zeros((H // 2, rows, width), own.dtype)
    for offset, chunk in chunks:
        other = across_cores(chunk)
        whole = lax.dynamic_update_slice(whole, chunk[None], (block_index(place + offset, core), 0, 0))
        whole = lax.dynamic_update_slice(
            whole, other[None], (block_index(place + offset, 1 - core), 0, 0)
        )
    return whole.reshape(H // 2 * rows, width)


def scatter_tokens(part, place, core):
    length = H // 4
    rows = part.shape[0] // (H // 2)
    half = rows // 2
    blocks = part.reshape(length // 2, 2, 2, rows, D)
    for_other = lax.dynamic_index_in_dim(blocks, 1 - core, 1, keepdims=False)
    from_other = across_cores(for_other)

    def term(offset):
        index = block_index(place + offset, core)
        z, y = index // 4, index % 2
        mine = lax.dynamic_slice(blocks, (z, core, y, 0, 0), (1, 1, 1, rows, D)).reshape(rows, D)
        theirs = lax.dynamic_slice(from_other, (z, y, 0, 0), (1, 1, rows, D)).reshape(rows, D)
        return mine.astype(F32) + theirs.astype(F32)

    far = term(length // 2).astype(BF)
    pad = jnp.zeros((rows - half, D), F32)
    up = jnp.concatenate([up_ring(far[:half]).astype(F32), pad], axis=0)
    down = jnp.concatenate([pad, down_ring(far[half:]).astype(F32)], axis=0)
    for hop in range(length // 2 - 1, 0, -1):
        up = up_ring((up + term(hop)).astype(BF)).astype(F32)
        down = down_ring((down + term(-hop)).astype(BF)).astype(F32)
    return term(0) + up + down


def turn(field, tables, sign):
    half_rot = ROT // 2
    first = pltpu.roll(field, 2 * HD - half_rot, 1)
    second = pltpu.roll(field, half_rot, 1)
    return field * tables[0] + sign * (second * tables[2] - first * tables[1])


def turn_tables(count):
    half_rot = ROT // 2
    inverse = jnp.power(10000.0, -2.0 * jnp.arange(half_rot, dtype=F32) / ROT)
    angles = jnp.arange(count, dtype=jnp.int32).astype(F32)[:, None] * inverse[None, :]
    cosine, sine = jnp.cos(angles), jnp.sin(angles)
    none = jnp.zeros_like(sine)
    rest_one, rest_none = jnp.ones((count, HD - ROT), F32), jnp.zeros((count, HD - ROT), F32)
    one = [
        jnp.concatenate([cosine, cosine, rest_one], axis=1),
        jnp.concatenate([sine, none, rest_none], axis=1),
        jnp.concatenate([none, sine, rest_none], axis=1),
    ]
    return jnp.stack([jnp.concatenate([t, t], axis=1) for t in one])


def head_lanes(value, head):
    lane = lax.broadcasted_iota(jnp.int32, value.shape, 1)
    return jnp.where((lane >= HD) if head else (lane < HD), value, jnp.zeros_like(value))


def dot_of(left, right, left_dim, right_dim):
    return lax.dot_general(
        left, right, (((left_dim,), (right_dim,)), ((), ())), preferred_element_type=F32
    )


def allowed_keys(starts, key_count, query_first):
    keys = lax.broadcasted_iota(jnp.int32, (key_count, BLOCK), 0)
    queries = query_first + lax.broadcasted_iota(jnp.int32, (1, BLOCK), 1)
    return (keys >= starts) & (keys <= queries)


def attend_forward(qkv_ref, bias_ref, tables_ref, starts_ref, q_ref, k_out, v_out, o_ref, low_ref, lse_ref, k_ref, v_ref):
    step = pl.program_id(0)
    width = 2 * HD
    raw = qkv_ref[...] + bias_ref[...]
    tables = tables_ref[...]
    here = pl.ds(pl.multiple_of(step * BLOCK, BLOCK), BLOCK)
    q_ref[...] = turn(raw[:, :width], tables, 1.0).astype(BF)
    k_ref[here, :] = turn(raw[:, width : 2 * width], tables, 1.0).astype(BF)
    v_ref[here, :] = raw[:, 2 * width :].astype(BF)
    k_out[...] = k_ref[here, :]
    v_out[...] = v_ref[here, :]

    def work(block):
        count = (block + 1) * BLOCK
        query = q_ref[...]
        key, value = k_ref[:count, :], v_ref[:count, :]
        allowed = allowed_keys(starts_ref[...], count, block * BLOCK)
        outs, logs = [], []
        for head in range(2):
            scores = dot_of(key, head_lanes(query, head), 1, 1) * 0.125
            scores = jnp.where(allowed, scores, NEG_FILL)
            top = jnp.max(scores, axis=0, keepdims=True)
            weights = jnp.exp(scores - top)
            total = jnp.sum(weights, axis=0, keepdims=True)
            outs.append(dot_of(value, weights.astype(BF), 0, 0) / total)
            logs.append(top + jnp.log(total))
        row = lax.broadcasted_iota(jnp.int32, outs[0].shape, 0)
        out = jnp.where(row < HD, outs[0], outs[1]).T
        o_ref[...] = out
        low_ref[...] = out.astype(BF)
        lse_ref[...] = jnp.concatenate(logs, axis=0)

    for block in range(pl.num_programs(0)):
        pl.when(step == block)(partial(work, block))


def attend_backward(q_ref, k_ref, v_ref, g_ref, o_ref, lse_ref, tables_ref, starts_ref, out_ref, gk_ref, gv_ref):
    step = pl.program_id(0)
    steps = pl.num_programs(0)
    width = 2 * HD

    @pl.when(step == 0)
    def _():
        gk_ref[...] = jnp.zeros_like(gk_ref)
        gv_ref[...] = jnp.zeros_like(gv_ref)

    def work(block):
        count = (block + 1) * BLOCK
        query, grad = q_ref[...], g_ref[...]
        key, value = k_ref[:count, :], v_ref[:count, :]
        allowed = allowed_keys(starts_ref[...], count, block * BLOCK)
        product = (grad.astype(F32) * o_ref[...]).T
        grad_q = None
        for head in range(2):
            dots = jnp.sum(product[head * HD : (head + 1) * HD], axis=0, keepdims=True)
            query_h, grad_h = head_lanes(query, head), head_lanes(grad, head)
            scores = dot_of(key, query_h, 1, 1) * 0.125
            probs = jnp.where(allowed, jnp.exp(scores - lse_ref[head : head + 1, :]), 0.0)
            grad_probs = dot_of(value, grad_h, 1, 1)
            grad_scores = (probs * (grad_probs - dots)).astype(BF)
            gv_ref[:count, :] += dot_of(probs.astype(BF), grad_h, 1, 0)
            gk_ref[:count, :] += dot_of(grad_scores, query_h, 1, 0)
            this = dot_of(head_lanes(key, head), grad_scores, 0, 0)
            grad_q = this if grad_q is None else grad_q + this
        here = slice(block * BLOCK, count)
        tables = tables_ref[...]

        def back(value):
            return turn((value * 0.125).astype(BF).astype(F32), tables, -1.0).astype(BF)

        out_ref[:, :width] = back(grad_q.T)
        out_ref[:, width : 2 * width] = back(gk_ref[here, :])
        out_ref[:, 2 * width :] = gv_ref[here, :].astype(BF)

    for block in range(steps):
        pl.when(step == steps - 1 - block)(partial(work, block))


def attention_forward(qkv, bias, tables, starts):
    count = qkv.shape[0]
    width = 2 * HD
    steps = count // BLOCK
    rows = lambda i: (i, 0)
    block = pl.BlockSpec((BLOCK, width), rows)
    return pl.pallas_call(
        attend_forward,
        grid=(steps,),
        in_specs=[
            pl.BlockSpec((BLOCK, 3 * width), rows),
            pl.BlockSpec((1, 3 * width), lambda i: (0, 0)),
            pl.BlockSpec((3, BLOCK, width), lambda i: (0, i, 0)),
            pl.BlockSpec((1, BLOCK), lambda i: (0, i)),
        ],
        out_specs=[block] * 5 + [pl.BlockSpec((2, BLOCK), lambda i: (0, i))],
        out_shape=[
            jax.ShapeDtypeStruct((count, width), BF),
            jax.ShapeDtypeStruct((count, width), BF),
            jax.ShapeDtypeStruct((count, width), BF),
            jax.ShapeDtypeStruct((count, width), F32),
            jax.ShapeDtypeStruct((count, width), BF),
            jax.ShapeDtypeStruct((2, count), F32),
        ],
        scratch_shapes=[pltpu.VMEM((count, width), BF), pltpu.VMEM((count, width), BF)],
        cost_estimate=pl.CostEstimate(
            flops=8 * count * count * HD, bytes_accessed=8 * count * width * 2, transcendentals=count * count
        ),
        name="attend_forward",
    )(qkv, bias, tables, starts)


def attention_backward(query, key, value, grad, out, logs, tables, starts):
    count = query.shape[0]
    width = 2 * HD
    steps = count // BLOCK
    rows = lambda i: (steps - 1 - i, 0)
    block = pl.BlockSpec((BLOCK, width), rows)
    full = pl.BlockSpec((count, width), lambda i: (0, 0))
    return pl.pallas_call(
        attend_backward,
        grid=(steps,),
        in_specs=[
            block,
            full,
            full,
            block,
            block,
            pl.BlockSpec((2, BLOCK), lambda i: (0, steps - 1 - i)),
            pl.BlockSpec((3, BLOCK, width), lambda i: (0, steps - 1 - i, 0)),
            pl.BlockSpec((1, BLOCK), lambda i: (0, steps - 1 - i)),
        ],
        out_specs=pl.BlockSpec((BLOCK, 3 * width), rows),
        out_shape=jax.ShapeDtypeStruct((count, 3 * width), BF),
        scratch_shapes=[pltpu.VMEM((count, width), F32), pltpu.VMEM((count, width), F32)],
        cost_estimate=pl.CostEstimate(
            flops=20 * count * count * HD, bytes_accessed=8 * count * width * 2, transcendentals=count * count
        ),
        name="attend_backward",
    )(query, key, value, grad, out, logs, tables, starts)


def normalize(values):
    center = values - jnp.mean(values, axis=-1, keepdims=True)
    scale = lax.rsqrt(jnp.mean(center * center, axis=-1, keepdims=True) + 1e-05)
    return center * scale, scale


def paired_step(
    inputs,
    doc_lengths,
    ln_gain,
    ln_bias,
    w_qkv,
    b_qkv,
    w_out,
    b_out,
    w_fc1,
    b_fc1,
    w_fc2,
    b_fc2,
    cotangent,
):
    rows = inputs.shape[1]
    count = rows * H
    rank = lax.axis_index("seq") * 4 + lax.axis_index("head")
    x = rank % 2
    y, core, z = (rank // 2) % 2, (rank // 4) % 2, rank // 8
    length = H // 4
    place = jnp.where(y == 0, z, length - 1 - z)
    doc_ends = jnp.cumsum(lax.dynamic_index_in_dim(doc_lengths, x, 0, keepdims=False))
    positions = jnp.arange(count, dtype=jnp.int32)
    starts = jnp.max(
        jnp.where(doc_ends[:, None] <= positions[None, :], doc_ends[:, None], 0), axis=0
    )[None, :]
    tables = turn_tables(count)

    def to_group(field):
        mine = lax.dynamic_index_in_dim(field, x, 0, keepdims=False)
        got = across_pair(lax.dynamic_index_in_dim(field, 1 - x, 0, keepdims=False))
        return jnp.where(x == 0, jnp.concatenate([mine, got]), jnp.concatenate([got, mine]))

    def from_group(field):
        mine = lax.dynamic_slice_in_dim(field, x * rows, rows, 0)
        got = across_pair(lax.dynamic_slice_in_dim(field, (1 - x) * rows, rows, 0))
        return jnp.where(x == 0, jnp.stack([mine, got]), jnp.stack([got, mine]))

    own_in = to_group(inputs)
    all_in = gather_tokens(own_in, place, core)
    small = jnp.concatenate([ln_gain, ln_bias, b_out, b_fc2, b_qkv, b_fc1]).astype(BF)
    small = lax.all_gather(small[None], AXES, axis=0, tiled=True).astype(F32)
    per = D // H
    gain, shift, out_bias, down_bias = [
        small[:, i * per : (i + 1) * per].reshape(1, D) for i in range(4)
    ]
    qkv_bias_all = small[:, 4 * per : 4 * per + 3 * per].reshape(3, H, HD)
    up_bias_all = small[:, 7 * per :]
    other = rank + 1 - 2 * x

    def both(table, axis):
        return [lax.dynamic_index_in_dim(table, i, axis, keepdims=False) for i in (rank, other)]

    qkv_bias = jnp.concatenate(both(qkv_bias_all, 1), axis=1).reshape(1, 6 * HD)
    up_bias = jnp.concatenate(both(up_bias_all, 0), axis=0)[None, :]

    per_ff = FF // H
    to_heads = jnp.concatenate(
        [
            w_qkv.astype(BF).reshape(per, 3, H, HD).transpose(2, 0, 1, 3).reshape(H, per, 3 * HD),
            w_fc1.astype(BF).reshape(per, H, per_ff).transpose(1, 0, 2),
        ],
        axis=2,
    )
    mine_w = lax.all_to_all(to_heads, AXES, 0, 0, tiled=True).reshape(D, 3 * HD + per_ff)
    pair_w = across_pair(mine_w)
    qkv_w = jnp.stack(
        [mine_w[:, : 3 * HD].reshape(D, 3, HD), pair_w[:, : 3 * HD].reshape(D, 3, HD)], axis=2
    ).reshape(D, 6 * HD)
    up_w = jnp.concatenate([mine_w[:, 3 * HD :], pair_w[:, 3 * HD :]], axis=1)
    mine_d = jnp.concatenate([w_out, w_fc2], axis=0).astype(BF)
    pair_d = across_pair(mine_d)
    down_w = jnp.concatenate([mine_d[:per], pair_d[:per], mine_d[per:], pair_d[per:]], axis=0)

    normed = (normalize(all_in.astype(F32))[0] * gain + shift).astype(BF)
    qkv = jnp.dot(normed, qkv_w, preferred_element_type=F32)
    query, key, value, out_full, attended, logs = attention_forward(qkv, qkv_bias, tables, starts)
    hidden = jnp.dot(normed, up_w, preferred_element_type=F32) + up_bias
    active, gelu_back = jax.vjp(gelu_tanh, hidden)
    mixed = jnp.concatenate([attended, active.astype(BF)], axis=1)
    forward_part = jnp.dot(mixed, down_w, preferred_element_type=F32).astype(BF)
    forward_sum = scatter_tokens(forward_part, place, core)
    output = from_group(
        (own_in.astype(F32) + (forward_sum + (out_bias + down_bias))).astype(BF)
    )

    own_cot = to_group(cotangent)
    all_cot = gather_tokens(own_cot, place, core)
    grad_mixed = dot_of(all_cot, down_w, 1, 1)
    grad_att = grad_mixed[:, : 2 * HD].astype(BF)
    grad_hidden = gelu_back(grad_mixed[:, 2 * HD :])[0].astype(BF)
    grad_down = dot_of(mixed, all_cot, 0, 0)
    grad_qkv = attention_backward(query, key, value, grad_att, out_full, logs, tables, starts)
    grad_qkv_w = dot_of(normed, grad_qkv, 0, 0)
    grad_up_w = dot_of(normed, grad_hidden, 0, 0)
    back_part = dot_of(grad_qkv, qkv_w, 1, 1) + dot_of(grad_hidden, up_w, 1, 1)
    normal_all = normalize(all_in.astype(F32))[0]
    grad_gain = jnp.sum(back_part * normal_all, axis=0)
    grad_shift = jnp.sum(back_part, axis=0)
    back_sum = scatter_tokens(back_part.astype(BF), place, core)
    normal, scale = normalize(own_in.astype(F32))
    scaled = back_sum * gain
    grad_in = scale * (
        scaled
        - jnp.mean(scaled, axis=-1, keepdims=True)
        - normal * jnp.mean(scaled * normal, axis=-1, keepdims=True)
    )
    grad_input = from_group((own_cot.astype(F32) + grad_in).astype(BF))

    def add_pair(mine, for_pair):
        return mine + across_pair(for_pair.astype(BF)).astype(F32)

    grad_out_rows = add_pair(grad_down[:per], grad_down[per : 2 * per])
    grad_down_rows = add_pair(
        grad_down[2 * per : 2 * per + per_ff], grad_down[2 * per + per_ff :]
    )
    grad_heads = grad_qkv_w.reshape(D, 3, 2, HD)
    grad_cols = jnp.concatenate(
        [
            add_pair(grad_heads[:, :, 0], grad_heads[:, :, 1]).reshape(D, 3 * HD),
            add_pair(grad_up_w[:, :per_ff], grad_up_w[:, per_ff:]),
        ],
        axis=1,
    ).astype(BF)
    grad_rows = lax.all_to_all(
        grad_cols.reshape(H, per, 3 * HD + per_ff), AXES, 0, 0, tiled=True
    ).astype(F32)
    grad_qkv_rows = (
        grad_rows[:, :, : 3 * HD].reshape(H, per, 3, HD).transpose(1, 2, 0, 3).reshape(per, 3 * D)
    )
    grad_up_rows = grad_rows[:, :, 3 * HD :].transpose(1, 0, 2).reshape(per, FF)

    cot_sum = jnp.sum(own_cot.astype(F32), axis=0)
    head_sums = jnp.sum(grad_qkv.astype(F32), axis=0).reshape(3, 2, HD)
    up_sums = jnp.sum(grad_hidden.astype(F32), axis=0).reshape(2, per_ff)
    qkv_sums = jnp.zeros((3, H, HD), F32)
    up_all = jnp.zeros((H, per_ff), F32)
    for which, index in enumerate((rank, other)):
        qkv_sums = lax.dynamic_update_slice(qkv_sums, head_sums[:, which : which + 1], (0, index, 0))
        up_all = lax.dynamic_update_slice(up_all, up_sums[which : which + 1], (index, 0))
    sums = jnp.concatenate(
        [
            grad_gain.reshape(H, per),
            grad_shift.reshape(H, per),
            cot_sum.reshape(H, per),
            qkv_sums.reshape(H, 3 * per),
            up_all,
        ],
        axis=1,
    )
    sums = lax.psum_scatter(sums, AXES, scatter_dimension=0, tiled=True).reshape(-1)
    return (
        output,
        grad_input,
        sums[:per],
        sums[per : 2 * per],
        grad_qkv_rows,
        sums[3 * per : 6 * per],
        grad_out_rows,
        sums[2 * per : 3 * per],
        grad_up_rows,
        sums[6 * per :],
        grad_down_rows,
        sums[2 * per : 3 * per],
    )


def solution(mesh):
    return jax.shard_map(
        paired_step if suits(mesh) else gathered_step,
        mesh=mesh,
        in_specs=(
            P(None, ("seq", "head"), None),
            P(),
            P(("seq", "head")),
            P(("seq", "head")),
            P(("seq", "head"), None),
            P(("seq", "head")),
            P(("seq", "head"), None),
            P(("seq", "head")),
            P(("seq", "head"), None),
            P(("seq", "head")),
            P(("seq", "head"), None),
            P(("seq", "head")),
            P(None, ("seq", "head"), None),
        ),
        out_specs=(
            P(None, ("seq", "head"), None),
            P(None, ("seq", "head"), None),
            P(("seq", "head")),
            P(("seq", "head")),
            P(("seq", "head"), None),
            P(("seq", "head")),
            P(("seq", "head"), None),
            P(("seq", "head")),
            P(("seq", "head"), None),
            P(("seq", "head")),
            P(("seq", "head"), None),
            P(("seq", "head")),
        ),
        check_vma=False,
    )
```

```python
from functools import partial

import jax
import jax.numpy as jnp
from jax import lax
from jax.experimental import pallas as pl
from jax.experimental.pallas import tpu as pltpu
from jax.sharding import PartitionSpec as P

D = 2048
H = 32
HD = 64
ROT = 32


NEG_FILL = -1e30


def from_behind(block, axis, distance):
    devices = range(lax.axis_size(axis))
    route = [(i - distance, i) for i in devices if i - distance in devices]
    return lax.ppermute(block, axis, route)


def from_behind_2(shard, axis, by):
    length = lax.axis_size(axis)
    return lax.ppermute(shard, axis, [(i, (i + by) % length) for i in range(length)])


def rotate(field, cosine, sine):
    half_rot = ROT // 2
    first_part = field[..., :half_rot]
    second_part = field[..., half_rot:ROT]
    return jnp.concatenate(
        [
            first_part * cosine - second_part * sine,
            second_part * cosine + first_part * sine,
            field[..., ROT:],
        ],
        axis=-1,
    )


def rotation_tables(positions):
    half_rot = ROT // 2
    inverse = jnp.power(10000.0, -2.0 * jnp.arange(half_rot, dtype=jnp.float32) / ROT)
    angles = positions.astype(jnp.float32)[:, None] * inverse[None, :]
    return (jnp.cos(angles)[:, None, :], jnp.sin(angles)[:, None, :])


def layer_norm(values, gain_value, shift_value):
    center = values - jnp.mean(values, axis=-1, keepdims=True)
    spread = jnp.mean(center * center, axis=-1, keepdims=True)
    return center * lax.rsqrt(spread + 1e-05) * gain_value + shift_value


def segment_ids(doc_ends, positions):
    return jnp.sum((doc_ends[:, None, :] <= positions[None, :, None]).astype(jnp.int32), axis=2)


def gelu_tanh(values):
    return jax.nn.gelu(values, approximate=True)


def allowed_pairs(query_pos, query_seg, key_pos, key_seg):
    return (key_pos[None, :] <= query_pos[:, None]) & (key_seg[None, :] == query_seg[:, None])


def masked_scores(query_seq, key_seq, allowed):
    raw_scores = (
        jnp.einsum("qhd,khd->hqk", query_seq, key_seq, preferred_element_type=jnp.float32) * 0.125
    )
    return jnp.where(allowed[None], raw_scores, NEG_FILL)


def forward_step(members, query_pos, key_pos):
    top_val, total_val, accum_val, query_seq, kv_seq, query_seg, key_seg = members
    kv_split = kv_seq.reshape(kv_seq.shape[0], 2, -1, HD)
    allowed = allowed_pairs(query_pos, query_seg, key_pos, key_seg)
    masked = masked_scores(query_seq, kv_split[:, 0], allowed)
    new_top = jnp.maximum(top_val, jnp.max(masked, axis=2))
    weights = jnp.where(allowed[None], jnp.exp(masked - new_top[:, :, None]), 0.0)
    factor = jnp.exp(top_val - new_top)
    new_total = total_val * factor + jnp.sum(weights, axis=2)
    new_accum = accum_val * factor[:, :, None] + jnp.einsum(
        "hqk,khd->hqd",
        weights.astype(jnp.bfloat16),
        kv_split[:, 1],
        preferred_element_type=jnp.float32,
    )
    return (new_top, new_total, new_accum)


def backward_step(members, query_pos, key_pos):
    grad_query, grad_kv, query_seq, kv_seq, grad_att, log_total, row_dot, query_seg, key_seg = (
        members
    )
    key_total = kv_seq.shape[0]
    kv_split = kv_seq.reshape(key_total, 2, -1, HD)
    allowed = allowed_pairs(query_pos, query_seg, key_pos, key_seg)
    masked = masked_scores(query_seq, kv_split[:, 0], allowed)
    prob_full = jnp.where(allowed[None], jnp.exp(masked - log_total[:, :, None]), 0.0)
    grad_value = jnp.einsum(
        "hqk,qhd->khd", prob_full.astype(jnp.bfloat16), grad_att, preferred_element_type=jnp.float32
    )
    grad_probs = jnp.einsum(
        "qhd,khd->hqk", grad_att, kv_split[:, 1], preferred_element_type=jnp.float32
    )
    grad_scores = (prob_full * (grad_probs - row_dot[:, :, None])).astype(jnp.bfloat16)
    grad_query = (
        grad_query
        + jnp.einsum(
            "hqk,khd->hqd", grad_scores, kv_split[:, 0], preferred_element_type=jnp.float32
        )
        * 0.125
    )
    grad_key = (
        jnp.einsum("hqk,qhd->khd", grad_scores, query_seq, preferred_element_type=jnp.float32)
        * 0.125
    )
    grad_kv = grad_kv + jnp.stack([grad_key, grad_value], axis=1).reshape(key_total, 2, -1)
    return (grad_query, grad_kv)


def gathered_step(
    inputs,
    doc_lengths,
    ln_gain,
    ln_bias,
    w_qkv,
    b_qkv,
    w_out,
    b_out,
    w_fc1,
    b_fc1,
    w_fc2,
    b_fc2,
    cotangent,
):
    seq_total = inputs.shape[0]
    row_count = inputs.shape[1]
    head_count = lax.axis_size("head")
    seq_devices = lax.axis_size("seq")
    heads_here = H // head_count
    group_width = heads_here * HD
    block_rows = row_count * head_count
    seq_rank = lax.axis_index("seq")
    head_rank = lax.axis_index("head")
    doc_ends = jnp.cumsum(doc_lengths, axis=1)
    token_pos = (seq_rank * head_count + head_rank) * row_count + jnp.arange(
        row_count, dtype=jnp.int32
    )
    query_start = seq_rank * block_rows
    query_pos = query_start + jnp.arange(block_rows, dtype=jnp.int32)
    query_seg = segment_ids(doc_ends, query_pos)
    gathered = (
        lax.all_gather(ln_gain.astype(jnp.bfloat16), ("seq", "head"), axis=0, tiled=True),
        lax.all_gather(ln_bias.astype(jnp.bfloat16), ("seq", "head"), axis=0, tiled=True),
        lax.all_gather(w_qkv.astype(jnp.bfloat16), ("seq", "head"), axis=0, tiled=True),
        lax.all_gather(b_qkv.astype(jnp.bfloat16), ("seq", "head"), axis=0, tiled=True),
        lax.all_gather(w_out.astype(jnp.bfloat16), ("seq", "head"), axis=0, tiled=True),
        lax.all_gather(b_out.astype(jnp.bfloat16), ("seq", "head"), axis=0, tiled=True),
        lax.all_gather(w_fc1.astype(jnp.bfloat16), ("seq", "head"), axis=0, tiled=True),
        lax.all_gather(b_fc1.astype(jnp.bfloat16), ("seq", "head"), axis=0, tiled=True),
        lax.all_gather(w_fc2.astype(jnp.bfloat16), ("seq", "head"), axis=0, tiled=True),
        lax.all_gather(b_fc2.astype(jnp.bfloat16), ("seq", "head"), axis=0, tiled=True),
    )
    (
        gain_full,
        shift_full,
        qkv_weight,
        qkv_bias,
        out_weight,
        out_bias,
        up_weight,
        up_bias,
        down_weight,
        down_bias,
    ) = gathered
    flat_in = inputs.reshape(seq_total * row_count, D).astype(jnp.float32)
    normed, norm_back = jax.vjp(
        layer_norm, flat_in, gain_full.astype(jnp.float32), shift_full.astype(jnp.float32)
    )
    normed_low = normed.astype(jnp.bfloat16)
    qkv_all = (
        jnp.dot(normed_low, qkv_weight, preferred_element_type=jnp.float32)
        + qkv_bias.astype(jnp.float32)
    ).reshape(seq_total, row_count, 3, H, HD)
    cosine, sine = rotation_tables(token_pos)

    def turn_field(field):
        return rotate(field, cosine, sine)

    query_rot, turn_back = jax.vjp(turn_field, qkv_all[:, :, 0])
    key_rot = turn_field(qkv_all[:, :, 1])
    stacked = (
        jnp.stack([query_rot, key_rot, qkv_all[:, :, 2]], axis=2)
        .reshape(seq_total, row_count, 3, D)
        .astype(jnp.bfloat16)
    )
    by_heads = lax.all_to_all(stacked, "head", split_axis=3, concat_axis=1, tiled=True)
    query_heads = by_heads[:, :, 0].reshape(seq_total, block_rows, heads_here, HD)
    kv_heads = by_heads[:, :, 1:3]
    start_state = (
        jnp.full((seq_total, heads_here, block_rows), NEG_FILL, jnp.float32),
        jnp.zeros((seq_total, heads_here, block_rows), jnp.float32),
        jnp.zeros((seq_total, heads_here, block_rows, HD), jnp.float32),
    )
    shard_piece = lax.all_gather(kv_heads, "seq", axis=1, tiled=True)

    def one_turn(turn_index, current):
        kv_block = lax.dynamic_slice_in_dim(shard_piece, turn_index * block_rows, block_rows, 1)
        key_start = turn_index * block_rows
        key_pos = key_start + jnp.arange(block_rows, dtype=jnp.int32)
        key_seg = segment_ids(doc_ends, key_pos)

        def one_compute(state_in):
            return lax.map(
                partial(forward_step, query_pos=query_pos, key_pos=key_pos),
                (state_in[0], state_in[1], state_in[2], query_heads, kv_block, query_seg, key_seg),
            )

        return lax.cond(
            key_start < query_start + block_rows, one_compute, lambda state_in: state_in, current
        )

    top_all, total_all, accum_all = lax.fori_loop(
        0, shard_piece.shape[1] // block_rows, one_turn, start_state
    )
    attn_full = accum_all / total_all[:, :, :, None]
    log_total = top_all + jnp.log(total_all)
    attn_low = (
        jnp.transpose(attn_full, (0, 2, 1, 3))
        .reshape(seq_total, block_rows, group_width)
        .astype(jnp.bfloat16)
    )
    attended = lax.all_to_all(attn_low, "head", split_axis=1, concat_axis=2, tiled=True).reshape(
        seq_total * row_count, D
    )
    branch = jnp.dot(attended, out_weight, preferred_element_type=jnp.float32) + out_bias.astype(
        jnp.float32
    )
    hidden = jnp.dot(normed_low, up_weight, preferred_element_type=jnp.float32) + up_bias.astype(
        jnp.float32
    )
    active, gelu_back = jax.vjp(gelu_tanh, hidden)
    active_low = active.astype(jnp.bfloat16)
    feed = jnp.dot(active_low, down_weight, preferred_element_type=jnp.float32) + down_bias.astype(
        jnp.float32
    )
    output = (flat_in + branch + feed).astype(jnp.bfloat16).reshape(inputs.shape)
    qkv_weight, out_weight, up_weight, down_weight = (
        lax.all_gather(w_qkv.astype(jnp.bfloat16), ("seq", "head"), axis=0, tiled=True),
        lax.all_gather(w_out.astype(jnp.bfloat16), ("seq", "head"), axis=0, tiled=True),
        lax.all_gather(w_fc1.astype(jnp.bfloat16), ("seq", "head"), axis=0, tiled=True),
        lax.all_gather(w_fc2.astype(jnp.bfloat16), ("seq", "head"), axis=0, tiled=True),
    )
    grad_low = cotangent.reshape(seq_total * row_count, D)
    grad_full = grad_low.astype(jnp.float32)
    cot_sum = jnp.sum(grad_full, axis=0)
    grad_down_w = jnp.einsum("nf,nd->fd", active_low, grad_low, preferred_element_type=jnp.float32)
    grad_active = jnp.einsum("nd,fd->nf", grad_low, down_weight, preferred_element_type=jnp.float32)
    grad_hidden_low = gelu_back(grad_active)[0].astype(jnp.bfloat16)
    grad_up_w = jnp.einsum(
        "nm,nf->mf", normed_low, grad_hidden_low, preferred_element_type=jnp.float32
    )
    grad_up_b = jnp.sum(grad_hidden_low.astype(jnp.float32), axis=0)
    grad_normed = jnp.einsum(
        "nf,mf->nm", grad_hidden_low, up_weight, preferred_element_type=jnp.float32
    )
    grad_out_w = jnp.einsum("nm,nd->md", attended, grad_low, preferred_element_type=jnp.float32)
    grad_att_low = jnp.einsum(
        "nd,md->nm", grad_low, out_weight, preferred_element_type=jnp.float32
    ).astype(jnp.bfloat16)
    grad_heads = lax.all_to_all(
        grad_att_low.reshape(seq_total, row_count, D),
        "head",
        split_axis=2,
        concat_axis=1,
        tiled=True,
    ).reshape(seq_total, block_rows, heads_here, HD)
    row_dot = jnp.sum(
        jnp.transpose(grad_heads.astype(jnp.float32), (0, 2, 1, 3)) * attn_full, axis=3
    )

    def back_turn(turn_index, current):
        grad_query, grad_kv, kv_now = current
        source = (seq_rank - turn_index) % seq_devices
        key_pos = source * block_rows + jnp.arange(block_rows, dtype=jnp.int32)
        key_seg = segment_ids(doc_ends, key_pos)

        def back_compute(grads_in):
            return lax.map(
                partial(backward_step, query_pos=query_pos, key_pos=key_pos),
                (
                    grads_in[0],
                    grads_in[1],
                    query_heads,
                    kv_now,
                    grad_heads,
                    log_total,
                    row_dot,
                    query_seg,
                    key_seg,
                ),
            )

        return lax.cond(
            source <= seq_rank, back_compute, lambda grads_in: grads_in, (grad_query, grad_kv)
        )

    def pass_keys(kv_now):
        return from_behind(kv_now, "seq", 1)

    def pass_grads(grad_kv):
        return from_behind_2(grad_kv.astype(jnp.bfloat16), "seq", 1).astype(grad_kv.dtype)

    def loop_turn(turn_index, current):
        grad_query, grad_kv = back_turn(turn_index, current)
        return (grad_query, pass_grads(grad_kv), pass_keys(current[2]))

    start_grads = (
        jnp.zeros((seq_total, heads_here, block_rows, HD), jnp.float32),
        jnp.zeros((seq_total, block_rows, 2, group_width), jnp.float32),
        kv_heads,
    )
    loop_state = lax.fori_loop(0, seq_devices - 1, loop_turn, start_grads)
    grad_query, grad_kv = back_turn(seq_devices - 1, loop_state)
    grad_kv = pass_grads(grad_kv)
    back_heads = jnp.concatenate(
        [
            jnp.transpose(grad_query, (0, 2, 1, 3)).reshape(seq_total, block_rows, 1, group_width),
            grad_kv,
        ],
        axis=2,
    ).astype(jnp.bfloat16)
    back_tokens = (
        lax.all_to_all(back_heads, "head", split_axis=1, concat_axis=3, tiled=True)
        .astype(jnp.float32)
        .reshape(seq_total, row_count, 3, H, HD)
    )
    grad_qkv_low = (
        jnp.stack(
            [
                turn_back(back_tokens[:, :, 0])[0],
                turn_back(back_tokens[:, :, 1])[0],
                back_tokens[:, :, 2],
            ],
            axis=2,
        )
        .reshape(seq_total * row_count, 3 * D)
        .astype(jnp.bfloat16)
    )
    grad_qkv_w = jnp.einsum(
        "nm,nk->mk", normed_low, grad_qkv_low, preferred_element_type=jnp.float32
    )
    grad_qkv_b = jnp.sum(grad_qkv_low.astype(jnp.float32), axis=0)
    grad_normed = grad_normed + jnp.einsum(
        "nk,mk->nm", grad_qkv_low, qkv_weight, preferred_element_type=jnp.float32
    )
    grad_in, grad_gain, grad_shift = norm_back(grad_normed)
    grad_input = (grad_full + grad_in).astype(jnp.bfloat16).reshape(inputs.shape)
    sums_all = (
        lax.psum_scatter(grad_gain, ("seq", "head"), scatter_dimension=0, tiled=True),
        lax.psum_scatter(grad_shift, ("seq", "head"), scatter_dimension=0, tiled=True),
        lax.psum_scatter(grad_qkv_w, ("seq", "head"), scatter_dimension=0, tiled=True),
        lax.psum_scatter(grad_qkv_b, ("seq", "head"), scatter_dimension=0, tiled=True),
        lax.psum_scatter(grad_out_w, ("seq", "head"), scatter_dimension=0, tiled=True),
        lax.psum_scatter(cot_sum, ("seq", "head"), scatter_dimension=0, tiled=True),
        lax.psum_scatter(grad_up_w, ("seq", "head"), scatter_dimension=0, tiled=True),
        lax.psum_scatter(grad_up_b, ("seq", "head"), scatter_dimension=0, tiled=True),
        lax.psum_scatter(grad_down_w, ("seq", "head"), scatter_dimension=0, tiled=True),
    )
    return (
        output,
        grad_input,
        sums_all[0],
        sums_all[1],
        sums_all[2],
        sums_all[3],
        sums_all[4],
        sums_all[5],
        sums_all[6],
        sums_all[7],
        sums_all[8],
        sums_all[5],
    )


BF = jnp.bfloat16
F32 = jnp.float32
AXES = ("seq", "head")
FF = 8192
BLOCK = 256
KEYS = 512


QUICK = pl.CostEstimate(flops=1 << 20, bytes_accessed=1 << 16, transcendentals=0)


def suits(mesh):
    return mesh.shape["seq"] * mesh.shape["head"] == H and mesh.shape["head"] == 4


def coordinates(rank):
    return rank // 8, (rank // 4) % 2, (rank // 2) % 2, rank % 2


def rank_of(z, core, y, x):
    return ((z * 2 + core) * 2 + y) * 2 + x


def route(step):
    return [(rank, rank_of(*step(*coordinates(rank)))) for rank in range(H)]


def ring_place(z, y, length):
    return z if y == 0 else length - 1 - z


def ring_point(place, length):
    place = place % length
    return (place, 0) if place < length // 2 else (length - 1 - place, 1)


def ring_route(by):
    length = H // 4

    def step(z, core, y, x):
        new_z, new_y = ring_point(ring_place(z, y, length) + by, length)
        return new_z, core, new_y, x

    return route(step)


def across_pair(value):
    return lax.ppermute(value, AXES, route(lambda z, core, y, x: (z, core, y, 1 - x)))


def across_cores(value):
    return lax.ppermute(value, AXES, route(lambda z, core, y, x: (z, 1 - core, y, x)))


def up_ring(value):
    return lax.ppermute(value, AXES, ring_route(1))


def down_ring(value):
    return lax.ppermute(value, AXES, ring_route(-1))


def block_index(place, core):
    length = H // 4
    place = place % length
    z = jnp.where(place < length // 2, place, length - 1 - place)
    y = (place >= length // 2).astype(jnp.int32)
    return (z * 2 + core) * 2 + y


class Line:
    def __init__(self):
        self.last = ()

    def gate(self, *values):
        values = lax.optimization_barrier((values, self.last))[0] if self.last else values
        return values if len(values) > 1 else values[0]

    def mark(self, *values):
        self.last = values
        return values if len(values) > 1 else values[0]


class Gather:
    def __init__(self, line, own, place, core):
        self.line, self.place, self.core = line, place, core
        self.flying = (own, own)
        self.arrived = []
        self.land([(0, own)])

    def land(self, chunks):
        here = [(block_index(self.place + o, self.core), chunk) for o, chunk in chunks]
        there = [
            (block_index(self.place + o, 1 - self.core), across_cores(chunk)) for o, chunk in chunks
        ]
        self.arrived.append(here + there)

    def send(self):
        up, down = self.line.gate(*self.flying)
        if len(self.arrived) == H // 8:
            half = up.shape[0] // 2
            up, down = up[:half], down[half:]
        self.flying = up_ring(up), down_ring(down)

    def receive(self):
        hop = len(self.arrived)
        up, down = self.line.mark(*self.line.gate(*self.flying))
        if hop == H // 8:
            self.land([(hop, jnp.concatenate([up, down], axis=0))])
        else:
            self.flying = up, down
            self.land([(-hop, up), (hop, down)])


class Scatter:
    def __init__(self, line, own, other, place):
        length = H // 4
        self.line, self.place = line, place
        self.rows = own.shape[0] // length
        self.own = own.reshape(length, self.rows, D)
        self.got = across_cores(other).reshape(length, self.rows, D)
        self.hop = length // 2

    def term(self, offset):
        length = H // 4
        at = (self.place + offset) % length
        index = jnp.where(at < length // 2, 2 * at, 2 * (length - 1 - at) + 1)
        mine = lax.dynamic_index_in_dim(self.own, index, 0, keepdims=False)
        theirs = lax.dynamic_index_in_dim(self.got, index, 0, keepdims=False)
        return mine.astype(F32) + theirs.astype(F32)

    def start(self):
        self.got = self.line.gate(self.got)
        far = self.line.mark(self.term(self.hop).astype(BF))
        half = self.rows // 2
        self.flying = up_ring(far[:half]), down_ring(far[half:])

    def step(self):
        up, down = (part.astype(F32) for part in self.line.gate(*self.flying))
        if self.hop == H // 8:
            pad = jnp.zeros((self.rows // 2, D), F32)
            up, down = jnp.concatenate([up, pad], axis=0), jnp.concatenate([pad, down], axis=0)
        self.hop -= 1
        if not self.hop:
            return self.term(0) + up + down
        up = (up + self.term(self.hop)).astype(BF)
        down = (down + self.term(-self.hop)).astype(BF)
        self.line.mark(up, down)
        self.flying = up_ring(up), down_ring(down)


def settle(wholes, kept, chunks, vectors):
    rows, width = chunks[0][1].shape
    many, layers = len(chunks), 2 if vectors else 1

    def kernel(index_ref, *refs):
        blocks, rest = refs[:many], refs[many + (layers if kept else 0) :]
        outs = rest[len(vectors) : len(vectors) + layers]
        hold = rest[-1] if vectors else outs[0]
        for i, block in enumerate(blocks):

            @pl.when(pl.program_id(0) == i)
            def _(block=block):
                hold[...] = block[...]

        if vectors:
            values = hold[...].astype(F32)
            center = values - jnp.mean(values, axis=1, keepdims=True)
            scale = lax.rsqrt(jnp.mean(center * center, axis=1, keepdims=True) + 1e-05)
            normal = center * scale
            outs[0][...] = (normal * rest[0][...] + rest[1][...]).astype(BF)
            outs[1][...] = normal.astype(BF)

    whole = jax.ShapeDtypeStruct((wholes, width), BF)
    fixed = pl.BlockSpec((rows, width), lambda i, index: (0, 0))
    return pl.pallas_call(
        kernel,
        grid_spec=pltpu.PrefetchScalarGridSpec(
            num_scalar_prefetch=1,
            grid=(many,),
            in_specs=[fixed] * many
            + [pl.BlockSpec(memory_space=pl.ANY)] * (layers if kept else 0)
            + [pl.BlockSpec((1, width), lambda i, index: (0, 0))] * len(vectors),
            out_specs=[pl.BlockSpec((rows, width), lambda i, index: (index[i], 0))] * layers,
            scratch_shapes=[pltpu.VMEM((rows, width), BF)] if vectors else [],
        ),
        out_shape=[whole] * layers,
        input_output_aliases={1 + many + i: i for i in range(layers)} if kept else {},
        cost_estimate=QUICK,
        name="settle",
    )(jnp.stack([index for index, _ in chunks]), *[c for _, c in chunks], *(kept or ()), *vectors)


def turn(field, tables, sign):
    half_rot = ROT // 2
    first = pltpu.roll(field, 2 * HD - half_rot, 1)
    second = pltpu.roll(field, half_rot, 1)
    return field * tables[0] + sign * (second * tables[2] - first * tables[1])


def turn_tables(positions):
    half_rot = ROT // 2
    lane = jnp.arange(2 * HD, dtype=jnp.int32) % HD
    inverse = jnp.power(10000.0, -2.0 * (lane % half_rot).astype(F32) / ROT)
    angles = positions.astype(F32)[:, None] * inverse[None, :]
    sine = jnp.sin(angles)
    return jnp.stack(
        [
            jnp.where(lane < ROT, jnp.cos(angles), 1.0),
            jnp.where(lane < half_rot, sine, 0.0),
            jnp.where((lane >= half_rot) & (lane < ROT), sine, 0.0),
        ]
    )


def head_lanes(value, head):
    lane = lax.broadcasted_iota(jnp.int32, value.shape, 1)
    return jnp.where((lane >= HD) if head else (lane < HD), value, jnp.zeros_like(value))


def dot_of(left, right, left_dim, right_dim):
    return lax.dot_general(
        left, right, (((left_dim,), (right_dim,)), ((), ())), preferred_element_type=F32
    )


def project(normed_ref, w_ref, bias_ref, tables_ref, q_ref, k_ref, v_ref):
    width = 2 * HD
    raw = dot_of(normed_ref[...], w_ref[...], 1, 0) + bias_ref[...]
    tables = tables_ref[...]
    q_ref[...] = turn(raw[:, :width], tables, 1.0).astype(BF)
    k_ref[...] = turn(raw[:, width : 2 * width], tables, 1.0).astype(BF)
    v_ref[...] = raw[:, 2 * width :].astype(BF)


def feed(core_ref, normed_ref, att_ref, up_ref, bias_ref, down_ref, active_ref, slope_ref, *part_refs):
    root, cubic = 0.7978845608028654, 0.044715
    for side, part_ref in enumerate(part_refs):
        here = pl.ds(pl.multiple_of(BLOCK * ((core_ref[0] + side) % 2), BLOCK), BLOCK)
        hidden = dot_of(normed_ref[here, :], up_ref[...], 1, 0) + bias_ref[...]
        square = hidden * hidden
        bend = jnp.tanh(root * (hidden + cubic * (square * hidden)))
        active = (0.5 * hidden * (1.0 + bend)).astype(BF)
        active_ref[here, :] = active
        slope_ref[here, :] = 0.5 * (1.0 + bend) + 0.5 * hidden * (1.0 - bend * bend) * (
            root * (1.0 + 3.0 * cubic * square)
        )
        part = dot_of(att_ref[here, :], down_ref[: 2 * HD, :], 1, 0)
        part = part + dot_of(active, down_ref[2 * HD :, :], 1, 0)
        part_ref[...] = part.astype(BF)


def feed_back(cot_ref, down_ref, slope_ref, att_ref, hidden_ref, sum_ref):
    mixed = dot_of(cot_ref[...], down_ref[...], 1, 1)
    att_ref[...] = mixed[:, : 2 * HD].astype(BF)
    hidden = (mixed[:, 2 * HD :] * slope_ref[...]).astype(BF)
    hidden_ref[...] = hidden

    @pl.when(pl.program_id(0) == 0)
    def _():
        sum_ref[...] = jnp.zeros_like(sum_ref)

    sum_ref[...] += jnp.sum(hidden.astype(F32), axis=0, keepdims=True)


def project_back(core_ref, qkv_ref, hidden_ref, wq_ref, up_ref, normal_ref, sum_ref, *part_refs):
    @pl.when(pl.program_id(0) == 0)
    def _():
        sum_ref[...] = jnp.zeros_like(sum_ref)

    step = D // 4
    for side, part_ref in enumerate(part_refs):
        here = pl.ds(pl.multiple_of(BLOCK * ((core_ref[0] + side) % 2), BLOCK), BLOCK)
        qkv, hidden = qkv_ref[here, :], hidden_ref[here, :]
        for first in range(0, D, step):
            some = pl.ds(first, step)
            part = dot_of(qkv, wq_ref[some, :], 1, 1) + dot_of(hidden, up_ref[some, :], 1, 1)
            part_ref[:, some] = part.astype(BF)
            normal = normal_ref[here, some].astype(F32)
            sum_ref[0:1, some] += jnp.sum(part * normal, axis=0, keepdims=True)
            sum_ref[1:2, some] += jnp.sum(part, axis=0, keepdims=True)


def over_tokens(kernel, name, ins, outs, scalar=None):
    count = ins[0][0].shape[0]
    size = BLOCK if scalar is None else 2 * BLOCK
    scalars = [] if scalar is None else [jnp.reshape(scalar, (1,))]

    def spec(shape, how):
        if how in ("rows", "half"):
            rows = size if how == "rows" else size // 2
            return pl.BlockSpec((rows,) + shape[1:], lambda i, *_: (i, 0))
        if how == "tables":
            return pl.BlockSpec((shape[0], size, shape[2]), lambda i, *_: (0, i, 0))
        return pl.BlockSpec(shape, lambda i, *_: (0, 0))

    return pl.pallas_call(
        kernel,
        grid_spec=pltpu.PrefetchScalarGridSpec(
            num_scalar_prefetch=len(scalars),
            grid=(count // size,),
            in_specs=[spec(a.shape, how) for a, how in ins],
            out_specs=[spec(shape, how) for shape, _, how in outs],
        ),
        out_shape=[jax.ShapeDtypeStruct(shape, kind) for shape, kind, _ in outs],
        cost_estimate=QUICK,
        name=name,
    )(*scalars, *[a for a, _ in ins])


def key_chunk(index):
    return pl.ds(pl.multiple_of(index * KEYS, KEYS), KEYS)


def allowed_keys(starts, chunk, block):
    keys = chunk * KEYS + lax.broadcasted_iota(jnp.int32, (KEYS, BLOCK), 0)
    queries = block * BLOCK + lax.broadcasted_iota(jnp.int32, (1, BLOCK), 1)
    return (keys >= starts) & (keys <= queries)


def fold(value, how):
    return how(value.reshape(KEYS // 8, 8, BLOCK), axis=0)


def attend_forward(first_block, kept, q_ref, k_ref, v_ref, starts_ref, *refs):
    o_ref, low_ref, lse_ref, scores_ref, acc_ref, row_ref = refs[kept:]
    block = first_block + pl.program_id(0)
    query = q_ref[...] * 0.125
    queries = [head_lanes(query, head) for head in range(2)]
    starts = starts_ref[...]
    chunks = ((block + 1) * BLOCK + KEYS - 1) // KEYS
    row_ref[...] = jnp.full_like(row_ref, NEG_FILL)

    def score(chunk, carry):
        here = key_chunk(chunk)
        keys = k_ref[here, :]
        allowed = allowed_keys(starts, chunk, block)
        for head in range(2):
            scores = jnp.where(allowed, dot_of(keys, queries[head], 1, 1), NEG_FILL)
            scores_ref[head, here, :] = scores
            row_ref[head] = jnp.maximum(row_ref[head], fold(scores, jnp.max))
        return carry

    lax.fori_loop(0, chunks, score, 0)
    tops = [jnp.max(row_ref[head], axis=0, keepdims=True) for head in range(2)]
    acc_ref[...] = jnp.zeros_like(acc_ref)
    row_ref[...] = jnp.zeros_like(row_ref)

    def mix(chunk, carry):
        here = key_chunk(chunk)
        values = v_ref[here, :]
        for head in range(2):
            weights = jnp.exp(scores_ref[head, here, :] - tops[head])
            row_ref[head] += fold(weights, jnp.sum)
            acc_ref[head] += dot_of(values, weights.astype(BF), 0, 0)
        return carry

    lax.fori_loop(0, chunks, mix, 0)
    totals = [jnp.sum(row_ref[head], axis=0, keepdims=True) for head in range(2)]
    row = lax.broadcasted_iota(jnp.int32, acc_ref.shape[1:], 0)
    out = jnp.where(row < HD, acc_ref[0] / totals[0], acc_ref[1] / totals[1]).T
    o_ref[...] = out
    low_ref[...] = out.astype(BF)
    lse_ref[...] = jnp.concatenate([tops[i] + jnp.log(totals[i]) for i in range(2)], axis=0)


def attend_backward(q_ref, k_ref, v_ref, g_ref, o_ref, lse_ref, tables_ref, starts_ref, out_ref, gk_ref, gv_ref, gq_ref):
    step = pl.program_id(0)
    block = pl.num_programs(0) - 1 - step
    width = 2 * HD

    @pl.when(step == 0)
    def _():
        gk_ref[...] = jnp.zeros_like(gk_ref)
        gv_ref[...] = jnp.zeros_like(gv_ref)

    gq_ref[...] = jnp.zeros_like(gq_ref)
    query, grad = q_ref[...] * 0.125, g_ref[...]
    product = (grad.astype(F32) * o_ref[...]).T
    dots = [jnp.sum(product[i * HD : (i + 1) * HD], axis=0, keepdims=True) for i in range(2)]
    queries = [head_lanes(query, head) for head in range(2)]
    grads = [head_lanes(grad, head) for head in range(2)]
    logs = [lse_ref[head : head + 1, :] for head in range(2)]
    starts = starts_ref[...]

    def work(chunk, carry):
        here = key_chunk(chunk)
        keys, values = k_ref[here, :], v_ref[here, :]
        allowed = allowed_keys(starts, chunk, block)
        for head in range(2):
            scores = dot_of(keys, queries[head], 1, 1)
            probs = jnp.where(allowed, jnp.exp(scores - logs[head]), 0.0)
            grad_probs = dot_of(values, grads[head], 1, 1)
            grad_scores = (probs * (grad_probs - dots[head])).astype(BF)
            gv_ref[here, :] += dot_of(probs.astype(BF), grads[head], 1, 0)
            gk_ref[here, :] += dot_of(grad_scores, queries[head], 1, 0)
            gq_ref[...] += dot_of(head_lanes(keys, head), grad_scores, 0, 0)
        return carry

    lax.fori_loop(0, ((block + 1) * BLOCK + KEYS - 1) // KEYS, work, 0)
    tables = tables_ref[...]
    here = pl.ds(pl.multiple_of(block * BLOCK, BLOCK), BLOCK)

    def back(value):
        return turn(value.astype(BF).astype(F32), tables, -1.0).astype(BF)

    out_ref[:, :width] = back(gq_ref[...].T * 0.125)
    out_ref[:, width : 2 * width] = back(gk_ref[here, :])
    out_ref[:, 2 * width :] = gv_ref[here, :].astype(BF)


def attention_forward(query, key, value, starts, first, last, kept):
    count = query.shape[0]
    width = 2 * HD
    rows = lambda i: (i + first, 0)
    block = pl.BlockSpec((BLOCK, width), rows)
    row = lambda many: pl.BlockSpec((many, BLOCK), lambda i: (0, i + first))
    full = pl.BlockSpec((count, width), lambda i: (0, 0))
    return pl.pallas_call(
        partial(attend_forward, first, len(kept)),
        grid=(last - first,),
        in_specs=[block, full, full, row(1)] + [pl.BlockSpec(memory_space=pl.ANY)] * len(kept),
        out_specs=[block] * 2 + [row(2)],
        out_shape=[
            jax.ShapeDtypeStruct((count, width), F32),
            jax.ShapeDtypeStruct((count, width), BF),
            jax.ShapeDtypeStruct((2, count), F32),
        ],
        scratch_shapes=[
            pltpu.VMEM((2, count, BLOCK), F32),
            pltpu.VMEM((2, width, BLOCK), F32),
            pltpu.VMEM((2, 8, BLOCK), F32),
        ],
        input_output_aliases={4 + i: i for i in range(len(kept))},
        cost_estimate=QUICK,
        name="attend_forward",
    )(query, key, value, starts, *kept)


def attention_backward(query, key, value, grad, out, logs, tables, starts):
    count = query.shape[0]
    width = 2 * HD
    steps = count // BLOCK
    rows = lambda i: (steps - 1 - i, 0)
    block = pl.BlockSpec((BLOCK, width), rows)
    full = pl.BlockSpec((count, width), lambda i: (0, 0))
    return pl.pallas_call(
        attend_backward,
        grid=(steps,),
        in_specs=[
            block,
            full,
            full,
            block,
            block,
            pl.BlockSpec((2, BLOCK), lambda i: (0, steps - 1 - i)),
            pl.BlockSpec((3, BLOCK, width), lambda i: (0, steps - 1 - i, 0)),
            pl.BlockSpec((1, BLOCK), lambda i: (0, steps - 1 - i)),
        ],
        out_specs=pl.BlockSpec((BLOCK, 3 * width), rows),
        out_shape=jax.ShapeDtypeStruct((count, 3 * width), BF),
        scratch_shapes=[
            pltpu.VMEM((count, width), F32),
            pltpu.VMEM((count, width), F32),
            pltpu.VMEM((width, BLOCK), F32),
        ],
        cost_estimate=QUICK,
        name="attend_backward",
    )(query, key, value, grad, out, logs, tables, starts)


def unpack(rows, parts):
    many, half, _ = rows.shape
    columns = parts[1]

    def kernel(rows_ref, out_ref):
        for pair in range(many // 2):
            for part in range(parts[0]):
                lanes = slice(part * columns, (part + 1) * columns)
                first = (part * (many // 2) + pair) * columns
                for side in range(2):
                    out_ref[side * half : (side + 1) * half, first : first + columns] = rows_ref[
                        2 * pair + side, :, lanes
                    ].astype(F32)

    return pl.pallas_call(
        kernel,
        out_shape=jax.ShapeDtypeStruct((2 * half, parts[0] * columns * many // 2), F32),
        cost_estimate=QUICK,
        name="unpack",
    )(rows)


def normalize(values):
    center = values - jnp.mean(values, axis=-1, keepdims=True)
    scale = lax.rsqrt(jnp.mean(center * center, axis=-1, keepdims=True) + 1e-05)
    return center * scale, scale


def paired_step(
    inputs,
    doc_lengths,
    ln_gain,
    ln_bias,
    w_qkv,
    b_qkv,
    w_out,
    b_out,
    w_fc1,
    b_fc1,
    w_fc2,
    b_fc2,
    cotangent,
):
    rows = inputs.shape[1]
    count = rows * H
    rank = lax.axis_index("seq") * 4 + lax.axis_index("head")
    x = rank % 2
    y, core, z = (rank // 2) % 2, (rank // 4) % 2, rank // 8
    length = H // 4
    place = jnp.where(y == 0, z, length - 1 - z)

    def to_group(field):
        mine = lax.dynamic_index_in_dim(field, x, 0, keepdims=False)
        got = across_pair(lax.dynamic_index_in_dim(field, 1 - x, 0, keepdims=False))
        return jnp.where(x == 0, jnp.concatenate([mine, got]), jnp.concatenate([got, mine]))

    def from_group(field):
        mine = lax.dynamic_slice_in_dim(field, x * rows, rows, 0)
        got = across_pair(lax.dynamic_slice_in_dim(field, (1 - x) * rows, rows, 0))
        return jnp.where(x == 0, jnp.stack([mine, got]), jnp.stack([got, mine]))

    per = D // H
    per_ff = FF // H
    pairs = H // 2
    width = 2 * HD
    half = per // 2

    small = jnp.concatenate([ln_gain, ln_bias, b_out, b_fc2, b_qkv, b_fc1]).astype(BF).reshape(-1, per)
    small = jnp.pad(small, ((0, half - small.shape[0]), (0, width - per)))
    send_a = jnp.concatenate(
        [
            w_qkv.astype(BF).reshape(2, half, 3, pairs, width).transpose(3, 0, 1, 2, 4).reshape(H, half, 3 * width),
            jnp.broadcast_to(small[None], (H, half, width)),
        ],
        axis=2,
    )
    line = Line()
    gate, mark = line.gate, line.mark
    own_in = to_group(inputs)
    got_a = lax.all_to_all(send_a, AXES, 0, 0, tiled=True)
    ring_in = Gather(line, own_in, place, core)
    ring_in.send()
    mark(own_in, send_a)
    own_cot = to_group(gate(cotangent))
    send_b = mark(
        gate(w_fc1)
        .astype(BF)
        .reshape(2, half, pairs, 2 * per_ff)
        .transpose(2, 0, 1, 3)
        .reshape(H, half, 2 * per_ff)
    )
    mine_d = jnp.concatenate([gate(w_out), w_fc2], axis=0).astype(BF)
    pair_d = across_pair(mine_d)
    ring_in.receive()
    ring_in.send()
    positions = gate(jnp.arange(count, dtype=jnp.int32))
    doc_ends = jnp.cumsum(lax.dynamic_index_in_dim(doc_lengths, x, 0, keepdims=False))
    starts = jnp.max(
        jnp.where(doc_ends[:, None] <= positions[None, :], doc_ends[:, None], 0), axis=0
    )[None, :]
    tables = turn_tables(positions)
    mark(starts, tables)
    ring_in.receive()
    ring_in.send()

    got_a = gate(got_a)
    part_a = got_a[:, :, : 3 * width]
    small = got_a[:, :, 3 * width : 3 * width + per].astype(F32)
    mark(part_a, small)
    pair_a = across_pair(part_a)
    gain, shift, out_bias, down_bias = [small[:, i].reshape(1, D) for i in range(4)]
    norm = (gain, shift)
    member = rank // 2
    qkv_bias = small[:, 4:7].reshape(3, pairs, width)
    qkv_bias = lax.dynamic_index_in_dim(qkv_bias, member, 1, keepdims=False).reshape(1, 3 * width)
    up_bias = small[:, 7:11].reshape(pairs, 2 * per_ff)
    up_bias = lax.dynamic_index_in_dim(up_bias, member, 0)

    def settling(kept, hops, *vectors):
        chunks = [chunk for hop in hops for chunk in hop]
        first = gate(chunks[0][1])
        return settle(count, kept, [(chunks[0][0], first)] + chunks[1:], vectors)

    kept = mark(*settling(None, ring_in.arrived[:3], *norm))
    ring_in.receive()
    ring_in.send()
    got_b = lax.all_to_all(gate(send_b), AXES, 0, 0, tiled=True)
    kept = mark(*settling(kept, ring_in.arrived[3:4], *norm))
    ring_in.receive()

    def join(mine, got):
        low, high = jnp.where(x == 0, mine, got), jnp.where(x == 0, got, mine)
        return jnp.stack([low, high], axis=1)

    ring_cot = Gather(line, own_cot, place, core)
    ring_cot.send()
    qkv_w = mark(join(*gate(part_a, pair_a)).reshape(D, 3 * width))
    normed, normal = mark(*settling(kept, ring_in.arrived[4:], *norm))
    query, key, value = mark(
        *over_tokens(
            project,
            "project",
            [(normed, "rows"), (qkv_w, ""), (qkv_bias, ""), (tables, "tables")],
            [((count, width), BF, "rows")] * 3,
        )
    )
    ring_cot.receive()
    ring_cot.send()
    blocks = count // BLOCK
    split = blocks * 5 // 8
    kept = mark(*attention_forward(gate(query), key, value, starts, 0, split, ()))
    ring_cot.receive()
    ring_cot.send()
    got_b = mark(gate(got_b))
    pair_b = across_pair(got_b)
    out_full, attended, logs = mark(
        *attention_forward(gate(query), key, value, starts, split, blocks, kept)
    )
    ring_cot.receive()
    ring_cot.send()
    mine_d, pair_d = gate(mine_d, pair_d)
    low_d, high_d = jnp.where(x == 0, mine_d, pair_d), jnp.where(x == 0, pair_d, mine_d)
    down_w = mark(
        jnp.concatenate([low_d[:per], high_d[:per], low_d[per:], high_d[per:]], axis=0)
    )
    kept = [mark(*settling(None, ring_cot.arrived[:4]))]
    up_w = mark(join(*gate(got_b, pair_b)).reshape(D, 2 * per_ff))
    active, slope, *forward_part = mark(
        *over_tokens(
            feed,
            "feed",
            [(normed, "rows"), (attended, "rows"), (up_w, ""), (up_bias, ""), (down_w, "")],
            [((count, 2 * per_ff), BF, "rows"), ((count, 2 * per_ff), F32, "rows")]
            + [((count // 2, D), BF, "half")] * 2,
            core,
        )
    )
    forward = Scatter(line, *forward_part, place)
    ring_cot.receive()
    all_cot = mark(*settling(kept, ring_cot.arrived[4:]))
    grad_att, grad_hidden, up_sums = mark(
        *over_tokens(
            feed_back,
            "feed_back",
            [(all_cot, "rows"), (down_w, ""), (slope, "rows")],
            [((count, width), BF, "rows"), ((count, 2 * per_ff), BF, "rows"), ((1, 2 * per_ff), F32, "")],
        )
    )
    forward.start()

    def split_pair(field, axis):
        mine = lax.dynamic_index_in_dim(field, x, axis, keepdims=False)
        other = lax.dynamic_index_in_dim(field, 1 - x, axis, keepdims=False).astype(BF)
        return mine, other

    grad_up_w = mark(dot_of(normed, gate(grad_hidden), 0, 0).astype(BF))
    mine_b, other_b = mark(*split_pair(grad_up_w.reshape(H, 2, half, 2 * per_ff), 1))
    other_b = across_pair(other_b)
    forward.step()
    grad_qkv = mark(
        attention_backward(query, key, value, gate(grad_att), out_full, logs, tables, starts)
    )
    forward.step()
    mine_b, other_b = gate(mine_b, other_b)
    send_b = mark((mine_b.astype(F32) + other_b.astype(F32)).astype(BF))
    got_b = lax.all_to_all(send_b, AXES, 0, 0, tiled=True)
    norm_sums, *back_part = mark(
        *over_tokens(
            project_back,
            "project_back",
            [(gate(grad_qkv), "rows"), (grad_hidden, "rows"), (qkv_w, ""), (up_w, ""), (normal, "rows")],
            [((2, D), F32, "")] + [((count // 2, D), BF, "half")] * 2,
            core,
        )
    )
    backward = Scatter(line, *back_part, place)
    forward.step()
    grad_qkv_w = mark(dot_of(normed, gate(grad_qkv), 0, 0).astype(BF))
    mine_a, other_a = mark(*split_pair(grad_qkv_w.reshape(H, 2, half, 3 * width), 1))
    other_a = across_pair(other_a)
    backward.start()
    forward_sum = forward.step()
    output = mark((own_in.astype(F32) + (forward_sum + (out_bias + down_bias))).astype(BF))
    output = from_group(output)
    mixed = jnp.concatenate([attended, active], axis=1)
    grad_down = mark(dot_of(gate(mixed), all_cot, 0, 0))
    mine_o, other_o = split_pair(grad_down[: 2 * per].reshape(2, per, D), 0)
    mine_d, other_d = split_pair(grad_down[2 * per :].reshape(2, per_ff, D), 0)
    mark(other_o, other_d)
    other_o, other_d = across_pair(other_o), across_pair(other_d)
    backward.step()
    cot_sum = jnp.sum(own_cot.astype(F32), axis=0)
    qkv_sums = jnp.sum(gate(grad_qkv).astype(F32), axis=0).reshape(3, 1, width)
    qkv_all = lax.dynamic_update_slice(jnp.zeros((3, pairs, width), F32), qkv_sums, (0, member, 0))
    up_all = lax.dynamic_update_slice(jnp.zeros((pairs, 2 * per_ff), F32), up_sums, (member, 0))
    sums = jnp.concatenate(
        [
            norm_sums.reshape(2, H, per).transpose(1, 0, 2),
            cot_sum.reshape(H, 1, per),
            qkv_all.reshape(H, 3, per),
            up_all.reshape(H, 4, per),
        ],
        axis=1,
    )
    sums = mark(jnp.pad(sums, ((0, 0), (0, half - sums.shape[1]), (0, width - per))).astype(BF))
    mine_a, other_a = gate(mine_a, other_a)
    sum_a = (mine_a.astype(F32) + other_a.astype(F32)).astype(BF)
    send_a = mark(jnp.concatenate([sum_a, sums], axis=2))
    got_a = lax.all_to_all(send_a, AXES, 0, 0, tiled=True)
    backward.step()
    grad_up_rows = mark(unpack(gate(got_b), (1, 2 * per_ff)))
    backward.step()
    mine_o, other_o, mine_d, other_d = gate(mine_o, other_o, mine_d, other_d)
    grad_out_rows = mine_o + other_o.astype(F32)
    grad_down_rows = mine_d + other_d.astype(F32)
    mark(grad_out_rows, grad_down_rows)
    back_sum = backward.step()
    normal, scale = normalize(own_in.astype(F32))
    scaled = back_sum * gain
    grad_in = scale * (
        scaled
        - jnp.mean(scaled, axis=-1, keepdims=True)
        - normal * jnp.mean(scaled * normal, axis=-1, keepdims=True)
    )
    grad_input = mark((own_cot.astype(F32) + grad_in).astype(BF))
    grad_input = from_group(grad_input)
    got_a = gate(got_a)
    grad_qkv_rows = unpack(got_a, (3, width))
    sums = jnp.sum(got_a[:, :10, 3 * width : 3 * width + per].astype(F32), axis=0)
    return (
        output,
        grad_input,
        sums[0],
        sums[1],
        grad_qkv_rows,
        sums[3:6].reshape(-1),
        grad_out_rows,
        sums[2],
        grad_up_rows,
        sums[6:10].reshape(-1),
        grad_down_rows,
        sums[2],
    )


def solution(mesh):
    return jax.shard_map(
        paired_step if suits(mesh) else gathered_step,
        mesh=mesh,
        in_specs=(
            P(None, ("seq", "head"), None),
            P(),
            P(("seq", "head")),
            P(("seq", "head")),
            P(("seq", "head"), None),
            P(("seq", "head")),
            P(("seq", "head"), None),
            P(("seq", "head")),
            P(("seq", "head"), None),
            P(("seq", "head")),
            P(("seq", "head"), None),
            P(("seq", "head")),
            P(None, ("seq", "head"), None),
        ),
        out_specs=(
            P(None, ("seq", "head"), None),
            P(None, ("seq", "head"), None),
            P(("seq", "head")),
            P(("seq", "head")),
            P(("seq", "head"), None),
            P(("seq", "head")),
            P(("seq", "head"), None),
            P(("seq", "head")),
            P(("seq", "head"), None),
            P(("seq", "head")),
            P(("seq", "head"), None),
            P(("seq", "head")),
        ),
        check_vma=False,
    )
```

```python
from functools import partial

import jax
import jax.numpy as jnp
from jax import lax
from jax.experimental import pallas as pl
from jax.experimental.pallas import tpu as pltpu
from jax.sharding import PartitionSpec as P

D = 2048
H = 32
HD = 64
ROT = 32


NEG_FILL = -1e30


def from_behind(block, axis, distance):
    devices = range(lax.axis_size(axis))
    route = [(i - distance, i) for i in devices if i - distance in devices]
    return lax.ppermute(block, axis, route)


def from_behind_2(shard, axis, by):
    length = lax.axis_size(axis)
    return lax.ppermute(shard, axis, [(i, (i + by) % length) for i in range(length)])


def rotate(field, cosine, sine):
    half_rot = ROT // 2
    first_part = field[..., :half_rot]
    second_part = field[..., half_rot:ROT]
    return jnp.concatenate(
        [
            first_part * cosine - second_part * sine,
            second_part * cosine + first_part * sine,
            field[..., ROT:],
        ],
        axis=-1,
    )


def rotation_tables(positions):
    half_rot = ROT // 2
    inverse = jnp.power(10000.0, -2.0 * jnp.arange(half_rot, dtype=jnp.float32) / ROT)
    angles = positions.astype(jnp.float32)[:, None] * inverse[None, :]
    return (jnp.cos(angles)[:, None, :], jnp.sin(angles)[:, None, :])


def layer_norm(values, gain_value, shift_value):
    center = values - jnp.mean(values, axis=-1, keepdims=True)
    spread = jnp.mean(center * center, axis=-1, keepdims=True)
    return center * lax.rsqrt(spread + 1e-05) * gain_value + shift_value


def segment_ids(doc_ends, positions):
    return jnp.sum((doc_ends[:, None, :] <= positions[None, :, None]).astype(jnp.int32), axis=2)


def gelu_tanh(values):
    return jax.nn.gelu(values, approximate=True)


def allowed_pairs(query_pos, query_seg, key_pos, key_seg):
    return (key_pos[None, :] <= query_pos[:, None]) & (key_seg[None, :] == query_seg[:, None])


def masked_scores(query_seq, key_seq, allowed):
    raw_scores = (
        jnp.einsum("qhd,khd->hqk", query_seq, key_seq, preferred_element_type=jnp.float32) * 0.125
    )
    return jnp.where(allowed[None], raw_scores, NEG_FILL)


def forward_step(members, query_pos, key_pos):
    top_val, total_val, accum_val, query_seq, kv_seq, query_seg, key_seg = members
    kv_split = kv_seq.reshape(kv_seq.shape[0], 2, -1, HD)
    allowed = allowed_pairs(query_pos, query_seg, key_pos, key_seg)
    masked = masked_scores(query_seq, kv_split[:, 0], allowed)
    new_top = jnp.maximum(top_val, jnp.max(masked, axis=2))
    weights = jnp.where(allowed[None], jnp.exp(masked - new_top[:, :, None]), 0.0)
    factor = jnp.exp(top_val - new_top)
    new_total = total_val * factor + jnp.sum(weights, axis=2)
    new_accum = accum_val * factor[:, :, None] + jnp.einsum(
        "hqk,khd->hqd",
        weights.astype(jnp.bfloat16),
        kv_split[:, 1],
        preferred_element_type=jnp.float32,
    )
    return (new_top, new_total, new_accum)


def backward_step(members, query_pos, key_pos):
    grad_query, grad_kv, query_seq, kv_seq, grad_att, log_total, row_dot, query_seg, key_seg = (
        members
    )
    key_total = kv_seq.shape[0]
    kv_split = kv_seq.reshape(key_total, 2, -1, HD)
    allowed = allowed_pairs(query_pos, query_seg, key_pos, key_seg)
    masked = masked_scores(query_seq, kv_split[:, 0], allowed)
    prob_full = jnp.where(allowed[None], jnp.exp(masked - log_total[:, :, None]), 0.0)
    grad_value = jnp.einsum(
        "hqk,qhd->khd", prob_full.astype(jnp.bfloat16), grad_att, preferred_element_type=jnp.float32
    )
    grad_probs = jnp.einsum(
        "qhd,khd->hqk", grad_att, kv_split[:, 1], preferred_element_type=jnp.float32
    )
    grad_scores = (prob_full * (grad_probs - row_dot[:, :, None])).astype(jnp.bfloat16)
    grad_query = (
        grad_query
        + jnp.einsum(
            "hqk,khd->hqd", grad_scores, kv_split[:, 0], preferred_element_type=jnp.float32
        )
        * 0.125
    )
    grad_key = (
        jnp.einsum("hqk,qhd->khd", grad_scores, query_seq, preferred_element_type=jnp.float32)
        * 0.125
    )
    grad_kv = grad_kv + jnp.stack([grad_key, grad_value], axis=1).reshape(key_total, 2, -1)
    return (grad_query, grad_kv)


def gathered_step(
    inputs,
    doc_lengths,
    ln_gain,
    ln_bias,
    w_qkv,
    b_qkv,
    w_out,
    b_out,
    w_fc1,
    b_fc1,
    w_fc2,
    b_fc2,
    cotangent,
):
    seq_total = inputs.shape[0]
    row_count = inputs.shape[1]
    head_count = lax.axis_size("head")
    seq_devices = lax.axis_size("seq")
    heads_here = H // head_count
    group_width = heads_here * HD
    block_rows = row_count * head_count
    seq_rank = lax.axis_index("seq")
    head_rank = lax.axis_index("head")
    doc_ends = jnp.cumsum(doc_lengths, axis=1)
    token_pos = (seq_rank * head_count + head_rank) * row_count + jnp.arange(
        row_count, dtype=jnp.int32
    )
    query_start = seq_rank * block_rows
    query_pos = query_start + jnp.arange(block_rows, dtype=jnp.int32)
    query_seg = segment_ids(doc_ends, query_pos)
    gathered = (
        lax.all_gather(ln_gain.astype(jnp.bfloat16), ("seq", "head"), axis=0, tiled=True),
        lax.all_gather(ln_bias.astype(jnp.bfloat16), ("seq", "head"), axis=0, tiled=True),
        lax.all_gather(w_qkv.astype(jnp.bfloat16), ("seq", "head"), axis=0, tiled=True),
        lax.all_gather(b_qkv.astype(jnp.bfloat16), ("seq", "head"), axis=0, tiled=True),
        lax.all_gather(w_out.astype(jnp.bfloat16), ("seq", "head"), axis=0, tiled=True),
        lax.all_gather(b_out.astype(jnp.bfloat16), ("seq", "head"), axis=0, tiled=True),
        lax.all_gather(w_fc1.astype(jnp.bfloat16), ("seq", "head"), axis=0, tiled=True),
        lax.all_gather(b_fc1.astype(jnp.bfloat16), ("seq", "head"), axis=0, tiled=True),
        lax.all_gather(w_fc2.astype(jnp.bfloat16), ("seq", "head"), axis=0, tiled=True),
        lax.all_gather(b_fc2.astype(jnp.bfloat16), ("seq", "head"), axis=0, tiled=True),
    )
    (
        gain_full,
        shift_full,
        qkv_weight,
        qkv_bias,
        out_weight,
        out_bias,
        up_weight,
        up_bias,
        down_weight,
        down_bias,
    ) = gathered
    flat_in = inputs.reshape(seq_total * row_count, D).astype(jnp.float32)
    normed, norm_back = jax.vjp(
        layer_norm, flat_in, gain_full.astype(jnp.float32), shift_full.astype(jnp.float32)
    )
    normed_low = normed.astype(jnp.bfloat16)
    qkv_all = (
        jnp.dot(normed_low, qkv_weight, preferred_element_type=jnp.float32)
        + qkv_bias.astype(jnp.float32)
    ).reshape(seq_total, row_count, 3, H, HD)
    cosine, sine = rotation_tables(token_pos)

    def turn_field(field):
        return rotate(field, cosine, sine)

    query_rot, turn_back = jax.vjp(turn_field, qkv_all[:, :, 0])
    key_rot = turn_field(qkv_all[:, :, 1])
    stacked = (
        jnp.stack([query_rot, key_rot, qkv_all[:, :, 2]], axis=2)
        .reshape(seq_total, row_count, 3, D)
        .astype(jnp.bfloat16)
    )
    by_heads = lax.all_to_all(stacked, "head", split_axis=3, concat_axis=1, tiled=True)
    query_heads = by_heads[:, :, 0].reshape(seq_total, block_rows, heads_here, HD)
    kv_heads = by_heads[:, :, 1:3]
    start_state = (
        jnp.full((seq_total, heads_here, block_rows), NEG_FILL, jnp.float32),
        jnp.zeros((seq_total, heads_here, block_rows), jnp.float32),
        jnp.zeros((seq_total, heads_here, block_rows, HD), jnp.float32),
    )
    shard_piece = lax.all_gather(kv_heads, "seq", axis=1, tiled=True)

    def one_turn(turn_index, current):
        kv_block = lax.dynamic_slice_in_dim(shard_piece, turn_index * block_rows, block_rows, 1)
        key_start = turn_index * block_rows
        key_pos = key_start + jnp.arange(block_rows, dtype=jnp.int32)
        key_seg = segment_ids(doc_ends, key_pos)

        def one_compute(state_in):
            return lax.map(
                partial(forward_step, query_pos=query_pos, key_pos=key_pos),
                (state_in[0], state_in[1], state_in[2], query_heads, kv_block, query_seg, key_seg),
            )

        return lax.cond(
            key_start < query_start + block_rows, one_compute, lambda state_in: state_in, current
        )

    top_all, total_all, accum_all = lax.fori_loop(
        0, shard_piece.shape[1] // block_rows, one_turn, start_state
    )
    attn_full = accum_all / total_all[:, :, :, None]
    log_total = top_all + jnp.log(total_all)
    attn_low = (
        jnp.transpose(attn_full, (0, 2, 1, 3))
        .reshape(seq_total, block_rows, group_width)
        .astype(jnp.bfloat16)
    )
    attended = lax.all_to_all(attn_low, "head", split_axis=1, concat_axis=2, tiled=True).reshape(
        seq_total * row_count, D
    )
    branch = jnp.dot(attended, out_weight, preferred_element_type=jnp.float32) + out_bias.astype(
        jnp.float32
    )
    hidden = jnp.dot(normed_low, up_weight, preferred_element_type=jnp.float32) + up_bias.astype(
        jnp.float32
    )
    active, gelu_back = jax.vjp(gelu_tanh, hidden)
    active_low = active.astype(jnp.bfloat16)
    feed = jnp.dot(active_low, down_weight, preferred_element_type=jnp.float32) + down_bias.astype(
        jnp.float32
    )
    output = (flat_in + branch + feed).astype(jnp.bfloat16).reshape(inputs.shape)
    qkv_weight, out_weight, up_weight, down_weight = (
        lax.all_gather(w_qkv.astype(jnp.bfloat16), ("seq", "head"), axis=0, tiled=True),
        lax.all_gather(w_out.astype(jnp.bfloat16), ("seq", "head"), axis=0, tiled=True),
        lax.all_gather(w_fc1.astype(jnp.bfloat16), ("seq", "head"), axis=0, tiled=True),
        lax.all_gather(w_fc2.astype(jnp.bfloat16), ("seq", "head"), axis=0, tiled=True),
    )
    grad_low = cotangent.reshape(seq_total * row_count, D)
    grad_full = grad_low.astype(jnp.float32)
    cot_sum = jnp.sum(grad_full, axis=0)
    grad_down_w = jnp.einsum("nf,nd->fd", active_low, grad_low, preferred_element_type=jnp.float32)
    grad_active = jnp.einsum("nd,fd->nf", grad_low, down_weight, preferred_element_type=jnp.float32)
    grad_hidden_low = gelu_back(grad_active)[0].astype(jnp.bfloat16)
    grad_up_w = jnp.einsum(
        "nm,nf->mf", normed_low, grad_hidden_low, preferred_element_type=jnp.float32
    )
    grad_up_b = jnp.sum(grad_hidden_low.astype(jnp.float32), axis=0)
    grad_normed = jnp.einsum(
        "nf,mf->nm", grad_hidden_low, up_weight, preferred_element_type=jnp.float32
    )
    grad_out_w = jnp.einsum("nm,nd->md", attended, grad_low, preferred_element_type=jnp.float32)
    grad_att_low = jnp.einsum(
        "nd,md->nm", grad_low, out_weight, preferred_element_type=jnp.float32
    ).astype(jnp.bfloat16)
    grad_heads = lax.all_to_all(
        grad_att_low.reshape(seq_total, row_count, D),
        "head",
        split_axis=2,
        concat_axis=1,
        tiled=True,
    ).reshape(seq_total, block_rows, heads_here, HD)
    row_dot = jnp.sum(
        jnp.transpose(grad_heads.astype(jnp.float32), (0, 2, 1, 3)) * attn_full, axis=3
    )

    def back_turn(turn_index, current):
        grad_query, grad_kv, kv_now = current
        source = (seq_rank - turn_index) % seq_devices
        key_pos = source * block_rows + jnp.arange(block_rows, dtype=jnp.int32)
        key_seg = segment_ids(doc_ends, key_pos)

        def back_compute(grads_in):
            return lax.map(
                partial(backward_step, query_pos=query_pos, key_pos=key_pos),
                (
                    grads_in[0],
                    grads_in[1],
                    query_heads,
                    kv_now,
                    grad_heads,
                    log_total,
                    row_dot,
                    query_seg,
                    key_seg,
                ),
            )

        return lax.cond(
            source <= seq_rank, back_compute, lambda grads_in: grads_in, (grad_query, grad_kv)
        )

    def pass_keys(kv_now):
        return from_behind(kv_now, "seq", 1)

    def pass_grads(grad_kv):
        return from_behind_2(grad_kv.astype(jnp.bfloat16), "seq", 1).astype(grad_kv.dtype)

    def loop_turn(turn_index, current):
        grad_query, grad_kv = back_turn(turn_index, current)
        return (grad_query, pass_grads(grad_kv), pass_keys(current[2]))

    start_grads = (
        jnp.zeros((seq_total, heads_here, block_rows, HD), jnp.float32),
        jnp.zeros((seq_total, block_rows, 2, group_width), jnp.float32),
        kv_heads,
    )
    loop_state = lax.fori_loop(0, seq_devices - 1, loop_turn, start_grads)
    grad_query, grad_kv = back_turn(seq_devices - 1, loop_state)
    grad_kv = pass_grads(grad_kv)
    back_heads = jnp.concatenate(
        [
            jnp.transpose(grad_query, (0, 2, 1, 3)).reshape(seq_total, block_rows, 1, group_width),
            grad_kv,
        ],
        axis=2,
    ).astype(jnp.bfloat16)
    back_tokens = (
        lax.all_to_all(back_heads, "head", split_axis=1, concat_axis=3, tiled=True)
        .astype(jnp.float32)
        .reshape(seq_total, row_count, 3, H, HD)
    )
    grad_qkv_low = (
        jnp.stack(
            [
                turn_back(back_tokens[:, :, 0])[0],
                turn_back(back_tokens[:, :, 1])[0],
                back_tokens[:, :, 2],
            ],
            axis=2,
        )
        .reshape(seq_total * row_count, 3 * D)
        .astype(jnp.bfloat16)
    )
    grad_qkv_w = jnp.einsum(
        "nm,nk->mk", normed_low, grad_qkv_low, preferred_element_type=jnp.float32
    )
    grad_qkv_b = jnp.sum(grad_qkv_low.astype(jnp.float32), axis=0)
    grad_normed = grad_normed + jnp.einsum(
        "nk,mk->nm", grad_qkv_low, qkv_weight, preferred_element_type=jnp.float32
    )
    grad_in, grad_gain, grad_shift = norm_back(grad_normed)
    grad_input = (grad_full + grad_in).astype(jnp.bfloat16).reshape(inputs.shape)
    sums_all = (
        lax.psum_scatter(grad_gain, ("seq", "head"), scatter_dimension=0, tiled=True),
        lax.psum_scatter(grad_shift, ("seq", "head"), scatter_dimension=0, tiled=True),
        lax.psum_scatter(grad_qkv_w, ("seq", "head"), scatter_dimension=0, tiled=True),
        lax.psum_scatter(grad_qkv_b, ("seq", "head"), scatter_dimension=0, tiled=True),
        lax.psum_scatter(grad_out_w, ("seq", "head"), scatter_dimension=0, tiled=True),
        lax.psum_scatter(cot_sum, ("seq", "head"), scatter_dimension=0, tiled=True),
        lax.psum_scatter(grad_up_w, ("seq", "head"), scatter_dimension=0, tiled=True),
        lax.psum_scatter(grad_up_b, ("seq", "head"), scatter_dimension=0, tiled=True),
        lax.psum_scatter(grad_down_w, ("seq", "head"), scatter_dimension=0, tiled=True),
    )
    return (
        output,
        grad_input,
        sums_all[0],
        sums_all[1],
        sums_all[2],
        sums_all[3],
        sums_all[4],
        sums_all[5],
        sums_all[6],
        sums_all[7],
        sums_all[8],
        sums_all[5],
    )


BF = jnp.bfloat16
F32 = jnp.float32
AXES = ("seq", "head")
FF = 8192
BLOCK = 256
KEYS = 512


QUICK = pl.CostEstimate(flops=1 << 20, bytes_accessed=1 << 16, transcendentals=0)


def suits(mesh):
    return mesh.shape["seq"] * mesh.shape["head"] == H and mesh.shape["head"] == 4


def coordinates(rank):
    return rank // 8, (rank // 4) % 2, (rank // 2) % 2, rank % 2


def rank_of(z, core, y, x):
    return ((z * 2 + core) * 2 + y) * 2 + x


def route(step):
    return [(rank, rank_of(*step(*coordinates(rank)))) for rank in range(H)]


def ring_place(z, y, length):
    return z if y == 0 else length - 1 - z


def ring_point(place, length):
    place = place % length
    return (place, 0) if place < length // 2 else (length - 1 - place, 1)


def ring_route(by):
    length = H // 4

    def step(z, core, y, x):
        new_z, new_y = ring_point(ring_place(z, y, length) + by, length)
        return new_z, core, new_y, x

    return route(step)


def across_pair(value):
    return lax.ppermute(value, AXES, route(lambda z, core, y, x: (z, core, y, 1 - x)))


def across_cores(value):
    return lax.ppermute(value, AXES, route(lambda z, core, y, x: (z, 1 - core, y, x)))


def up_ring(value):
    return lax.ppermute(value, AXES, ring_route(1))


def down_ring(value):
    return lax.ppermute(value, AXES, ring_route(-1))


def block_index(place, core):
    length = H // 4
    place = place % length
    z = jnp.where(place < length // 2, place, length - 1 - place)
    y = (place >= length // 2).astype(jnp.int32)
    return (z * 2 + core) * 2 + y


def fence(value, *others):
    anywhere = pl.BlockSpec(memory_space=pl.ANY)
    return pl.pallas_call(
        lambda *refs: None,
        in_specs=[anywhere] * (1 + len(others)),
        out_specs=anywhere,
        out_shape=jax.ShapeDtypeStruct(value.shape, value.dtype),
        input_output_aliases={0: 0},
        cost_estimate=QUICK,
        name="fence",
    )(value, *others)


class Line:
    def __init__(self):
        self.last = ()

    def gate(self, *values):
        values = lax.optimization_barrier((values, self.last))[0] if self.last else values
        return values if len(values) > 1 else values[0]

    def mark(self, *values):
        self.last = values
        return values if len(values) > 1 else values[0]


class Gather:
    def __init__(self, line, own, place, core):
        self.line, self.place, self.core = line, place, core
        self.flying = (own, own)
        self.arrived, self.hop = [], 0
        self.land([(0, own)])

    def land(self, chunks):
        self.arrived += [(self.place + offset, chunk, across_cores(chunk)) for offset, chunk in chunks]
        self.hop = self.hop + 1

    def send(self):
        up, down = self.line.gate(*self.flying)
        if self.hop == H // 8:
            half = up.shape[0] // 2
            up, down = up[:half], down[half:]
        self.flying = up_ring(up), down_ring(down)

    def receive(self):
        hop = self.hop
        before = [other for _, _, other in self.arrived[-2:]]
        up, down, *before = self.line.mark(*self.line.gate(*self.flying, *before))
        for i, other in enumerate(before, len(self.arrived) - len(before)):
            self.arrived[i] = (*self.arrived[i][:2], other)
        if hop == H // 8:
            self.land([(hop, jnp.concatenate([up, down], axis=0))])
        else:
            self.flying = up, down
            self.land([(-hop, up), (hop, down)])


class Scatter:
    def __init__(self, line, own, other, place):
        length = H // 4
        self.line, self.place = line, place
        self.rows = own.shape[0] // length
        self.own = own.reshape(length, self.rows, D)
        self.got = across_cores(other).reshape(length, self.rows, D)
        self.hop = length // 2

    def term(self, offset):
        length = H // 4
        at = (self.place + offset) % length
        index = jnp.where(at < length // 2, 2 * at, 2 * (length - 1 - at) + 1)
        mine = lax.dynamic_index_in_dim(self.own, index, 0, keepdims=False)
        theirs = lax.dynamic_index_in_dim(self.got, index, 0, keepdims=False)
        return mine.astype(F32) + theirs.astype(F32)

    def start(self):
        self.got = self.line.gate(self.got)
        far = self.line.mark(self.term(self.hop).astype(BF))
        half = self.rows // 2
        self.flying = up_ring(far[:half]), down_ring(far[half:])

    def step(self):
        up, down = (part.astype(F32) for part in self.line.gate(*self.flying))
        if self.hop == H // 8:
            pad = jnp.zeros((self.rows // 2, D), F32)
            up, down = jnp.concatenate([up, pad], axis=0), jnp.concatenate([pad, down], axis=0)
        self.hop -= 1
        if not self.hop:
            return self.term(0) + up + down
        up = (up + self.term(self.hop)).astype(BF)
        down = (down + self.term(-self.hop)).astype(BF)
        self.line.mark(up, down)
        self.flying = up_ring(up), down_ring(down)


class Scatter:
    def __init__(self, line, own, other, place):
        length = H // 4
        self.line, self.place = line, place
        self.rows = own.shape[0] // length
        self.own = own.reshape(length, self.rows, D)
        self.got = across_cores(other).reshape(length, self.rows, D)
        self.hop = length // 2

    def term(self, offset):
        length = H // 4
        at = (self.place + offset) % length
        index = jnp.where(at < length // 2, 2 * at, 2 * (length - 1 - at) + 1)
        mine = lax.dynamic_index_in_dim(self.own, index, 0, keepdims=False)
        theirs = lax.dynamic_index_in_dim(self.got, index, 0, keepdims=False)
        return mine.astype(F32) + theirs.astype(F32)

    def start(self):
        self.got = self.line.gate(self.got)
        far = self.line.mark(self.term(self.hop).astype(BF))
        half = self.rows // 2
        self.flying = up_ring(far[:half]), down_ring(far[half:])

    def step(self):
        up, down = (part.astype(F32) for part in self.line.gate(*self.flying))
        if self.hop == H // 8:
            pad = jnp.zeros((self.rows // 2, D), F32)
            up, down = jnp.concatenate([up, pad], axis=0), jnp.concatenate([pad, down], axis=0)
        self.hop -= 1
        if not self.hop:
            return self.term(0) + up + down
        up = (up + self.term(self.hop)).astype(BF)
        down = (down + self.term(-self.hop)).astype(BF)
        self.line.mark(up, down)
        self.flying = up_ring(up), down_ring(down)


def settle(wholes, kept, chunks, vectors):
    rows, width = chunks[0][1].shape
    many, layers = len(chunks), 2 if vectors else 1

    def kernel(index_ref, *refs):
        blocks, rest = refs[:many], refs[many + (layers if kept else 0) :]
        outs = rest[len(vectors) : len(vectors) + layers]
        hold = rest[-1] if vectors else outs[0]
        for i, block in enumerate(blocks):

            @pl.when(pl.program_id(0) == i)
            def _(block=block):
                hold[...] = block[...]

        if vectors:
            values = hold[...].astype(F32)
            center = values - jnp.mean(values, axis=1, keepdims=True)
            scale = lax.rsqrt(jnp.mean(center * center, axis=1, keepdims=True) + 1e-05)
            normal = center * scale
            outs[0][...] = (normal * rest[0][...] + rest[1][...]).astype(BF)
            outs[1][...] = normal.astype(BF)

    whole = jax.ShapeDtypeStruct((wholes, width), BF)
    fixed = pl.BlockSpec((rows, width), lambda i, index: (0, 0))
    return pl.pallas_call(
        kernel,
        grid_spec=pltpu.PrefetchScalarGridSpec(
            num_scalar_prefetch=1,
            grid=(many,),
            in_specs=[fixed] * many
            + [pl.BlockSpec(memory_space=pl.ANY)] * (layers if kept else 0)
            + [pl.BlockSpec((1, width), lambda i, index: (0, 0))] * len(vectors),
            out_specs=[pl.BlockSpec((rows, width), lambda i, index: (index[i], 0))] * layers,
            scratch_shapes=[pltpu.VMEM((rows, width), BF)] if vectors else [],
        ),
        out_shape=[whole] * layers,
        input_output_aliases={1 + many + i: i for i in range(layers)} if kept else {},
        cost_estimate=QUICK,
        name="settle",
    )(jnp.stack([index for index, _ in chunks]), *[c for _, c in chunks], *(kept or ()), *vectors)


def turn(field, tables, sign):
    half_rot = ROT // 2
    first = pltpu.roll(field, 2 * HD - half_rot, 1)
    second = pltpu.roll(field, half_rot, 1)
    return field * tables[0] + sign * (second * tables[2] - first * tables[1])


def turn_tables(positions):
    half_rot = ROT // 2
    lane = jnp.arange(2 * HD, dtype=jnp.int32) % HD
    inverse = jnp.power(10000.0, -2.0 * (lane % half_rot).astype(F32) / ROT)
    angles = positions.astype(F32)[:, None] * inverse[None, :]
    sine = jnp.sin(angles)
    return jnp.stack(
        [
            jnp.where(lane < ROT, jnp.cos(angles), 1.0),
            jnp.where(lane < half_rot, sine, 0.0),
            jnp.where((lane >= half_rot) & (lane < ROT), sine, 0.0),
        ]
    )


def head_lanes(value, head):
    lane = lax.broadcasted_iota(jnp.int32, value.shape, 1)
    return jnp.where((lane >= HD) if head else (lane < HD), value, jnp.zeros_like(value))


def dot_of(left, right, left_dim, right_dim):
    return lax.dot_general(
        left, right, (((left_dim,), (right_dim,)), ((), ())), preferred_element_type=F32
    )


def project(values, gain_ref, shift_ref, w_ref, bias_ref, tables_ref, normed_ref, q_ref, k_ref, v_ref):
    values = values.astype(F32)
    center = values - jnp.mean(values, axis=1, keepdims=True)
    scale = lax.rsqrt(jnp.mean(center * center, axis=1, keepdims=True) + 1e-05)
    normed = (center * scale * gain_ref[...] + shift_ref[...]).astype(BF)
    normed_ref[...] = normed.reshape(normed_ref.shape)
    width = 2 * HD
    raw = dot_of(normed, w_ref[...], 1, 0) + bias_ref[...]
    tables = tables_ref[...].reshape(3, BLOCK, width)
    q_ref[...] = turn(raw[:, :width], tables, 1.0).astype(BF).reshape(q_ref.shape)
    k_ref[...] = turn(raw[:, width : 2 * width], tables, 1.0).astype(BF).reshape(k_ref.shape)
    v_ref[...] = raw[:, 2 * width :].astype(BF).reshape(v_ref.shape)


def feed(core_ref, normed_ref, att_ref, up_ref, bias_ref, down_ref, mixed_ref, slope_ref, *part_refs):
    root, cubic = 0.7978845608028654, 0.044715
    for side, part_ref in enumerate(part_refs):
        here = pl.ds(pl.multiple_of(BLOCK * ((core_ref[0] + side) % 2), BLOCK), BLOCK)
        hidden = dot_of(normed_ref[here, :], up_ref[...], 1, 0) + bias_ref[...]
        square = hidden * hidden
        bend = jnp.tanh(root * (hidden + cubic * (square * hidden)))
        active = (0.5 * hidden * (1.0 + bend)).astype(BF)
        mixed_ref[here, : 2 * HD] = att_ref[here, :]
        mixed_ref[here, 2 * HD :] = active
        slope_ref[here, :] = 0.5 * (1.0 + bend) + 0.5 * hidden * (1.0 - bend * bend) * (
            root * (1.0 + 3.0 * cubic * square)
        )
        part = dot_of(att_ref[here, :], down_ref[: 2 * HD, :], 1, 0)
        part = part + dot_of(active, down_ref[2 * HD :, :], 1, 0)
        part_ref[...] = part.astype(BF)


def feed_back(cot, down_ref, slope_ref, att_ref, hidden_ref, whole_ref, sum_ref):
    whole_ref[...] = cot.reshape(whole_ref.shape)
    mixed = dot_of(cot, down_ref[...], 1, 1)
    att_ref[...] = mixed[:, : 2 * HD].astype(BF).reshape(att_ref.shape)
    slope = slope_ref[...].reshape(BLOCK, slope_ref.shape[-1])
    hidden = (mixed[:, 2 * HD :] * slope).astype(BF)
    hidden_ref[...] = hidden.reshape(hidden_ref.shape)

    @pl.when(pl.program_id(0) == 0)
    def _():
        sum_ref[...] = jnp.zeros_like(sum_ref)

    sum_ref[...] += jnp.sum(hidden.astype(F32), axis=0, keepdims=True)


def project_back(core_ref, qkv_ref, hidden_ref, wq_ref, up_ref, normed_ref, gain_ref, shift_ref, sum_ref, *part_refs):
    @pl.when(pl.program_id(0) == 0)
    def _():
        sum_ref[...] = jnp.zeros_like(sum_ref)

    step = D // 4
    for side, part_ref in enumerate(part_refs):
        here = pl.ds(pl.multiple_of(BLOCK * ((core_ref[0] + side) % 2), BLOCK), BLOCK)
        qkv, hidden = qkv_ref[here, :], hidden_ref[here, :]
        for first in range(0, D, step):
            some = pl.ds(first, step)
            part = dot_of(qkv, wq_ref[some, :], 1, 1) + dot_of(hidden, up_ref[some, :], 1, 1)
            part_ref[:, some] = part.astype(BF)
            normal = (normed_ref[here, some].astype(F32) - shift_ref[:, some]) / gain_ref[:, some]
            sum_ref[0:1, some] += jnp.sum(part * normal, axis=0, keepdims=True)
            sum_ref[1:2, some] += jnp.sum(part, axis=0, keepdims=True)


def over_arrivals(kernel, name, arrived, core, ins, outs):
    length = H // 4
    rows, lanes = arrived[0][1].shape
    places = jnp.stack([place for place, _, _ in arrived]) % length
    y = (places >= length // 2).astype(jnp.int32)
    z = jnp.where(y == 0, places, length - 1 - places)
    lead = (length // 2, 2, 2, rows)

    def body(core_ref, z_ref, y_ref, *refs):
        blocks, rest, hold = refs[: 2 * length], refs[2 * length : -1], refs[-1]
        for step in range(length):

            @pl.when(pl.program_id(0) == step)
            def _(step=step):
                for side in range(2):
                    first = pl.multiple_of(rows * ((core_ref[0] + side) % 2), rows)
                    hold[pl.ds(first, rows), :] = blocks[2 * step + side][...]

        kernel(hold[...], *rest)

    def view(array, how):
        if how == "rows":
            return array.reshape(lead + array.shape[1:])
        return array.reshape(array.shape[:1] + lead + array.shape[2:]) if how == "tables" else array

    def spec(shape, how):
        if how == "rows":
            return pl.BlockSpec((1, 2, 1, rows, shape[-1]), lambda i, c, z, y: (z[i], 0, y[i], 0, 0))
        if how == "tables":
            return pl.BlockSpec(
                (shape[0], 1, 2, 1, rows, shape[-1]), lambda i, c, z, y: (0, z[i], 0, y[i], 0, 0)
            )
        return pl.BlockSpec(shape, lambda i, *_: (0, 0))

    once = pl.BlockSpec((rows, lanes), lambda i, *_: (0, 0), pipeline_mode=pl.Buffered(1))
    results = pl.pallas_call(
        body,
        grid_spec=pltpu.PrefetchScalarGridSpec(
            num_scalar_prefetch=3,
            grid=(length,),
            in_specs=[once] * (2 * length) + [spec(a.shape, how) for a, how in ins],
            out_specs=[spec(shape, how) for shape, _, how in outs],
            scratch_shapes=[pltpu.VMEM((2 * rows, lanes), BF)],
        ),
        out_shape=[
            jax.ShapeDtypeStruct(lead + shape[1:] if how == "rows" else shape, kind)
            for shape, kind, how in outs
        ],
        cost_estimate=QUICK,
        name=name,
    )(
        jnp.reshape(core, (1,)),
        z,
        y,
        *[block for _, mine, other in arrived for block in (mine, other)],
        *[view(a, how) for a, how in ins],
    )
    return [result.reshape(shape) for result, (shape, _, _) in zip(results, outs)]


def over_tokens(kernel, name, ins, outs, scalar=None):
    count = ins[0][0].shape[0]
    size = BLOCK if scalar is None else 2 * BLOCK
    scalars = [] if scalar is None else [jnp.reshape(scalar, (1,))]

    def spec(shape, how):
        if how in ("rows", "half"):
            rows = size if how == "rows" else size // 2
            return pl.BlockSpec((rows,) + shape[1:], lambda i, *_: (i, 0))
        if how == "tables":
            return pl.BlockSpec((shape[0], size, shape[2]), lambda i, *_: (0, i, 0))
        return pl.BlockSpec(shape, lambda i, *_: (0, 0))

    return pl.pallas_call(
        kernel,
        grid_spec=pltpu.PrefetchScalarGridSpec(
            num_scalar_prefetch=len(scalars),
            grid=(count // size,),
            in_specs=[spec(a.shape, how) for a, how in ins],
            out_specs=[spec(shape, how) for shape, _, how in outs],
        ),
        out_shape=[jax.ShapeDtypeStruct(shape, kind) for shape, kind, _ in outs],
        cost_estimate=QUICK,
        name=name,
    )(*scalars, *[a for a, _ in ins])


def key_chunk(index):
    return pl.ds(pl.multiple_of(index * KEYS, KEYS), KEYS)


def allowed_keys(starts, chunk, block):
    keys = chunk * KEYS + lax.broadcasted_iota(jnp.int32, (KEYS, BLOCK), 0)
    queries = block * BLOCK + lax.broadcasted_iota(jnp.int32, (1, BLOCK), 1)
    return (keys >= starts) & (keys <= queries)


def fold(value, how):
    return how(value.reshape(KEYS // 8, 8, BLOCK), axis=0)


def attend_forward(first_block, kept, q_ref, k_ref, v_ref, starts_ref, *refs):
    o_ref, low_ref, lse_ref, scores_ref, acc_ref, row_ref = refs[kept:]
    block = first_block + pl.program_id(0)
    query = q_ref[...] * 0.125
    queries = [head_lanes(query, head) for head in range(2)]
    starts = starts_ref[...]
    chunks = ((block + 1) * BLOCK + KEYS - 1) // KEYS
    row_ref[...] = jnp.full_like(row_ref, NEG_FILL)

    def score(chunk, carry):
        here = key_chunk(chunk)
        keys = k_ref[here, :]
        allowed = allowed_keys(starts, chunk, block)
        for head in range(2):
            scores = jnp.where(allowed, dot_of(keys, queries[head], 1, 1), NEG_FILL)
            scores_ref[head, here, :] = scores
            row_ref[head] = jnp.maximum(row_ref[head], fold(scores, jnp.max))
        return carry

    lax.fori_loop(0, chunks, score, 0)
    tops = [jnp.max(row_ref[head], axis=0, keepdims=True) for head in range(2)]
    acc_ref[...] = jnp.zeros_like(acc_ref)
    row_ref[...] = jnp.zeros_like(row_ref)

    def mix(chunk, carry):
        here = key_chunk(chunk)
        values = v_ref[here, :]
        for head in range(2):
            weights = jnp.exp(scores_ref[head, here, :] - tops[head])
            row_ref[head] += fold(weights, jnp.sum)
            acc_ref[head] += dot_of(values, weights.astype(BF), 0, 0)
        return carry

    lax.fori_loop(0, chunks, mix, 0)
    totals = [jnp.sum(row_ref[head], axis=0, keepdims=True) for head in range(2)]
    row = lax.broadcasted_iota(jnp.int32, acc_ref.shape[1:], 0)
    out = jnp.where(row < HD, acc_ref[0] / totals[0], acc_ref[1] / totals[1]).T
    o_ref[...] = out
    low_ref[...] = out.astype(BF)
    lse_ref[...] = jnp.concatenate([tops[i] + jnp.log(totals[i]) for i in range(2)], axis=0)


def attend_backward(last_block, kept, q_ref, k_ref, v_ref, g_ref, o_ref, lse_ref, tables_ref, starts_ref, *refs):
    before, (out_ref, gk_ref, gv_ref, gq_ref) = refs[:kept], refs[kept:]
    step = pl.program_id(0)
    block = last_block - step
    width = 2 * HD

    @pl.when(step == 0)
    def _():
        gk_ref[...] = before[1][...] if kept else jnp.zeros_like(gk_ref)
        gv_ref[...] = before[2][...] if kept else jnp.zeros_like(gv_ref)

    gq_ref[...] = jnp.zeros_like(gq_ref)
    query, grad = q_ref[...] * 0.125, g_ref[...]
    product = (grad.astype(F32) * o_ref[...]).T
    dots = [jnp.sum(product[i * HD : (i + 1) * HD], axis=0, keepdims=True) for i in range(2)]
    queries = [head_lanes(query, head) for head in range(2)]
    grads = [head_lanes(grad, head) for head in range(2)]
    logs = [lse_ref[head : head + 1, :] for head in range(2)]
    starts = starts_ref[...]

    def work(chunk, carry):
        here = key_chunk(chunk)
        keys, values = k_ref[here, :], v_ref[here, :]
        allowed = allowed_keys(starts, chunk, block)
        for head in range(2):
            scores = dot_of(keys, queries[head], 1, 1)
            probs = jnp.where(allowed, jnp.exp(scores - logs[head]), 0.0)
            grad_probs = dot_of(values, grads[head], 1, 1)
            grad_scores = (probs * (grad_probs - dots[head])).astype(BF)
            gv_ref[here, :] += dot_of(probs.astype(BF), grads[head], 1, 0)
            gk_ref[here, :] += dot_of(grad_scores, queries[head], 1, 0)
            gq_ref[...] += dot_of(head_lanes(keys, head), grad_scores, 0, 0)
        return carry

    lax.fori_loop(0, ((block + 1) * BLOCK + KEYS - 1) // KEYS, work, 0)
    tables = tables_ref[...]
    here = pl.ds(pl.multiple_of(block * BLOCK, BLOCK), BLOCK)

    def back(value):
        return turn(value.astype(BF).astype(F32), tables, -1.0).astype(BF)

    out_ref[:, :width] = back(gq_ref[...].T * 0.125)
    out_ref[:, width : 2 * width] = back(gk_ref[here, :])
    out_ref[:, 2 * width :] = gv_ref[here, :].astype(BF)


def attention_forward(query, key, value, starts, first, last, kept):
    count = query.shape[0]
    width = 2 * HD
    rows = lambda i: (i + first, 0)
    block = pl.BlockSpec((BLOCK, width), rows)
    row = lambda many: pl.BlockSpec((many, BLOCK), lambda i: (0, i + first))
    full = pl.BlockSpec((count, width), lambda i: (0, 0))
    return pl.pallas_call(
        partial(attend_forward, first, len(kept)),
        grid=(last - first,),
        in_specs=[block, full, full, row(1)] + [pl.BlockSpec(memory_space=pl.ANY)] * len(kept),
        out_specs=[block] * 2 + [row(2)],
        out_shape=[
            jax.ShapeDtypeStruct((count, width), F32),
            jax.ShapeDtypeStruct((count, width), BF),
            jax.ShapeDtypeStruct((2, count), F32),
        ],
        scratch_shapes=[
            pltpu.VMEM((2, count, BLOCK), F32),
            pltpu.VMEM((2, width, BLOCK), F32),
            pltpu.VMEM((2, 8, BLOCK), F32),
        ],
        input_output_aliases={4 + i: i for i in range(len(kept))},
        cost_estimate=QUICK,
        name="attend_forward",
    )(query, key, value, starts, *kept)


def attention_backward(query, key, value, grad, out, logs, tables, starts, first, last, kept):
    count = query.shape[0]
    width = 2 * HD
    rows = lambda i: (last - 1 - i, 0)
    block = pl.BlockSpec((BLOCK, width), rows)
    full = pl.BlockSpec((count, width), lambda i: (0, 0))
    row = lambda many: pl.BlockSpec((many, BLOCK), lambda i: (0, last - 1 - i))
    return pl.pallas_call(
        partial(attend_backward, last - 1, len(kept)),
        grid=(last - first,),
        in_specs=[
            block,
            full,
            full,
            block,
            block,
            row(2),
            pl.BlockSpec((3, BLOCK, width), lambda i: (0, last - 1 - i, 0)),
            row(1),
        ]
        + [pl.BlockSpec(memory_space=pl.ANY), full, full][: len(kept)],
        out_specs=[pl.BlockSpec((BLOCK, 3 * width), rows), full, full],
        out_shape=[
            jax.ShapeDtypeStruct((count, 3 * width), BF),
            jax.ShapeDtypeStruct((count, width), F32),
            jax.ShapeDtypeStruct((count, width), F32),
        ],
        scratch_shapes=[pltpu.VMEM((width, BLOCK), F32)],
        input_output_aliases={8: 0} if kept else {},
        cost_estimate=QUICK,
        name="attend_backward",
    )(query, key, value, grad, out, logs, tables, starts, *kept)


def unpack(rows, parts):
    many, half, _ = rows.shape
    columns = parts[1]

    def kernel(rows_ref, out_ref):
        for pair in range(many // 2):
            for part in range(parts[0]):
                lanes = slice(part * columns, (part + 1) * columns)
                first = (part * (many // 2) + pair) * columns
                for side in range(2):
                    out_ref[side * half : (side + 1) * half, first : first + columns] = rows_ref[
                        2 * pair + side, :, lanes
                    ].astype(F32)

    return pl.pallas_call(
        kernel,
        out_shape=jax.ShapeDtypeStruct((2 * half, parts[0] * columns * many // 2), F32),
        cost_estimate=QUICK,
        name="unpack",
    )(rows)


def normalize(values):
    center = values - jnp.mean(values, axis=-1, keepdims=True)
    scale = lax.rsqrt(jnp.mean(center * center, axis=-1, keepdims=True) + 1e-05)
    return center * scale, scale


def paired_step(
    inputs,
    doc_lengths,
    ln_gain,
    ln_bias,
    w_qkv,
    b_qkv,
    w_out,
    b_out,
    w_fc1,
    b_fc1,
    w_fc2,
    b_fc2,
    cotangent,
):
    rows = inputs.shape[1]
    count = rows * H
    rank = lax.axis_index("seq") * 4 + lax.axis_index("head")
    x = rank % 2
    y, core, z = (rank // 2) % 2, (rank // 4) % 2, rank // 8
    length = H // 4
    place = jnp.where(y == 0, z, length - 1 - z)

    def split_rows(field):
        mine = lax.dynamic_slice_in_dim(field, x * rows, rows, 0)
        return mine, across_pair(lax.dynamic_slice_in_dim(field, (1 - x) * rows, rows, 0))

    def join_rows(mine, got):
        return jnp.where(x == 0, jnp.stack([mine, got]), jnp.stack([got, mine]))

    per = D // H
    per_ff = FF // H
    pairs = H // 2
    width = 2 * HD
    half = per // 2

    line = Line()
    gate, mark = line.gate, line.mark

    def pair_blocks(field):
        mine = lax.dynamic_index_in_dim(field, x, 0, keepdims=False)
        return mine, lax.dynamic_index_in_dim(field, 1 - x, 0, keepdims=False)

    def pair_rows(mine, got):
        return jnp.where(x == 0, jnp.concatenate([mine, got]), jnp.concatenate([got, mine]))

    mine_in, other_in = mark(*pair_blocks(inputs))
    got_in = across_pair(other_in)
    small = jnp.concatenate([ln_gain, ln_bias, b_out, b_fc2, b_qkv, b_fc1]).astype(BF).reshape(-1, per)
    small = jnp.pad(small, ((0, half - small.shape[0]), (0, width - per)))
    send_a = jnp.concatenate(
        [
            gate(w_qkv).astype(BF).reshape(2, half, 3, pairs, width).transpose(3, 0, 1, 2, 4).reshape(H, half, 3 * width),
            jnp.broadcast_to(small[None], (H, half, width)),
        ],
        axis=2,
    )
    own_in = mark(pair_rows(mine_in, got_in))
    ring_in = Gather(line, own_in, place, core)
    ring_in.send()
    send_a = mark(gate(send_a))
    got_a = lax.all_to_all(send_a, AXES, 0, 0, tiled=True)
    mine_cot, other_cot = pair_blocks(gate(cotangent))
    mine_d = jnp.concatenate([gate(w_out), w_fc2], axis=0).astype(BF)
    mark(other_cot, mine_d)
    got_cot = across_pair(other_cot)
    pair_d = across_pair(mine_d)
    send_b = mark(
        gate(w_fc1)
        .astype(BF)
        .reshape(2, half, pairs, 2 * per_ff)
        .transpose(2, 0, 1, 3)
        .reshape(H, half, 2 * per_ff)
    )
    positions = gate(jnp.arange(count, dtype=jnp.int32))
    doc_ends = jnp.cumsum(lax.dynamic_index_in_dim(doc_lengths, x, 0, keepdims=False))
    starts = jnp.max(
        jnp.where(doc_ends[:, None] <= positions[None, :], doc_ends[:, None], 0), axis=0
    )[None, :]
    tables = turn_tables(positions)
    mark(starts, tables)
    ring_in.receive()
    ring_in.send()
    own_cot = mark(pair_rows(*gate(mine_cot, got_cot)))
    ring_in.receive()
    ring_in.send()

    got_a = gate(got_a)
    part_a = got_a[:, :, : 3 * width]
    small = got_a[:, :, 3 * width : 3 * width + per].astype(F32)
    mark(part_a, small)
    pair_a = across_pair(part_a)
    gain, shift, out_bias, down_bias = [small[:, i].reshape(1, D) for i in range(4)]
    member = rank // 2
    qkv_bias = small[:, 4:7].reshape(3, pairs, width)
    qkv_bias = lax.dynamic_index_in_dim(qkv_bias, member, 1, keepdims=False).reshape(1, 3 * width)
    up_bias = small[:, 7:11].reshape(pairs, 2 * per_ff)
    up_bias = lax.dynamic_index_in_dim(up_bias, member, 0)

    def join(mine, got):
        low, high = jnp.where(x == 0, mine, got), jnp.where(x == 0, got, mine)
        return jnp.stack([low, high], axis=1)

    ring_in.receive()
    ring_in.send()
    mine_d, pair_d = gate(mine_d, pair_d)
    low_d, high_d = jnp.where(x == 0, mine_d, pair_d), jnp.where(x == 0, pair_d, mine_d)
    down_w = mark(
        jnp.concatenate([low_d[:per], high_d[:per], low_d[per:], high_d[per:]], axis=0)
    )
    ring_in.receive()
    send_b = gate(send_b)
    got_b = lax.all_to_all(send_b, AXES, 0, 0, tiled=True)
    qkv_w = mark(join(*gate(part_a, pair_a)).reshape(D, 3 * width))
    ring_cot = Gather(line, own_cot, place, core)
    ring_cot.send()
    normed, query, key, value = mark(
        *over_arrivals(
            project,
            "project",
            ring_in.arrived,
            core,
            [(gate(gain), ""), (shift, ""), (qkv_w, ""), (qkv_bias, ""), (tables, "tables")],
            [((count, D), BF, "rows")] + [((count, width), BF, "rows")] * 3,
        )
    )
    blocks = count // BLOCK
    split = blocks * 5 // 8
    ring_cot.receive()
    ring_cot.send()
    kept = mark(*attention_forward(gate(query), key, value, starts, 0, split, ()))
    got_b = mark(gate(got_b))
    pair_b = across_pair(got_b)
    ring_cot.receive()
    ring_cot.send()
    out_full, attended, logs = mark(
        *attention_forward(gate(query), key, value, starts, split, blocks, kept)
    )
    ring_cot.receive()
    ring_cot.send()
    up_w = mark(join(*gate(got_b, pair_b)).reshape(D, 2 * per_ff))
    ring_cot.receive()
    mixed, slope, *forward_part = mark(
        *over_tokens(
            feed,
            "feed",
            [(gate(normed), "rows"), (attended, "rows"), (up_w, ""), (up_bias, ""), (down_w, "")],
            [((count, 2 * per_ff + width), BF, "rows"), ((count, 2 * per_ff), F32, "rows")]
            + [((count // 2, D), BF, "half")] * 2,
            core,
        )
    )
    forward = Scatter(line, *forward_part, place)
    grad_att, grad_hidden, all_cot, up_sums = mark(
        *over_arrivals(
            feed_back,
            "feed_back",
            ring_cot.arrived,
            core,
            [(gate(down_w), ""), (slope, "rows")],
            [
                ((count, width), BF, "rows"),
                ((count, 2 * per_ff), BF, "rows"),
                ((count, D), BF, "rows"),
                ((1, 2 * per_ff), F32, ""),
            ],
        )
    )
    forward.start()

    def split_pair(field, axis):
        mine = lax.dynamic_index_in_dim(field, x, axis, keepdims=False)
        other = lax.dynamic_index_in_dim(field, 1 - x, axis, keepdims=False).astype(BF)
        return mine, other

    grad_up_w = mark(dot_of(normed, gate(grad_hidden), 0, 0).astype(BF))
    mine_b, other_b = mark(*split_pair(grad_up_w.reshape(H, 2, half, 2 * per_ff), 1))
    other_b = across_pair(other_b)
    forward.step()
    back_in = (query, key, value, grad_att, out_full, logs, tables, starts)
    kept = mark(*attention_backward(gate(query), *back_in[1:], split, blocks, ()))
    forward.step()
    mine_b, other_b = gate(mine_b, other_b)
    send_b = mark((mine_b.astype(F32) + other_b.astype(F32)).astype(BF))
    got_b = lax.all_to_all(send_b, AXES, 0, 0, tiled=True)
    grad_qkv = mark(attention_backward(gate(query), *back_in[1:], 0, split, kept)[0])
    forward.step()
    norm_sums, *back_part = mark(
        *over_tokens(
            project_back,
            "project_back",
            [(gate(grad_qkv), "rows"), (grad_hidden, "rows"), (qkv_w, ""), (up_w, ""), (normed, "rows"), (gain, ""), (shift, "")],
            [((2, D), F32, "")] + [((count // 2, D), BF, "half")] * 2,
            core,
        )
    )
    backward = Scatter(line, *back_part, place)
    backward.start()
    grad_qkv = fence(grad_qkv, *line.last)
    grad_qkv_w = mark(dot_of(normed, grad_qkv, 0, 0).astype(BF))
    mine_a, other_a = mark(*split_pair(grad_qkv_w.reshape(H, 2, half, 3 * width), 1))
    other_a = across_pair(other_a)
    got_b = mark(gate(got_b))
    backward.step()
    cot_sum = jnp.sum(own_cot.astype(F32), axis=0)
    qkv_sums = jnp.sum(gate(grad_qkv).astype(F32), axis=0).reshape(3, 1, width)
    qkv_all = lax.dynamic_update_slice(jnp.zeros((3, pairs, width), F32), qkv_sums, (0, member, 0))
    up_all = lax.dynamic_update_slice(jnp.zeros((pairs, 2 * per_ff), F32), up_sums, (member, 0))
    sums = jnp.concatenate(
        [
            norm_sums.reshape(2, H, per).transpose(1, 0, 2),
            cot_sum.reshape(H, 1, per),
            qkv_all.reshape(H, 3, per),
            up_all.reshape(H, 4, per),
        ],
        axis=1,
    )
    sums = mark(jnp.pad(sums, ((0, 0), (0, half - sums.shape[1]), (0, width - per))).astype(BF))
    mine_a, other_a = gate(mine_a, other_a)
    sum_a = (mine_a.astype(F32) + other_a.astype(F32)).astype(BF)
    send_a = mark(jnp.concatenate([sum_a, sums], axis=2))
    got_a = lax.all_to_all(send_a, AXES, 0, 0, tiled=True)
    forward_sum = forward.step()
    output = mark((own_in.astype(F32) + (forward_sum + (out_bias + down_bias))).astype(BF))
    output = split_rows(output)
    grad_down = mark(dot_of(fence(mixed, *line.last), all_cot, 0, 0))
    mine_o, other_o = split_pair(grad_down[: 2 * per].reshape(2, per, D), 0)
    mine_d, other_d = split_pair(grad_down[2 * per :].reshape(2, per_ff, D), 0)
    mark(other_o, other_d)
    other_o, other_d = across_pair(other_o), across_pair(other_d)
    backward.step()
    got_a = mark(gate(got_a))
    backward.step()
    back_sum = backward.step()
    normal, scale = normalize(own_in.astype(F32))
    scaled = back_sum * gain
    grad_in = scale * (
        scaled
        - jnp.mean(scaled, axis=-1, keepdims=True)
        - normal * jnp.mean(scaled * normal, axis=-1, keepdims=True)
    )
    grad_input = mark((own_cot.astype(F32) + grad_in).astype(BF))
    grad_input = split_rows(grad_input)
    output = mark(join_rows(*gate(*output)))
    mine_o, other_o, mine_d, other_d = gate(mine_o, other_o, mine_d, other_d)
    grad_out_rows = mine_o + other_o.astype(F32)
    grad_down_rows = mine_d + other_d.astype(F32)
    mark(grad_out_rows, grad_down_rows)
    grad_up_rows = mark(unpack(gate(got_b), (1, 2 * per_ff)))
    grad_input = mark(join_rows(*gate(*grad_input)))
    grad_qkv_rows = unpack(got_a, (3, width))
    sums = jnp.sum(got_a[:, :10, 3 * width : 3 * width + per].astype(F32), axis=0)
    return (
        output,
        grad_input,
        sums[0],
        sums[1],
        grad_qkv_rows,
        sums[3:6].reshape(-1),
        grad_out_rows,
        sums[2],
        grad_up_rows,
        sums[6:10].reshape(-1),
        grad_down_rows,
        sums[2],
    )


def solution(mesh):
    return jax.shard_map(
        paired_step if suits(mesh) else gathered_step,
        mesh=mesh,
        in_specs=(
            P(None, ("seq", "head"), None),
            P(),
            P(("seq", "head")),
            P(("seq", "head")),
            P(("seq", "head"), None),
            P(("seq", "head")),
            P(("seq", "head"), None),
            P(("seq", "head")),
            P(("seq", "head"), None),
            P(("seq", "head")),
            P(("seq", "head"), None),
            P(("seq", "head")),
            P(None, ("seq", "head"), None),
        ),
        out_specs=(
            P(None, ("seq", "head"), None),
            P(None, ("seq", "head"), None),
            P(("seq", "head")),
            P(("seq", "head")),
            P(("seq", "head"), None),
            P(("seq", "head")),
            P(("seq", "head"), None),
            P(("seq", "head")),
            P(("seq", "head"), None),
            P(("seq", "head")),
            P(("seq", "head"), None),
            P(("seq", "head")),
        ),
        check_vma=False,
    )
```

```python
from functools import partial

import jax
import jax.numpy as jnp
from jax import lax
from jax.experimental import pallas as pl
from jax.experimental.pallas import tpu as pltpu
from jax.sharding import PartitionSpec as P

D = 2048
H = 32
HD = 64
ROT = 32


NEG_FILL = -1e30


def from_behind(block, axis, distance):
    devices = range(lax.axis_size(axis))
    route = [(i - distance, i) for i in devices if i - distance in devices]
    return lax.ppermute(block, axis, route)


def from_behind_2(shard, axis, by):
    length = lax.axis_size(axis)
    return lax.ppermute(shard, axis, [(i, (i + by) % length) for i in range(length)])


def rotate(field, cosine, sine):
    half_rot = ROT // 2
    first_part = field[..., :half_rot]
    second_part = field[..., half_rot:ROT]
    return jnp.concatenate(
        [
            first_part * cosine - second_part * sine,
            second_part * cosine + first_part * sine,
            field[..., ROT:],
        ],
        axis=-1,
    )


def rotation_tables(positions):
    half_rot = ROT // 2
    inverse = jnp.power(10000.0, -2.0 * jnp.arange(half_rot, dtype=jnp.float32) / ROT)
    angles = positions.astype(jnp.float32)[:, None] * inverse[None, :]
    return (jnp.cos(angles)[:, None, :], jnp.sin(angles)[:, None, :])


def layer_norm(values, gain_value, shift_value):
    center = values - jnp.mean(values, axis=-1, keepdims=True)
    spread = jnp.mean(center * center, axis=-1, keepdims=True)
    return center * lax.rsqrt(spread + 1e-05) * gain_value + shift_value


def segment_ids(doc_ends, positions):
    return jnp.sum((doc_ends[:, None, :] <= positions[None, :, None]).astype(jnp.int32), axis=2)


def gelu_tanh(values):
    return jax.nn.gelu(values, approximate=True)


def allowed_pairs(query_pos, query_seg, key_pos, key_seg):
    return (key_pos[None, :] <= query_pos[:, None]) & (key_seg[None, :] == query_seg[:, None])


def masked_scores(query_seq, key_seq, allowed):
    raw_scores = (
        jnp.einsum("qhd,khd->hqk", query_seq, key_seq, preferred_element_type=jnp.float32) * 0.125
    )
    return jnp.where(allowed[None], raw_scores, NEG_FILL)


def forward_step(members, query_pos, key_pos):
    top_val, total_val, accum_val, query_seq, kv_seq, query_seg, key_seg = members
    kv_split = kv_seq.reshape(kv_seq.shape[0], 2, -1, HD)
    allowed = allowed_pairs(query_pos, query_seg, key_pos, key_seg)
    masked = masked_scores(query_seq, kv_split[:, 0], allowed)
    new_top = jnp.maximum(top_val, jnp.max(masked, axis=2))
    weights = jnp.where(allowed[None], jnp.exp(masked - new_top[:, :, None]), 0.0)
    factor = jnp.exp(top_val - new_top)
    new_total = total_val * factor + jnp.sum(weights, axis=2)
    new_accum = accum_val * factor[:, :, None] + jnp.einsum(
        "hqk,khd->hqd",
        weights.astype(jnp.bfloat16),
        kv_split[:, 1],
        preferred_element_type=jnp.float32,
    )
    return (new_top, new_total, new_accum)


def backward_step(members, query_pos, key_pos):
    grad_query, grad_kv, query_seq, kv_seq, grad_att, log_total, row_dot, query_seg, key_seg = (
        members
    )
    key_total = kv_seq.shape[0]
    kv_split = kv_seq.reshape(key_total, 2, -1, HD)
    allowed = allowed_pairs(query_pos, query_seg, key_pos, key_seg)
    masked = masked_scores(query_seq, kv_split[:, 0], allowed)
    prob_full = jnp.where(allowed[None], jnp.exp(masked - log_total[:, :, None]), 0.0)
    grad_value = jnp.einsum(
        "hqk,qhd->khd", prob_full.astype(jnp.bfloat16), grad_att, preferred_element_type=jnp.float32
    )
    grad_probs = jnp.einsum(
        "qhd,khd->hqk", grad_att, kv_split[:, 1], preferred_element_type=jnp.float32
    )
    grad_scores = (prob_full * (grad_probs - row_dot[:, :, None])).astype(jnp.bfloat16)
    grad_query = (
        grad_query
        + jnp.einsum(
            "hqk,khd->hqd", grad_scores, kv_split[:, 0], preferred_element_type=jnp.float32
        )
        * 0.125
    )
    grad_key = (
        jnp.einsum("hqk,qhd->khd", grad_scores, query_seq, preferred_element_type=jnp.float32)
        * 0.125
    )
    grad_kv = grad_kv + jnp.stack([grad_key, grad_value], axis=1).reshape(key_total, 2, -1)
    return (grad_query, grad_kv)


def gathered_step(
    inputs,
    doc_lengths,
    ln_gain,
    ln_bias,
    w_qkv,
    b_qkv,
    w_out,
    b_out,
    w_fc1,
    b_fc1,
    w_fc2,
    b_fc2,
    cotangent,
):
    seq_total = inputs.shape[0]
    row_count = inputs.shape[1]
    head_count = lax.axis_size("head")
    seq_devices = lax.axis_size("seq")
    heads_here = H // head_count
    group_width = heads_here * HD
    block_rows = row_count * head_count
    seq_rank = lax.axis_index("seq")
    head_rank = lax.axis_index("head")
    doc_ends = jnp.cumsum(doc_lengths, axis=1)
    token_pos = (seq_rank * head_count + head_rank) * row_count + jnp.arange(
        row_count, dtype=jnp.int32
    )
    query_start = seq_rank * block_rows
    query_pos = query_start + jnp.arange(block_rows, dtype=jnp.int32)
    query_seg = segment_ids(doc_ends, query_pos)
    gathered = (
        lax.all_gather(ln_gain.astype(jnp.bfloat16), ("seq", "head"), axis=0, tiled=True),
        lax.all_gather(ln_bias.astype(jnp.bfloat16), ("seq", "head"), axis=0, tiled=True),
        lax.all_gather(w_qkv.astype(jnp.bfloat16), ("seq", "head"), axis=0, tiled=True),
        lax.all_gather(b_qkv.astype(jnp.bfloat16), ("seq", "head"), axis=0, tiled=True),
        lax.all_gather(w_out.astype(jnp.bfloat16), ("seq", "head"), axis=0, tiled=True),
        lax.all_gather(b_out.astype(jnp.bfloat16), ("seq", "head"), axis=0, tiled=True),
        lax.all_gather(w_fc1.astype(jnp.bfloat16), ("seq", "head"), axis=0, tiled=True),
        lax.all_gather(b_fc1.astype(jnp.bfloat16), ("seq", "head"), axis=0, tiled=True),
        lax.all_gather(w_fc2.astype(jnp.bfloat16), ("seq", "head"), axis=0, tiled=True),
        lax.all_gather(b_fc2.astype(jnp.bfloat16), ("seq", "head"), axis=0, tiled=True),
    )
    (
        gain_full,
        shift_full,
        qkv_weight,
        qkv_bias,
        out_weight,
        out_bias,
        up_weight,
        up_bias,
        down_weight,
        down_bias,
    ) = gathered
    flat_in = inputs.reshape(seq_total * row_count, D).astype(jnp.float32)
    normed, norm_back = jax.vjp(
        layer_norm, flat_in, gain_full.astype(jnp.float32), shift_full.astype(jnp.float32)
    )
    normed_low = normed.astype(jnp.bfloat16)
    qkv_all = (
        jnp.dot(normed_low, qkv_weight, preferred_element_type=jnp.float32)
        + qkv_bias.astype(jnp.float32)
    ).reshape(seq_total, row_count, 3, H, HD)
    cosine, sine = rotation_tables(token_pos)

    def turn_field(field):
        return rotate(field, cosine, sine)

    query_rot, turn_back = jax.vjp(turn_field, qkv_all[:, :, 0])
    key_rot = turn_field(qkv_all[:, :, 1])
    stacked = (
        jnp.stack([query_rot, key_rot, qkv_all[:, :, 2]], axis=2)
        .reshape(seq_total, row_count, 3, D)
        .astype(jnp.bfloat16)
    )
    by_heads = lax.all_to_all(stacked, "head", split_axis=3, concat_axis=1, tiled=True)
    query_heads = by_heads[:, :, 0].reshape(seq_total, block_rows, heads_here, HD)
    kv_heads = by_heads[:, :, 1:3]
    start_state = (
        jnp.full((seq_total, heads_here, block_rows), NEG_FILL, jnp.float32),
        jnp.zeros((seq_total, heads_here, block_rows), jnp.float32),
        jnp.zeros((seq_total, heads_here, block_rows, HD), jnp.float32),
    )
    shard_piece = lax.all_gather(kv_heads, "seq", axis=1, tiled=True)

    def one_turn(turn_index, current):
        kv_block = lax.dynamic_slice_in_dim(shard_piece, turn_index * block_rows, block_rows, 1)
        key_start = turn_index * block_rows
        key_pos = key_start + jnp.arange(block_rows, dtype=jnp.int32)
        key_seg = segment_ids(doc_ends, key_pos)

        def one_compute(state_in):
            return lax.map(
                partial(forward_step, query_pos=query_pos, key_pos=key_pos),
                (state_in[0], state_in[1], state_in[2], query_heads, kv_block, query_seg, key_seg),
            )

        return lax.cond(
            key_start < query_start + block_rows, one_compute, lambda state_in: state_in, current
        )

    top_all, total_all, accum_all = lax.fori_loop(
        0, shard_piece.shape[1] // block_rows, one_turn, start_state
    )
    attn_full = accum_all / total_all[:, :, :, None]
    log_total = top_all + jnp.log(total_all)
    attn_low = (
        jnp.transpose(attn_full, (0, 2, 1, 3))
        .reshape(seq_total, block_rows, group_width)
        .astype(jnp.bfloat16)
    )
    attended = lax.all_to_all(attn_low, "head", split_axis=1, concat_axis=2, tiled=True).reshape(
        seq_total * row_count, D
    )
    branch = jnp.dot(attended, out_weight, preferred_element_type=jnp.float32) + out_bias.astype(
        jnp.float32
    )
    hidden = jnp.dot(normed_low, up_weight, preferred_element_type=jnp.float32) + up_bias.astype(
        jnp.float32
    )
    active, gelu_back = jax.vjp(gelu_tanh, hidden)
    active_low = active.astype(jnp.bfloat16)
    feed = jnp.dot(active_low, down_weight, preferred_element_type=jnp.float32) + down_bias.astype(
        jnp.float32
    )
    output = (flat_in + branch + feed).astype(jnp.bfloat16).reshape(inputs.shape)
    qkv_weight, out_weight, up_weight, down_weight = (
        lax.all_gather(w_qkv.astype(jnp.bfloat16), ("seq", "head"), axis=0, tiled=True),
        lax.all_gather(w_out.astype(jnp.bfloat16), ("seq", "head"), axis=0, tiled=True),
        lax.all_gather(w_fc1.astype(jnp.bfloat16), ("seq", "head"), axis=0, tiled=True),
        lax.all_gather(w_fc2.astype(jnp.bfloat16), ("seq", "head"), axis=0, tiled=True),
    )
    grad_low = cotangent.reshape(seq_total * row_count, D)
    grad_full = grad_low.astype(jnp.float32)
    cot_sum = jnp.sum(grad_full, axis=0)
    grad_down_w = jnp.einsum("nf,nd->fd", active_low, grad_low, preferred_element_type=jnp.float32)
    grad_active = jnp.einsum("nd,fd->nf", grad_low, down_weight, preferred_element_type=jnp.float32)
    grad_hidden_low = gelu_back(grad_active)[0].astype(jnp.bfloat16)
    grad_up_w = jnp.einsum(
        "nm,nf->mf", normed_low, grad_hidden_low, preferred_element_type=jnp.float32
    )
    grad_up_b = jnp.sum(grad_hidden_low.astype(jnp.float32), axis=0)
    grad_normed = jnp.einsum(
        "nf,mf->nm", grad_hidden_low, up_weight, preferred_element_type=jnp.float32
    )
    grad_out_w = jnp.einsum("nm,nd->md", attended, grad_low, preferred_element_type=jnp.float32)
    grad_att_low = jnp.einsum(
        "nd,md->nm", grad_low, out_weight, preferred_element_type=jnp.float32
    ).astype(jnp.bfloat16)
    grad_heads = lax.all_to_all(
        grad_att_low.reshape(seq_total, row_count, D),
        "head",
        split_axis=2,
        concat_axis=1,
        tiled=True,
    ).reshape(seq_total, block_rows, heads_here, HD)
    row_dot = jnp.sum(
        jnp.transpose(grad_heads.astype(jnp.float32), (0, 2, 1, 3)) * attn_full, axis=3
    )

    def back_turn(turn_index, current):
        grad_query, grad_kv, kv_now = current
        source = (seq_rank - turn_index) % seq_devices
        key_pos = source * block_rows + jnp.arange(block_rows, dtype=jnp.int32)
        key_seg = segment_ids(doc_ends, key_pos)

        def back_compute(grads_in):
            return lax.map(
                partial(backward_step, query_pos=query_pos, key_pos=key_pos),
                (
                    grads_in[0],
                    grads_in[1],
                    query_heads,
                    kv_now,
                    grad_heads,
                    log_total,
                    row_dot,
                    query_seg,
                    key_seg,
                ),
            )

        return lax.cond(
            source <= seq_rank, back_compute, lambda grads_in: grads_in, (grad_query, grad_kv)
        )

    def pass_keys(kv_now):
        return from_behind(kv_now, "seq", 1)

    def pass_grads(grad_kv):
        return from_behind_2(grad_kv.astype(jnp.bfloat16), "seq", 1).astype(grad_kv.dtype)

    def loop_turn(turn_index, current):
        grad_query, grad_kv = back_turn(turn_index, current)
        return (grad_query, pass_grads(grad_kv), pass_keys(current[2]))

    start_grads = (
        jnp.zeros((seq_total, heads_here, block_rows, HD), jnp.float32),
        jnp.zeros((seq_total, block_rows, 2, group_width), jnp.float32),
        kv_heads,
    )
    loop_state = lax.fori_loop(0, seq_devices - 1, loop_turn, start_grads)
    grad_query, grad_kv = back_turn(seq_devices - 1, loop_state)
    grad_kv = pass_grads(grad_kv)
    back_heads = jnp.concatenate(
        [
            jnp.transpose(grad_query, (0, 2, 1, 3)).reshape(seq_total, block_rows, 1, group_width),
            grad_kv,
        ],
        axis=2,
    ).astype(jnp.bfloat16)
    back_tokens = (
        lax.all_to_all(back_heads, "head", split_axis=1, concat_axis=3, tiled=True)
        .astype(jnp.float32)
        .reshape(seq_total, row_count, 3, H, HD)
    )
    grad_qkv_low = (
        jnp.stack(
            [
                turn_back(back_tokens[:, :, 0])[0],
                turn_back(back_tokens[:, :, 1])[0],
                back_tokens[:, :, 2],
            ],
            axis=2,
        )
        .reshape(seq_total * row_count, 3 * D)
        .astype(jnp.bfloat16)
    )
    grad_qkv_w = jnp.einsum(
        "nm,nk->mk", normed_low, grad_qkv_low, preferred_element_type=jnp.float32
    )
    grad_qkv_b = jnp.sum(grad_qkv_low.astype(jnp.float32), axis=0)
    grad_normed = grad_normed + jnp.einsum(
        "nk,mk->nm", grad_qkv_low, qkv_weight, preferred_element_type=jnp.float32
    )
    grad_in, grad_gain, grad_shift = norm_back(grad_normed)
    grad_input = (grad_full + grad_in).astype(jnp.bfloat16).reshape(inputs.shape)
    sums_all = (
        lax.psum_scatter(grad_gain, ("seq", "head"), scatter_dimension=0, tiled=True),
        lax.psum_scatter(grad_shift, ("seq", "head"), scatter_dimension=0, tiled=True),
        lax.psum_scatter(grad_qkv_w, ("seq", "head"), scatter_dimension=0, tiled=True),
        lax.psum_scatter(grad_qkv_b, ("seq", "head"), scatter_dimension=0, tiled=True),
        lax.psum_scatter(grad_out_w, ("seq", "head"), scatter_dimension=0, tiled=True),
        lax.psum_scatter(cot_sum, ("seq", "head"), scatter_dimension=0, tiled=True),
        lax.psum_scatter(grad_up_w, ("seq", "head"), scatter_dimension=0, tiled=True),
        lax.psum_scatter(grad_up_b, ("seq", "head"), scatter_dimension=0, tiled=True),
        lax.psum_scatter(grad_down_w, ("seq", "head"), scatter_dimension=0, tiled=True),
    )
    return (
        output,
        grad_input,
        sums_all[0],
        sums_all[1],
        sums_all[2],
        sums_all[3],
        sums_all[4],
        sums_all[5],
        sums_all[6],
        sums_all[7],
        sums_all[8],
        sums_all[5],
    )


BF = jnp.bfloat16
F32 = jnp.float32
AXES = ("seq", "head")
FF = 8192
BLOCK = 256
KEYS = 512


QUICK = pl.CostEstimate(flops=1 << 20, bytes_accessed=1 << 16, transcendentals=0)


def suits(mesh):
    return mesh.shape["seq"] * mesh.shape["head"] == H and mesh.shape["head"] == 4


def coordinates(rank):
    return rank // 8, (rank // 4) % 2, (rank // 2) % 2, rank % 2


def rank_of(z, core, y, x):
    return ((z * 2 + core) * 2 + y) * 2 + x


def route(step):
    return [(rank, rank_of(*step(*coordinates(rank)))) for rank in range(H)]


def ring_place(z, y, length):
    return z if y == 0 else length - 1 - z


def ring_point(place, length):
    place = place % length
    return (place, 0) if place < length // 2 else (length - 1 - place, 1)


def ring_route(by):
    length = H // 4

    def step(z, core, y, x):
        new_z, new_y = ring_point(ring_place(z, y, length) + by, length)
        return new_z, core, new_y, x

    return route(step)


def across_pair(value):
    return lax.ppermute(value, AXES, route(lambda z, core, y, x: (z, core, y, 1 - x)))


def across_cores(value):
    return lax.ppermute(value, AXES, route(lambda z, core, y, x: (z, 1 - core, y, x)))


def up_ring(value):
    return lax.ppermute(value, AXES, ring_route(1))


def down_ring(value):
    return lax.ppermute(value, AXES, ring_route(-1))


def block_index(place, core):
    length = H // 4
    place = place % length
    z = jnp.where(place < length // 2, place, length - 1 - place)
    y = (place >= length // 2).astype(jnp.int32)
    return (z * 2 + core) * 2 + y


def fence(value, *others):
    anywhere = pl.BlockSpec(memory_space=pl.ANY)
    return pl.pallas_call(
        lambda *refs: None,
        in_specs=[anywhere] * (1 + len(others)),
        out_specs=anywhere,
        out_shape=jax.ShapeDtypeStruct(value.shape, value.dtype),
        input_output_aliases={0: 0},
        cost_estimate=QUICK,
        name="fence",
    )(value, *others)


class Line:
    def __init__(self):
        self.last = ()

    def gate(self, *values):
        values = lax.optimization_barrier((values, self.last))[0] if self.last else values
        return values if len(values) > 1 else values[0]

    def mark(self, *values):
        self.last = values
        return values if len(values) > 1 else values[0]


class Gather:
    def __init__(self, line, own, place, core):
        self.line, self.place, self.core = line, place, core
        self.flying = (own, own)
        self.arrived, self.hop = [], 0
        self.land([(0, own)])

    def land(self, chunks):
        self.arrived += [(self.place + offset, chunk, across_cores(chunk)) for offset, chunk in chunks]
        self.hop = self.hop + 1

    def send(self):
        up, down = self.line.gate(*self.flying)
        if self.hop == H // 8:
            half = up.shape[0] // 2
            up, down = up[:half], down[half:]
        self.flying = up_ring(up), down_ring(down)

    def receive(self):
        hop = self.hop
        before = [other for _, _, other in self.arrived[-2:]]
        up, down, *before = self.line.mark(*self.line.gate(*self.flying, *before))
        for i, other in enumerate(before, len(self.arrived) - len(before)):
            self.arrived[i] = (*self.arrived[i][:2], other)
        if hop == H // 8:
            self.land([(hop, self.line.mark(jnp.concatenate([up, down], axis=0)))])
        else:
            self.flying = up, down
            self.land([(-hop, up), (hop, down)])


class Scatter:
    def __init__(self, line, own, other, place):
        length = H // 4
        self.line, self.place = line, place
        self.rows = own.shape[0] // length
        self.own = own.reshape(length, self.rows, D)
        self.got = across_cores(other).reshape(length, self.rows, D)
        self.hop = length // 2

    def term(self, offset):
        length = H // 4
        at = (self.place + offset) % length
        index = jnp.where(at < length // 2, 2 * at, 2 * (length - 1 - at) + 1)
        mine = lax.dynamic_index_in_dim(self.own, index, 0, keepdims=False)
        theirs = lax.dynamic_index_in_dim(self.got, index, 0, keepdims=False)
        return mine.astype(F32) + theirs.astype(F32)

    def start(self):
        self.got = self.line.gate(self.got)
        far = self.line.mark(self.term(self.hop).astype(BF))
        half = self.rows // 2
        self.flying = up_ring(far[:half]), down_ring(far[half:])

    def step(self):
        up, down = (part.astype(F32) for part in self.line.gate(*self.flying))
        if self.hop == H // 8:
            pad = jnp.zeros((self.rows // 2, D), F32)
            up, down = jnp.concatenate([up, pad], axis=0), jnp.concatenate([pad, down], axis=0)
        self.hop -= 1
        if not self.hop:
            return self.term(0) + up + down
        up = (up + self.term(self.hop)).astype(BF)
        down = (down + self.term(-self.hop)).astype(BF)
        self.line.mark(up, down)
        self.flying = up_ring(up), down_ring(down)


class Scatter:
    def __init__(self, line, own, other, place):
        length = H // 4
        self.line, self.place = line, place
        self.rows = own.shape[0] // length
        self.own = own.reshape(length, self.rows, D)
        self.got = across_cores(other).reshape(length, self.rows, D)
        self.hop = length // 2

    def term(self, offset):
        length = H // 4
        at = (self.place + offset) % length
        index = jnp.where(at < length // 2, 2 * at, 2 * (length - 1 - at) + 1)
        mine = lax.dynamic_index_in_dim(self.own, index, 0, keepdims=False)
        theirs = lax.dynamic_index_in_dim(self.got, index, 0, keepdims=False)
        return mine.astype(F32) + theirs.astype(F32)

    def start(self):
        self.got = self.line.gate(self.got)
        far = self.line.mark(self.term(self.hop).astype(BF))
        half = self.rows // 2
        self.flying = up_ring(far[:half]), down_ring(far[half:])

    def step(self):
        up, down = (part.astype(F32) for part in self.line.gate(*self.flying))
        if self.hop == H // 8:
            pad = jnp.zeros((self.rows // 2, D), F32)
            up, down = jnp.concatenate([up, pad], axis=0), jnp.concatenate([pad, down], axis=0)
        self.hop -= 1
        if not self.hop:
            return self.term(0) + up + down
        up = (up + self.term(self.hop)).astype(BF)
        down = (down + self.term(-self.hop)).astype(BF)
        self.line.mark(up, down)
        self.flying = up_ring(up), down_ring(down)


def settle(wholes, kept, chunks, vectors):
    rows, width = chunks[0][1].shape
    many, layers = len(chunks), 2 if vectors else 1

    def kernel(index_ref, *refs):
        blocks, rest = refs[:many], refs[many + (layers if kept else 0) :]
        outs = rest[len(vectors) : len(vectors) + layers]
        hold = rest[-1] if vectors else outs[0]
        for i, block in enumerate(blocks):

            @pl.when(pl.program_id(0) == i)
            def _(block=block):
                hold[...] = block[...]

        if vectors:
            values = hold[...].astype(F32)
            center = values - jnp.mean(values, axis=1, keepdims=True)
            scale = lax.rsqrt(jnp.mean(center * center, axis=1, keepdims=True) + 1e-05)
            normal = center * scale
            outs[0][...] = (normal * rest[0][...] + rest[1][...]).astype(BF)
            outs[1][...] = normal.astype(BF)

    whole = jax.ShapeDtypeStruct((wholes, width), BF)
    fixed = pl.BlockSpec((rows, width), lambda i, index: (0, 0))
    return pl.pallas_call(
        kernel,
        grid_spec=pltpu.PrefetchScalarGridSpec(
            num_scalar_prefetch=1,
            grid=(many,),
            in_specs=[fixed] * many
            + [pl.BlockSpec(memory_space=pl.ANY)] * (layers if kept else 0)
            + [pl.BlockSpec((1, width), lambda i, index: (0, 0))] * len(vectors),
            out_specs=[pl.BlockSpec((rows, width), lambda i, index: (index[i], 0))] * layers,
            scratch_shapes=[pltpu.VMEM((rows, width), BF)] if vectors else [],
        ),
        out_shape=[whole] * layers,
        input_output_aliases={1 + many + i: i for i in range(layers)} if kept else {},
        cost_estimate=QUICK,
        name="settle",
    )(jnp.stack([index for index, _ in chunks]), *[c for _, c in chunks], *(kept or ()), *vectors)


def turn(field, tables, sign):
    half_rot = ROT // 2
    first = pltpu.roll(field, 2 * HD - half_rot, 1)
    second = pltpu.roll(field, half_rot, 1)
    return field * tables[0] + sign * (second * tables[2] - first * tables[1])


def turn_tables(positions):
    half_rot = ROT // 2
    lane = jnp.arange(2 * HD, dtype=jnp.int32) % HD
    inverse = jnp.power(10000.0, -2.0 * (lane % half_rot).astype(F32) / ROT)
    angles = positions.astype(F32)[:, None] * inverse[None, :]
    sine = jnp.sin(angles)
    return jnp.stack(
        [
            jnp.where(lane < ROT, jnp.cos(angles), 1.0),
            jnp.where(lane < half_rot, sine, 0.0),
            jnp.where((lane >= half_rot) & (lane < ROT), sine, 0.0),
        ]
    )


def head_lanes(value, head):
    lane = lax.broadcasted_iota(jnp.int32, value.shape, 1)
    return jnp.where((lane >= HD) if head else (lane < HD), value, jnp.zeros_like(value))


def dot_of(left, right, left_dim, right_dim):
    return lax.dot_general(
        left, right, (((left_dim,), (right_dim,)), ((), ())), preferred_element_type=F32
    )


def project(values, gain_ref, shift_ref, w_ref, bias_ref, tables_ref, normed_ref, q_ref, k_ref, v_ref):
    values = values.astype(F32)
    center = values - jnp.mean(values, axis=1, keepdims=True)
    scale = lax.rsqrt(jnp.mean(center * center, axis=1, keepdims=True) + 1e-05)
    normed = (center * scale * gain_ref[...] + shift_ref[...]).astype(BF)
    normed_ref[...] = normed.reshape(normed_ref.shape)
    width = 2 * HD
    raw = dot_of(normed, w_ref[...], 1, 0) + bias_ref[...]
    tables = tables_ref[...].reshape(3, BLOCK, width)
    q_ref[...] = turn(raw[:, :width], tables, 1.0).astype(BF).reshape(q_ref.shape)
    k_ref[...] = turn(raw[:, width : 2 * width], tables, 1.0).astype(BF).reshape(k_ref.shape)
    v_ref[...] = raw[:, 2 * width :].astype(BF).reshape(v_ref.shape)


def feed(core_ref, normed_ref, att_ref, up_ref, bias_ref, down_ref, mixed_ref, slope_ref, *part_refs):
    root, cubic = 0.7978845608028654, 0.044715
    for side, part_ref in enumerate(part_refs):
        here = pl.ds(pl.multiple_of(BLOCK * ((core_ref[0] + side) % 2), BLOCK), BLOCK)
        hidden = dot_of(normed_ref[here, :], up_ref[...], 1, 0) + bias_ref[...]
        square = hidden * hidden
        bend = jnp.tanh(root * (hidden + cubic * (square * hidden)))
        active = (0.5 * hidden * (1.0 + bend)).astype(BF)
        mixed_ref[here, : 2 * HD] = att_ref[here, :]
        mixed_ref[here, 2 * HD :] = active
        slope_ref[here, :] = 0.5 * (1.0 + bend) + 0.5 * hidden * (1.0 - bend * bend) * (
            root * (1.0 + 3.0 * cubic * square)
        )
        part = dot_of(att_ref[here, :], down_ref[: 2 * HD, :], 1, 0)
        part = part + dot_of(active, down_ref[2 * HD :, :], 1, 0)
        part_ref[...] = part.astype(BF)


def feed_back(cot, down_ref, slope_ref, att_ref, hidden_ref, whole_ref, sum_ref):
    whole_ref[...] = cot.reshape(whole_ref.shape)
    mixed = dot_of(cot, down_ref[...], 1, 1)
    att_ref[...] = mixed[:, : 2 * HD].astype(BF).reshape(att_ref.shape)
    slope = slope_ref[...].reshape(BLOCK, slope_ref.shape[-1])
    hidden = (mixed[:, 2 * HD :] * slope).astype(BF)
    hidden_ref[...] = hidden.reshape(hidden_ref.shape)

    @pl.when(pl.program_id(0) == 0)
    def _():
        sum_ref[...] = jnp.zeros_like(sum_ref)

    sum_ref[...] += jnp.sum(hidden.astype(F32), axis=0, keepdims=True)


def project_back(core_ref, qkv_ref, hidden_ref, wq_ref, up_ref, normed_ref, gain_ref, shift_ref, sum_ref, *part_refs):
    @pl.when(pl.program_id(0) == 0)
    def _():
        sum_ref[...] = jnp.zeros_like(sum_ref)

    step = D // 4
    for side, part_ref in enumerate(part_refs):
        here = pl.ds(pl.multiple_of(BLOCK * ((core_ref[0] + side) % 2), BLOCK), BLOCK)
        qkv, hidden = qkv_ref[here, :], hidden_ref[here, :]
        for first in range(0, D, step):
            some = pl.ds(first, step)
            part = dot_of(qkv, wq_ref[some, :], 1, 1) + dot_of(hidden, up_ref[some, :], 1, 1)
            part_ref[:, some] = part.astype(BF)
            normal = (normed_ref[here, some].astype(F32) - shift_ref[:, some]) / gain_ref[:, some]
            sum_ref[0:1, some] += jnp.sum(part * normal, axis=0, keepdims=True)
            sum_ref[1:2, some] += jnp.sum(part, axis=0, keepdims=True)


def over_arrivals(kernel, name, arrived, core, ins, outs):
    length = H // 4
    rows, lanes = arrived[0][1].shape
    places = jnp.stack([place for place, _, _ in arrived]) % length
    y = (places >= length // 2).astype(jnp.int32)
    z = jnp.where(y == 0, places, length - 1 - places)
    lead = (length // 2, 2, 2, rows)

    def body(core_ref, z_ref, y_ref, *refs):
        blocks, rest, hold = refs[: 2 * length], refs[2 * length : -1], refs[-1]
        for step in range(length):

            @pl.when(pl.program_id(0) == step)
            def _(step=step):
                for side in range(2):
                    first = pl.multiple_of(rows * ((core_ref[0] + side) % 2), rows)
                    hold[pl.ds(first, rows), :] = blocks[2 * step + side][...]

        kernel(hold[...], *rest)

    def view(array, how):
        if how == "rows":
            return array.reshape(lead + array.shape[1:])
        return array.reshape(array.shape[:1] + lead + array.shape[2:]) if how == "tables" else array

    def spec(shape, how):
        if how == "rows":
            return pl.BlockSpec((1, 2, 1, rows, shape[-1]), lambda i, c, z, y: (z[i], 0, y[i], 0, 0))
        if how == "tables":
            return pl.BlockSpec(
                (shape[0], 1, 2, 1, rows, shape[-1]), lambda i, c, z, y: (0, z[i], 0, y[i], 0, 0)
            )
        return pl.BlockSpec(shape, lambda i, *_: (0, 0))

    once = pl.BlockSpec((rows, lanes), lambda i, *_: (0, 0), pipeline_mode=pl.Buffered(1))
    results = pl.pallas_call(
        body,
        grid_spec=pltpu.PrefetchScalarGridSpec(
            num_scalar_prefetch=3,
            grid=(length,),
            in_specs=[once] * (2 * length) + [spec(a.shape, how) for a, how in ins],
            out_specs=[spec(shape, how) for shape, _, how in outs],
            scratch_shapes=[pltpu.VMEM((2 * rows, lanes), BF)],
        ),
        out_shape=[
            jax.ShapeDtypeStruct(lead + shape[1:] if how == "rows" else shape, kind)
            for shape, kind, how in outs
        ],
        cost_estimate=QUICK,
        name=name,
    )(
        jnp.reshape(core, (1,)),
        z,
        y,
        *[block for _, mine, other in arrived for block in (mine, other)],
        *[view(a, how) for a, how in ins],
    )
    return [result.reshape(shape) for result, (shape, _, _) in zip(results, outs)]


def over_tokens(kernel, name, ins, outs, core, part=(0, 1), kept=()):
    count = ins[0][0].shape[0]
    size = 2 * BLOCK
    steps = count // size // part[1]
    first = part[0] * steps

    def spec(shape, how):
        if how in ("rows", "half"):
            rows = size if how == "rows" else size // 2
            return pl.BlockSpec((rows,) + shape[1:], lambda i, *_: (i + first, 0))
        return pl.BlockSpec(shape, lambda i, *_: (0, 0))

    def body(core_ref, *refs):
        kernel(core_ref, *refs[: len(ins)], *refs[len(ins) + len(kept) :])

    return pl.pallas_call(
        body,
        grid_spec=pltpu.PrefetchScalarGridSpec(
            num_scalar_prefetch=1,
            grid=(steps,),
            in_specs=[spec(a.shape, how) for a, how in ins]
            + [pl.BlockSpec(memory_space=pl.ANY)] * len(kept),
            out_specs=[spec(shape, how) for shape, _, how in outs],
        ),
        out_shape=[jax.ShapeDtypeStruct(shape, kind) for shape, kind, _ in outs],
        input_output_aliases={1 + len(ins) + i: i for i in range(len(kept))},
        cost_estimate=QUICK,
        name=name,
    )(jnp.reshape(core, (1,)), *[a for a, _ in ins], *kept)


def key_chunk(index):
    return pl.ds(pl.multiple_of(index * KEYS, KEYS), KEYS)


def allowed_keys(starts, chunk, block):
    keys = chunk * KEYS + lax.broadcasted_iota(jnp.int32, (KEYS, BLOCK), 0)
    queries = block * BLOCK + lax.broadcasted_iota(jnp.int32, (1, BLOCK), 1)
    return (keys >= starts) & (keys <= queries)


def fold(value, how):
    return how(value.reshape(KEYS // 8, 8, BLOCK), axis=0)


def attend_forward(first_block, kept, q_ref, k_ref, v_ref, starts_ref, *refs):
    o_ref, low_ref, lse_ref, scores_ref, acc_ref, row_ref = refs[kept:]
    block = first_block + pl.program_id(0)
    query = q_ref[...] * 0.125
    queries = [head_lanes(query, head) for head in range(2)]
    starts = starts_ref[...]
    chunks = ((block + 1) * BLOCK + KEYS - 1) // KEYS
    row_ref[...] = jnp.full_like(row_ref, NEG_FILL)

    def score(chunk, carry):
        here = key_chunk(chunk)
        keys = k_ref[here, :]
        allowed = allowed_keys(starts, chunk, block)
        for head in range(2):
            scores = jnp.where(allowed, dot_of(keys, queries[head], 1, 1), NEG_FILL)
            scores_ref[head, here, :] = scores
            row_ref[head] = jnp.maximum(row_ref[head], fold(scores, jnp.max))
        return carry

    lax.fori_loop(0, chunks, score, 0)
    tops = [jnp.max(row_ref[head], axis=0, keepdims=True) for head in range(2)]
    acc_ref[...] = jnp.zeros_like(acc_ref)
    row_ref[...] = jnp.zeros_like(row_ref)

    def mix(chunk, carry):
        here = key_chunk(chunk)
        values = v_ref[here, :]
        for head in range(2):
            weights = jnp.exp(scores_ref[head, here, :] - tops[head])
            row_ref[head] += fold(weights, jnp.sum)
            acc_ref[head] += dot_of(values, weights.astype(BF), 0, 0)
        return carry

    lax.fori_loop(0, chunks, mix, 0)
    totals = [jnp.sum(row_ref[head], axis=0, keepdims=True) for head in range(2)]
    row = lax.broadcasted_iota(jnp.int32, acc_ref.shape[1:], 0)
    out = jnp.where(row < HD, acc_ref[0] / totals[0], acc_ref[1] / totals[1]).T
    o_ref[...] = out
    low_ref[...] = out.astype(BF)
    lse_ref[...] = jnp.concatenate([tops[i] + jnp.log(totals[i]) for i in range(2)], axis=0)


def attend_backward(last_block, kept, q_ref, k_ref, v_ref, g_ref, o_ref, lse_ref, tables_ref, starts_ref, *refs):
    before, (out_ref, gk_ref, gv_ref, gq_ref) = refs[:kept], refs[kept:]
    step = pl.program_id(0)
    block = last_block - step
    width = 2 * HD

    @pl.when(step == 0)
    def _():
        gk_ref[...] = before[1][...] if kept else jnp.zeros_like(gk_ref)
        gv_ref[...] = before[2][...] if kept else jnp.zeros_like(gv_ref)

    gq_ref[...] = jnp.zeros_like(gq_ref)
    query, grad = q_ref[...] * 0.125, g_ref[...]
    product = (grad.astype(F32) * o_ref[...]).T
    dots = [jnp.sum(product[i * HD : (i + 1) * HD], axis=0, keepdims=True) for i in range(2)]
    queries = [head_lanes(query, head) for head in range(2)]
    grads = [head_lanes(grad, head) for head in range(2)]
    logs = [lse_ref[head : head + 1, :] for head in range(2)]
    starts = starts_ref[...]

    def work(chunk, carry):
        here = key_chunk(chunk)
        keys, values = k_ref[here, :], v_ref[here, :]
        allowed = allowed_keys(starts, chunk, block)
        for head in range(2):
            scores = dot_of(keys, queries[head], 1, 1)
            probs = jnp.where(allowed, jnp.exp(scores - logs[head]), 0.0)
            grad_probs = dot_of(values, grads[head], 1, 1)
            grad_scores = (probs * (grad_probs - dots[head])).astype(BF)
            gv_ref[here, :] += dot_of(probs.astype(BF), grads[head], 1, 0)
            gk_ref[here, :] += dot_of(grad_scores, queries[head], 1, 0)
            gq_ref[...] += dot_of(head_lanes(keys, head), grad_scores, 0, 0)
        return carry

    lax.fori_loop(0, ((block + 1) * BLOCK + KEYS - 1) // KEYS, work, 0)
    tables = tables_ref[...]
    here = pl.ds(pl.multiple_of(block * BLOCK, BLOCK), BLOCK)

    def back(value):
        return turn(value.astype(BF).astype(F32), tables, -1.0).astype(BF)

    out_ref[:, :width] = back(gq_ref[...].T * 0.125)
    out_ref[:, width : 2 * width] = back(gk_ref[here, :])
    out_ref[:, 2 * width :] = gv_ref[here, :].astype(BF)


def attention_forward(query, key, value, starts, first, last, kept):
    count = query.shape[0]
    width = 2 * HD
    rows = lambda i: (i + first, 0)
    block = pl.BlockSpec((BLOCK, width), rows)
    row = lambda many: pl.BlockSpec((many, BLOCK), lambda i: (0, i + first))
    full = pl.BlockSpec((count, width), lambda i: (0, 0))
    return pl.pallas_call(
        partial(attend_forward, first, len(kept)),
        grid=(last - first,),
        in_specs=[block, full, full, row(1)] + [pl.BlockSpec(memory_space=pl.ANY)] * len(kept),
        out_specs=[block] * 2 + [row(2)],
        out_shape=[
            jax.ShapeDtypeStruct((count, width), F32),
            jax.ShapeDtypeStruct((count, width), BF),
            jax.ShapeDtypeStruct((2, count), F32),
        ],
        scratch_shapes=[
            pltpu.VMEM((2, count, BLOCK), F32),
            pltpu.VMEM((2, width, BLOCK), F32),
            pltpu.VMEM((2, 8, BLOCK), F32),
        ],
        input_output_aliases={4 + i: i for i in range(len(kept))},
        cost_estimate=QUICK,
        name="attend_forward",
    )(query, key, value, starts, *kept)


def attention_backward(query, key, value, grad, out, logs, tables, starts, first, last, kept):
    count = query.shape[0]
    width = 2 * HD
    rows = lambda i: (last - 1 - i, 0)
    block = pl.BlockSpec((BLOCK, width), rows)
    full = pl.BlockSpec((count, width), lambda i: (0, 0))
    row = lambda many: pl.BlockSpec((many, BLOCK), lambda i: (0, last - 1 - i))
    return pl.pallas_call(
        partial(attend_backward, last - 1, len(kept)),
        grid=(last - first,),
        in_specs=[
            block,
            full,
            full,
            block,
            block,
            row(2),
            pl.BlockSpec((3, BLOCK, width), lambda i: (0, last - 1 - i, 0)),
            row(1),
        ]
        + [pl.BlockSpec(memory_space=pl.ANY), full, full][: len(kept)],
        out_specs=[pl.BlockSpec((BLOCK, 3 * width), rows), full, full],
        out_shape=[
            jax.ShapeDtypeStruct((count, 3 * width), BF),
            jax.ShapeDtypeStruct((count, width), F32),
            jax.ShapeDtypeStruct((count, width), F32),
        ],
        scratch_shapes=[pltpu.VMEM((width, BLOCK), F32)],
        input_output_aliases={8: 0} if kept else {},
        cost_estimate=QUICK,
        name="attend_backward",
    )(query, key, value, grad, out, logs, tables, starts, *kept)


def unpack(rows, parts):
    many, half, _ = rows.shape
    columns = parts[1]

    def kernel(rows_ref, out_ref):
        for pair in range(many // 2):
            for part in range(parts[0]):
                lanes = slice(part * columns, (part + 1) * columns)
                first = (part * (many // 2) + pair) * columns
                for side in range(2):
                    out_ref[side * half : (side + 1) * half, first : first + columns] = rows_ref[
                        2 * pair + side, :, lanes
                    ].astype(F32)

    return pl.pallas_call(
        kernel,
        out_shape=jax.ShapeDtypeStruct((2 * half, parts[0] * columns * many // 2), F32),
        cost_estimate=QUICK,
        name="unpack",
    )(rows)


def normalize(values):
    center = values - jnp.mean(values, axis=-1, keepdims=True)
    scale = lax.rsqrt(jnp.mean(center * center, axis=-1, keepdims=True) + 1e-05)
    return center * scale, scale


def paired_step(
    inputs,
    doc_lengths,
    ln_gain,
    ln_bias,
    w_qkv,
    b_qkv,
    w_out,
    b_out,
    w_fc1,
    b_fc1,
    w_fc2,
    b_fc2,
    cotangent,
):
    rows = inputs.shape[1]
    count = rows * H
    rank = lax.axis_index("seq") * 4 + lax.axis_index("head")
    x = rank % 2
    y, core, z = (rank // 2) % 2, (rank // 4) % 2, rank // 8
    length = H // 4
    place = jnp.where(y == 0, z, length - 1 - z)

    def split_rows(field):
        mine = lax.dynamic_slice_in_dim(field, x * rows, rows, 0)
        return mine, across_pair(lax.dynamic_slice_in_dim(field, (1 - x) * rows, rows, 0))

    def join_rows(mine, got):
        return jnp.where(x == 0, jnp.stack([mine, got]), jnp.stack([got, mine]))

    per = D // H
    per_ff = FF // H
    pairs = H // 2
    width = 2 * HD
    half = per // 2

    line = Line()
    gate, mark = line.gate, line.mark

    def pair_blocks(field):
        mine = lax.dynamic_index_in_dim(field, x, 0, keepdims=False)
        return mine, lax.dynamic_index_in_dim(field, 1 - x, 0, keepdims=False)

    def pair_rows(mine, got):
        return jnp.where(x == 0, jnp.concatenate([mine, got]), jnp.concatenate([got, mine]))

    mine_in, other_in = mark(*pair_blocks(inputs))
    got_in = across_pair(other_in)
    small = jnp.concatenate([ln_gain, ln_bias, b_out, b_fc2, b_qkv, b_fc1]).astype(BF).reshape(-1, per)
    small = jnp.pad(small, ((0, half - small.shape[0]), (0, width - per)))
    send_a = jnp.concatenate(
        [
            gate(w_qkv).astype(BF).reshape(2, half, 3, pairs, width).transpose(3, 0, 1, 2, 4).reshape(H, half, 3 * width),
            jnp.broadcast_to(small[None], (H, half, width)),
        ],
        axis=2,
    )
    own_in = mark(pair_rows(mine_in, got_in))
    send_a = mark(gate(send_a))
    got_a = lax.all_to_all(send_a, AXES, 0, 0, tiled=True)
    mine_cot, other_cot = pair_blocks(gate(cotangent))
    mine_d = jnp.concatenate([gate(w_out), w_fc2], axis=0).astype(BF)
    mark(other_cot, mine_d)
    got_cot = across_pair(other_cot)
    pair_d = across_pair(mine_d)
    send_b = mark(
        gate(w_fc1)
        .astype(BF)
        .reshape(2, half, pairs, 2 * per_ff)
        .transpose(2, 0, 1, 3)
        .reshape(H, half, 2 * per_ff)
    )
    positions = gate(jnp.arange(count, dtype=jnp.int32))
    doc_ends = jnp.cumsum(lax.dynamic_index_in_dim(doc_lengths, x, 0, keepdims=False))
    starts = jnp.max(
        jnp.where(doc_ends[:, None] <= positions[None, :], doc_ends[:, None], 0), axis=0
    )[None, :]
    starts, tables = mark(*lax.optimization_barrier((starts, turn_tables(positions))))
    ring_in = Gather(line, gate(own_in), place, core)
    ring_in.send()
    ring_in.receive()
    ring_in.send()
    mine_d, pair_d = gate(mine_d, pair_d)
    low_d, high_d = jnp.where(x == 0, mine_d, pair_d), jnp.where(x == 0, pair_d, mine_d)
    down_w = mark(
        jnp.concatenate([low_d[:per], high_d[:per], low_d[per:], high_d[per:]], axis=0)
    )
    got_a = gate(got_a)
    part_a = got_a[:, :, : 3 * width]
    small = got_a[:, :, 3 * width : 3 * width + per].astype(F32)
    gain, shift, out_bias, down_bias = [small[:, i].reshape(1, D) for i in range(4)]
    member = rank // 2
    qkv_bias = small[:, 4:7].reshape(3, pairs, width)
    qkv_bias = lax.dynamic_index_in_dim(qkv_bias, member, 1, keepdims=False).reshape(1, 3 * width)
    up_bias = small[:, 7:11].reshape(pairs, 2 * per_ff)
    up_bias = lax.dynamic_index_in_dim(up_bias, member, 0)
    small = (gain, shift, qkv_bias, up_bias, out_bias, down_bias)
    part_a, *small = mark(*lax.optimization_barrier((part_a, *small)))
    gain, shift, qkv_bias, up_bias, out_bias, down_bias = small
    pair_a = across_pair(part_a)

    def join(mine, got):
        low, high = jnp.where(x == 0, mine, got), jnp.where(x == 0, got, mine)
        return jnp.stack([low, high], axis=1)

    own_cot = mark(pair_rows(*gate(mine_cot, got_cot)))
    ring_in.receive()
    ring_in.send()
    ring_in.receive()
    qkv_w = mark(join(*gate(part_a, pair_a)).reshape(D, 3 * width))
    ring_in.send()
    ring_in.receive()
    send_b = gate(send_b)
    got_b = lax.all_to_all(send_b, AXES, 0, 0, tiled=True)
    normed, query, key, value = mark(
        *over_arrivals(
            project,
            "project",
            ring_in.arrived,
            core,
            [(gate(gain), ""), (shift, ""), (qkv_w, ""), (qkv_bias, ""), (tables, "tables")],
            [((count, D), BF, "rows")] + [((count, width), BF, "rows")] * 3,
        )
    )
    blocks = count // BLOCK
    split = blocks * 5 // 8
    got_b = mark(gate(got_b))
    pair_b = across_pair(got_b)
    ring_cot = Gather(line, gate(own_cot), place, core)
    ring_cot.send()
    kept = mark(*attention_forward(gate(query), key, value, starts, 0, split, ()))
    out_full, attended, logs = mark(
        *attention_forward(gate(query), key, value, starts, split, blocks, kept)
    )
    ring_cot.receive()
    ring_cot.send()
    up_w = mark(join(*gate(got_b, pair_b)).reshape(D, 2 * per_ff))

    def fed(part, kept):
        return mark(
            *over_tokens(
                feed,
                "feed",
                [(gate(normed), "rows"), (attended, "rows"), (up_w, ""), (up_bias, ""), (down_w, "")],
                [((count, 2 * per_ff + width), BF, "rows"), ((count, 2 * per_ff), F32, "rows")]
                + [((count // 2, D), BF, "half")] * 2,
                core,
                part,
                kept,
            )
        )

    kept = fed((0, 2), ())
    ring_cot.receive()
    ring_cot.send()
    mixed, slope, own_part, other_part = fed((1, 2), kept)
    ring_cot.receive()
    ring_cot.send()
    forward = Scatter(line, own_part, gate(other_part), place)
    ring_cot.receive()
    forward.start()
    grad_att, grad_hidden, all_cot, up_sums = mark(
        *over_arrivals(
            feed_back,
            "feed_back",
            ring_cot.arrived,
            core,
            [(gate(down_w), ""), (slope, "rows")],
            [
                ((count, width), BF, "rows"),
                ((count, 2 * per_ff), BF, "rows"),
                ((count, D), BF, "rows"),
                ((1, 2 * per_ff), F32, ""),
            ],
        )
    )

    def split_pair(field, axis):
        mine = lax.dynamic_index_in_dim(field, x, axis, keepdims=False)
        other = lax.dynamic_index_in_dim(field, 1 - x, axis, keepdims=False).astype(BF)
        return mine, other

    forward.step()
    grad_hidden = fence(grad_hidden, *line.last)
    grad_up_w = mark(dot_of(normed, grad_hidden, 0, 0).astype(BF))
    mine_b, other_b = mark(*split_pair(grad_up_w.reshape(H, 2, half, 2 * per_ff), 1))
    other_b = across_pair(other_b)
    back_in = (query, key, value, grad_att, out_full, logs, tables, starts)
    kept = mark(*attention_backward(gate(query), *back_in[1:], split, blocks, ()))
    forward.step()
    grad_qkv = mark(attention_backward(gate(query), *back_in[1:], 0, split, kept)[0])
    forward.step()
    mine_b, other_b = gate(mine_b, other_b)
    send_b = mark((mine_b.astype(F32) + other_b.astype(F32)).astype(BF))
    got_b = lax.all_to_all(send_b, AXES, 0, 0, tiled=True)
    norm_sums, *back_part = mark(
        *over_tokens(
            project_back,
            "project_back",
            [(gate(grad_qkv), "rows"), (grad_hidden, "rows"), (qkv_w, ""), (up_w, ""), (normed, "rows"), (gain, ""), (shift, "")],
            [((2, D), F32, "")] + [((count // 2, D), BF, "half")] * 2,
            core,
        )
    )
    backward = Scatter(line, *back_part, place)
    backward.start()
    grad_qkv = fence(grad_qkv, *line.last)
    grad_qkv_w = mark(dot_of(normed, grad_qkv, 0, 0).astype(BF))
    mine_a, other_a = mark(*split_pair(grad_qkv_w.reshape(H, 2, half, 3 * width), 1))
    other_a = across_pair(other_a)
    got_b = mark(gate(got_b))
    backward.step()
    cot_sum = jnp.sum(own_cot.astype(F32), axis=0)
    qkv_sums = jnp.sum(gate(grad_qkv).astype(F32), axis=0).reshape(3, 1, width)
    qkv_all = lax.dynamic_update_slice(jnp.zeros((3, pairs, width), F32), qkv_sums, (0, member, 0))
    up_all = lax.dynamic_update_slice(jnp.zeros((pairs, 2 * per_ff), F32), up_sums, (member, 0))
    sums = jnp.concatenate(
        [
            norm_sums.reshape(2, H, per).transpose(1, 0, 2),
            cot_sum.reshape(H, 1, per),
            qkv_all.reshape(H, 3, per),
            up_all.reshape(H, 4, per),
        ],
        axis=1,
    )
    sums = mark(jnp.pad(sums, ((0, 0), (0, half - sums.shape[1]), (0, width - per))).astype(BF))
    mine_a, other_a = gate(mine_a, other_a)
    sum_a = (mine_a.astype(F32) + other_a.astype(F32)).astype(BF)
    send_a = mark(jnp.concatenate([sum_a, sums], axis=2))
    got_a = lax.all_to_all(send_a, AXES, 0, 0, tiled=True)
    forward_sum = forward.step()
    output = mark((own_in.astype(F32) + (forward_sum + (out_bias + down_bias))).astype(BF))
    output = split_rows(output)
    grad_down = mark(dot_of(fence(mixed, *line.last), all_cot, 0, 0))
    mine_o, other_o = split_pair(grad_down[: 2 * per].reshape(2, per, D), 0)
    mine_d, other_d = split_pair(grad_down[2 * per :].reshape(2, per_ff, D), 0)
    mark(other_o, other_d)
    other_o, other_d = across_pair(other_o), across_pair(other_d)
    backward.step()
    got_a = mark(gate(got_a))
    backward.step()
    back_sum = backward.step()
    normal, scale = normalize(own_in.astype(F32))
    scaled = back_sum * gain
    grad_in = scale * (
        scaled
        - jnp.mean(scaled, axis=-1, keepdims=True)
        - normal * jnp.mean(scaled * normal, axis=-1, keepdims=True)
    )
    grad_input = mark((own_cot.astype(F32) + grad_in).astype(BF))
    grad_input = split_rows(grad_input)
    output = mark(join_rows(*gate(*output)))
    mine_o, other_o, mine_d, other_d = gate(mine_o, other_o, mine_d, other_d)
    grad_out_rows = mine_o + other_o.astype(F32)
    grad_down_rows = mine_d + other_d.astype(F32)
    mark(grad_out_rows, grad_down_rows)
    grad_up_rows = mark(unpack(gate(got_b), (1, 2 * per_ff)))
    grad_input = mark(join_rows(*gate(*grad_input)))
    grad_qkv_rows = unpack(got_a, (3, width))
    sums = jnp.sum(got_a[:, :10, 3 * width : 3 * width + per].astype(F32), axis=0)
    return (
        output,
        grad_input,
        sums[0],
        sums[1],
        grad_qkv_rows,
        sums[3:6].reshape(-1),
        grad_out_rows,
        sums[2],
        grad_up_rows,
        sums[6:10].reshape(-1),
        grad_down_rows,
        sums[2],
    )


def solution(mesh):
    return jax.shard_map(
        paired_step if suits(mesh) else gathered_step,
        mesh=mesh,
        in_specs=(
            P(None, ("seq", "head"), None),
            P(),
            P(("seq", "head")),
            P(("seq", "head")),
            P(("seq", "head"), None),
            P(("seq", "head")),
            P(("seq", "head"), None),
            P(("seq", "head")),
            P(("seq", "head"), None),
            P(("seq", "head")),
            P(("seq", "head"), None),
            P(("seq", "head")),
            P(None, ("seq", "head"), None),
        ),
        out_specs=(
            P(None, ("seq", "head"), None),
            P(None, ("seq", "head"), None),
            P(("seq", "head")),
            P(("seq", "head")),
            P(("seq", "head"), None),
            P(("seq", "head")),
            P(("seq", "head"), None),
            P(("seq", "head")),
            P(("seq", "head"), None),
            P(("seq", "head")),
            P(("seq", "head"), None),
            P(("seq", "head")),
        ),
        check_vma=False,
    )
```

```python
from functools import partial

import jax
import jax.numpy as jnp
from jax import lax
from jax.experimental import pallas as pl
from jax.experimental.pallas import tpu as pltpu
from jax.sharding import PartitionSpec as P

D = 2048
H = 32
HD = 64
ROT = 32


NEG_FILL = -1e30


def from_behind(block, axis, distance):
    devices = range(lax.axis_size(axis))
    route = [(i - distance, i) for i in devices if i - distance in devices]
    return lax.ppermute(block, axis, route)


def from_behind_2(shard, axis, by):
    length = lax.axis_size(axis)
    return lax.ppermute(shard, axis, [(i, (i + by) % length) for i in range(length)])


def rotate(field, cosine, sine):
    half_rot = ROT // 2
    first_part = field[..., :half_rot]
    second_part = field[..., half_rot:ROT]
    return jnp.concatenate(
        [
            first_part * cosine - second_part * sine,
            second_part * cosine + first_part * sine,
            field[..., ROT:],
        ],
        axis=-1,
    )


def rotation_tables(positions):
    half_rot = ROT // 2
    inverse = jnp.power(10000.0, -2.0 * jnp.arange(half_rot, dtype=jnp.float32) / ROT)
    angles = positions.astype(jnp.float32)[:, None] * inverse[None, :]
    return (jnp.cos(angles)[:, None, :], jnp.sin(angles)[:, None, :])


def layer_norm(values, gain_value, shift_value):
    center = values - jnp.mean(values, axis=-1, keepdims=True)
    spread = jnp.mean(center * center, axis=-1, keepdims=True)
    return center * lax.rsqrt(spread + 1e-05) * gain_value + shift_value


def segment_ids(doc_ends, positions):
    return jnp.sum((doc_ends[:, None, :] <= positions[None, :, None]).astype(jnp.int32), axis=2)


def gelu_tanh(values):
    return jax.nn.gelu(values, approximate=True)


def allowed_pairs(query_pos, query_seg, key_pos, key_seg):
    return (key_pos[None, :] <= query_pos[:, None]) & (key_seg[None, :] == query_seg[:, None])


def masked_scores(query_seq, key_seq, allowed):
    raw_scores = (
        jnp.einsum("qhd,khd->hqk", query_seq, key_seq, preferred_element_type=jnp.float32) * 0.125
    )
    return jnp.where(allowed[None], raw_scores, NEG_FILL)


def forward_step(members, query_pos, key_pos):
    top_val, total_val, accum_val, query_seq, kv_seq, query_seg, key_seg = members
    kv_split = kv_seq.reshape(kv_seq.shape[0], 2, -1, HD)
    allowed = allowed_pairs(query_pos, query_seg, key_pos, key_seg)
    masked = masked_scores(query_seq, kv_split[:, 0], allowed)
    new_top = jnp.maximum(top_val, jnp.max(masked, axis=2))
    weights = jnp.where(allowed[None], jnp.exp(masked - new_top[:, :, None]), 0.0)
    factor = jnp.exp(top_val - new_top)
    new_total = total_val * factor + jnp.sum(weights, axis=2)
    new_accum = accum_val * factor[:, :, None] + jnp.einsum(
        "hqk,khd->hqd",
        weights.astype(jnp.bfloat16),
        kv_split[:, 1],
        preferred_element_type=jnp.float32,
    )
    return (new_top, new_total, new_accum)


def backward_step(members, query_pos, key_pos):
    grad_query, grad_kv, query_seq, kv_seq, grad_att, log_total, row_dot, query_seg, key_seg = (
        members
    )
    key_total = kv_seq.shape[0]
    kv_split = kv_seq.reshape(key_total, 2, -1, HD)
    allowed = allowed_pairs(query_pos, query_seg, key_pos, key_seg)
    masked = masked_scores(query_seq, kv_split[:, 0], allowed)
    prob_full = jnp.where(allowed[None], jnp.exp(masked - log_total[:, :, None]), 0.0)
    grad_value = jnp.einsum(
        "hqk,qhd->khd", prob_full.astype(jnp.bfloat16), grad_att, preferred_element_type=jnp.float32
    )
    grad_probs = jnp.einsum(
        "qhd,khd->hqk", grad_att, kv_split[:, 1], preferred_element_type=jnp.float32
    )
    grad_scores = (prob_full * (grad_probs - row_dot[:, :, None])).astype(jnp.bfloat16)
    grad_query = (
        grad_query
        + jnp.einsum(
            "hqk,khd->hqd", grad_scores, kv_split[:, 0], preferred_element_type=jnp.float32
        )
        * 0.125
    )
    grad_key = (
        jnp.einsum("hqk,qhd->khd", grad_scores, query_seq, preferred_element_type=jnp.float32)
        * 0.125
    )
    grad_kv = grad_kv + jnp.stack([grad_key, grad_value], axis=1).reshape(key_total, 2, -1)
    return (grad_query, grad_kv)


def gathered_step(
    inputs,
    doc_lengths,
    ln_gain,
    ln_bias,
    w_qkv,
    b_qkv,
    w_out,
    b_out,
    w_fc1,
    b_fc1,
    w_fc2,
    b_fc2,
    cotangent,
):
    seq_total = inputs.shape[0]
    row_count = inputs.shape[1]
    head_count = lax.axis_size("head")
    seq_devices = lax.axis_size("seq")
    heads_here = H // head_count
    group_width = heads_here * HD
    block_rows = row_count * head_count
    seq_rank = lax.axis_index("seq")
    head_rank = lax.axis_index("head")
    doc_ends = jnp.cumsum(doc_lengths, axis=1)
    token_pos = (seq_rank * head_count + head_rank) * row_count + jnp.arange(
        row_count, dtype=jnp.int32
    )
    query_start = seq_rank * block_rows
    query_pos = query_start + jnp.arange(block_rows, dtype=jnp.int32)
    query_seg = segment_ids(doc_ends, query_pos)
    gathered = (
        lax.all_gather(ln_gain.astype(jnp.bfloat16), ("seq", "head"), axis=0, tiled=True),
        lax.all_gather(ln_bias.astype(jnp.bfloat16), ("seq", "head"), axis=0, tiled=True),
        lax.all_gather(w_qkv.astype(jnp.bfloat16), ("seq", "head"), axis=0, tiled=True),
        lax.all_gather(b_qkv.astype(jnp.bfloat16), ("seq", "head"), axis=0, tiled=True),
        lax.all_gather(w_out.astype(jnp.bfloat16), ("seq", "head"), axis=0, tiled=True),
        lax.all_gather(b_out.astype(jnp.bfloat16), ("seq", "head"), axis=0, tiled=True),
        lax.all_gather(w_fc1.astype(jnp.bfloat16), ("seq", "head"), axis=0, tiled=True),
        lax.all_gather(b_fc1.astype(jnp.bfloat16), ("seq", "head"), axis=0, tiled=True),
        lax.all_gather(w_fc2.astype(jnp.bfloat16), ("seq", "head"), axis=0, tiled=True),
        lax.all_gather(b_fc2.astype(jnp.bfloat16), ("seq", "head"), axis=0, tiled=True),
    )
    (
        gain_full,
        shift_full,
        qkv_weight,
        qkv_bias,
        out_weight,
        out_bias,
        up_weight,
        up_bias,
        down_weight,
        down_bias,
    ) = gathered
    flat_in = inputs.reshape(seq_total * row_count, D).astype(jnp.float32)
    normed, norm_back = jax.vjp(
        layer_norm, flat_in, gain_full.astype(jnp.float32), shift_full.astype(jnp.float32)
    )
    normed_low = normed.astype(jnp.bfloat16)
    qkv_all = (
        jnp.dot(normed_low, qkv_weight, preferred_element_type=jnp.float32)
        + qkv_bias.astype(jnp.float32)
    ).reshape(seq_total, row_count, 3, H, HD)
    cosine, sine = rotation_tables(token_pos)

    def turn_field(field):
        return rotate(field, cosine, sine)

    query_rot, turn_back = jax.vjp(turn_field, qkv_all[:, :, 0])
    key_rot = turn_field(qkv_all[:, :, 1])
    stacked = (
        jnp.stack([query_rot, key_rot, qkv_all[:, :, 2]], axis=2)
        .reshape(seq_total, row_count, 3, D)
        .astype(jnp.bfloat16)
    )
    by_heads = lax.all_to_all(stacked, "head", split_axis=3, concat_axis=1, tiled=True)
    query_heads = by_heads[:, :, 0].reshape(seq_total, block_rows, heads_here, HD)
    kv_heads = by_heads[:, :, 1:3]
    start_state = (
        jnp.full((seq_total, heads_here, block_rows), NEG_FILL, jnp.float32),
        jnp.zeros((seq_total, heads_here, block_rows), jnp.float32),
        jnp.zeros((seq_total, heads_here, block_rows, HD), jnp.float32),
    )
    shard_piece = lax.all_gather(kv_heads, "seq", axis=1, tiled=True)

    def one_turn(turn_index, current):
        kv_block = lax.dynamic_slice_in_dim(shard_piece, turn_index * block_rows, block_rows, 1)
        key_start = turn_index * block_rows
        key_pos = key_start + jnp.arange(block_rows, dtype=jnp.int32)
        key_seg = segment_ids(doc_ends, key_pos)

        def one_compute(state_in):
            return lax.map(
                partial(forward_step, query_pos=query_pos, key_pos=key_pos),
                (state_in[0], state_in[1], state_in[2], query_heads, kv_block, query_seg, key_seg),
            )

        return lax.cond(
            key_start < query_start + block_rows, one_compute, lambda state_in: state_in, current
        )

    top_all, total_all, accum_all = lax.fori_loop(
        0, shard_piece.shape[1] // block_rows, one_turn, start_state
    )
    attn_full = accum_all / total_all[:, :, :, None]
    log_total = top_all + jnp.log(total_all)
    attn_low = (
        jnp.transpose(attn_full, (0, 2, 1, 3))
        .reshape(seq_total, block_rows, group_width)
        .astype(jnp.bfloat16)
    )
    attended = lax.all_to_all(attn_low, "head", split_axis=1, concat_axis=2, tiled=True).reshape(
        seq_total * row_count, D
    )
    branch = jnp.dot(attended, out_weight, preferred_element_type=jnp.float32) + out_bias.astype(
        jnp.float32
    )
    hidden = jnp.dot(normed_low, up_weight, preferred_element_type=jnp.float32) + up_bias.astype(
        jnp.float32
    )
    active, gelu_back = jax.vjp(gelu_tanh, hidden)
    active_low = active.astype(jnp.bfloat16)
    feed = jnp.dot(active_low, down_weight, preferred_element_type=jnp.float32) + down_bias.astype(
        jnp.float32
    )
    output = (flat_in + branch + feed).astype(jnp.bfloat16).reshape(inputs.shape)
    qkv_weight, out_weight, up_weight, down_weight = (
        lax.all_gather(w_qkv.astype(jnp.bfloat16), ("seq", "head"), axis=0, tiled=True),
        lax.all_gather(w_out.astype(jnp.bfloat16), ("seq", "head"), axis=0, tiled=True),
        lax.all_gather(w_fc1.astype(jnp.bfloat16), ("seq", "head"), axis=0, tiled=True),
        lax.all_gather(w_fc2.astype(jnp.bfloat16), ("seq", "head"), axis=0, tiled=True),
    )
    grad_low = cotangent.reshape(seq_total * row_count, D)
    grad_full = grad_low.astype(jnp.float32)
    cot_sum = jnp.sum(grad_full, axis=0)
    grad_down_w = jnp.einsum("nf,nd->fd", active_low, grad_low, preferred_element_type=jnp.float32)
    grad_active = jnp.einsum("nd,fd->nf", grad_low, down_weight, preferred_element_type=jnp.float32)
    grad_hidden_low = gelu_back(grad_active)[0].astype(jnp.bfloat16)
    grad_up_w = jnp.einsum(
        "nm,nf->mf", normed_low, grad_hidden_low, preferred_element_type=jnp.float32
    )
    grad_up_b = jnp.sum(grad_hidden_low.astype(jnp.float32), axis=0)
    grad_normed = jnp.einsum(
        "nf,mf->nm", grad_hidden_low, up_weight, preferred_element_type=jnp.float32
    )
    grad_out_w = jnp.einsum("nm,nd->md", attended, grad_low, preferred_element_type=jnp.float32)
    grad_att_low = jnp.einsum(
        "nd,md->nm", grad_low, out_weight, preferred_element_type=jnp.float32
    ).astype(jnp.bfloat16)
    grad_heads = lax.all_to_all(
        grad_att_low.reshape(seq_total, row_count, D),
        "head",
        split_axis=2,
        concat_axis=1,
        tiled=True,
    ).reshape(seq_total, block_rows, heads_here, HD)
    row_dot = jnp.sum(
        jnp.transpose(grad_heads.astype(jnp.float32), (0, 2, 1, 3)) * attn_full, axis=3
    )

    def back_turn(turn_index, current):
        grad_query, grad_kv, kv_now = current
        source = (seq_rank - turn_index) % seq_devices
        key_pos = source * block_rows + jnp.arange(block_rows, dtype=jnp.int32)
        key_seg = segment_ids(doc_ends, key_pos)

        def back_compute(grads_in):
            return lax.map(
                partial(backward_step, query_pos=query_pos, key_pos=key_pos),
                (
                    grads_in[0],
                    grads_in[1],
                    query_heads,
                    kv_now,
                    grad_heads,
                    log_total,
                    row_dot,
                    query_seg,
                    key_seg,
                ),
            )

        return lax.cond(
            source <= seq_rank, back_compute, lambda grads_in: grads_in, (grad_query, grad_kv)
        )

    def pass_keys(kv_now):
        return from_behind(kv_now, "seq", 1)

    def pass_grads(grad_kv):
        return from_behind_2(grad_kv.astype(jnp.bfloat16), "seq", 1).astype(grad_kv.dtype)

    def loop_turn(turn_index, current):
        grad_query, grad_kv = back_turn(turn_index, current)
        return (grad_query, pass_grads(grad_kv), pass_keys(current[2]))

    start_grads = (
        jnp.zeros((seq_total, heads_here, block_rows, HD), jnp.float32),
        jnp.zeros((seq_total, block_rows, 2, group_width), jnp.float32),
        kv_heads,
    )
    loop_state = lax.fori_loop(0, seq_devices - 1, loop_turn, start_grads)
    grad_query, grad_kv = back_turn(seq_devices - 1, loop_state)
    grad_kv = pass_grads(grad_kv)
    back_heads = jnp.concatenate(
        [
            jnp.transpose(grad_query, (0, 2, 1, 3)).reshape(seq_total, block_rows, 1, group_width),
            grad_kv,
        ],
        axis=2,
    ).astype(jnp.bfloat16)
    back_tokens = (
        lax.all_to_all(back_heads, "head", split_axis=1, concat_axis=3, tiled=True)
        .astype(jnp.float32)
        .reshape(seq_total, row_count, 3, H, HD)
    )
    grad_qkv_low = (
        jnp.stack(
            [
                turn_back(back_tokens[:, :, 0])[0],
                turn_back(back_tokens[:, :, 1])[0],
                back_tokens[:, :, 2],
            ],
            axis=2,
        )
        .reshape(seq_total * row_count, 3 * D)
        .astype(jnp.bfloat16)
    )
    grad_qkv_w = jnp.einsum(
        "nm,nk->mk", normed_low, grad_qkv_low, preferred_element_type=jnp.float32
    )
    grad_qkv_b = jnp.sum(grad_qkv_low.astype(jnp.float32), axis=0)
    grad_normed = grad_normed + jnp.einsum(
        "nk,mk->nm", grad_qkv_low, qkv_weight, preferred_element_type=jnp.float32
    )
    grad_in, grad_gain, grad_shift = norm_back(grad_normed)
    grad_input = (grad_full + grad_in).astype(jnp.bfloat16).reshape(inputs.shape)
    sums_all = (
        lax.psum_scatter(grad_gain, ("seq", "head"), scatter_dimension=0, tiled=True),
        lax.psum_scatter(grad_shift, ("seq", "head"), scatter_dimension=0, tiled=True),
        lax.psum_scatter(grad_qkv_w, ("seq", "head"), scatter_dimension=0, tiled=True),
        lax.psum_scatter(grad_qkv_b, ("seq", "head"), scatter_dimension=0, tiled=True),
        lax.psum_scatter(grad_out_w, ("seq", "head"), scatter_dimension=0, tiled=True),
        lax.psum_scatter(cot_sum, ("seq", "head"), scatter_dimension=0, tiled=True),
        lax.psum_scatter(grad_up_w, ("seq", "head"), scatter_dimension=0, tiled=True),
        lax.psum_scatter(grad_up_b, ("seq", "head"), scatter_dimension=0, tiled=True),
        lax.psum_scatter(grad_down_w, ("seq", "head"), scatter_dimension=0, tiled=True),
    )
    return (
        output,
        grad_input,
        sums_all[0],
        sums_all[1],
        sums_all[2],
        sums_all[3],
        sums_all[4],
        sums_all[5],
        sums_all[6],
        sums_all[7],
        sums_all[8],
        sums_all[5],
    )


BF = jnp.bfloat16
F32 = jnp.float32
AXES = ("seq", "head")
FF = 8192
BLOCK = 256
KEYS = 512


QUICK = pl.CostEstimate(flops=1 << 20, bytes_accessed=1 << 16, transcendentals=0)


def suits(mesh):
    return mesh.shape["seq"] * mesh.shape["head"] == H and mesh.shape["head"] == 4


def coordinates(rank):
    return rank // 8, (rank // 4) % 2, (rank // 2) % 2, rank % 2


def rank_of(z, core, y, x):
    return ((z * 2 + core) * 2 + y) * 2 + x


def route(step):
    return [(rank, rank_of(*step(*coordinates(rank)))) for rank in range(H)]


def ring_place(z, y, length):
    return z if y == 0 else length - 1 - z


def ring_point(place, length):
    place = place % length
    return (place, 0) if place < length // 2 else (length - 1 - place, 1)


def ring_route(by):
    length = H // 4

    def step(z, core, y, x):
        new_z, new_y = ring_point(ring_place(z, y, length) + by, length)
        return new_z, core, new_y, x

    return route(step)


def across_pair(value):
    return lax.ppermute(value, AXES, route(lambda z, core, y, x: (z, core, y, 1 - x)))


def across_cores(value):
    return lax.ppermute(value, AXES, route(lambda z, core, y, x: (z, 1 - core, y, x)))


def up_ring(value):
    return lax.ppermute(value, AXES, ring_route(1))


def down_ring(value):
    return lax.ppermute(value, AXES, ring_route(-1))


def block_index(place, core):
    length = H // 4
    place = place % length
    z = jnp.where(place < length // 2, place, length - 1 - place)
    y = (place >= length // 2).astype(jnp.int32)
    return (z * 2 + core) * 2 + y


def fence(value, *others):
    anywhere = pl.BlockSpec(memory_space=pl.ANY)
    return pl.pallas_call(
        lambda *refs: None,
        in_specs=[anywhere] * (1 + len(others)),
        out_specs=anywhere,
        out_shape=jax.ShapeDtypeStruct(value.shape, value.dtype),
        input_output_aliases={0: 0},
        cost_estimate=QUICK,
        name="fence",
    )(value, *others)


class Line:
    def __init__(self):
        self.last = ()

    def gate(self, *values):
        values = lax.optimization_barrier((values, self.last))[0] if self.last else values
        return values if len(values) > 1 else values[0]

    def mark(self, *values):
        self.last = values
        return values if len(values) > 1 else values[0]


class Gather:
    def __init__(self, line, own, place, core):
        self.line, self.place, self.core = line, place, core
        self.flying = (own, own)
        self.arrived, self.hop = [], 0
        self.land([(0, own)])

    def land(self, chunks):
        self.arrived += [(self.place + offset, chunk, across_cores(chunk)) for offset, chunk in chunks]
        self.hop = self.hop + 1

    def send(self):
        up, down = self.line.gate(*self.flying)
        if self.hop == H // 8:
            half = up.shape[0] // 2
            up, down = up[:half], down[half:]
        self.flying = up_ring(up), down_ring(down)

    def receive(self):
        hop = self.hop
        before = [other for _, _, other in self.arrived[-2:]]
        up, down, *before = self.line.mark(*self.line.gate(*self.flying, *before))
        for i, other in enumerate(before, len(self.arrived) - len(before)):
            self.arrived[i] = (*self.arrived[i][:2], other)
        if hop == H // 8:
            self.land([(hop, self.line.mark(jnp.concatenate([up, down], axis=0)))])
        else:
            self.flying = up, down
            self.land([(-hop, up), (hop, down)])


class Scatter:
    def __init__(self, line, own, other, place):
        length = H // 4
        self.line, self.place = line, place
        self.rows = own.shape[0] // length
        self.own = own.reshape(length, self.rows, D)
        self.got = across_cores(other).reshape(length, self.rows, D)
        self.hop = length // 2

    def term(self, offset):
        length = H // 4
        at = (self.place + offset) % length
        index = jnp.where(at < length // 2, 2 * at, 2 * (length - 1 - at) + 1)
        mine = lax.dynamic_index_in_dim(self.own, index, 0, keepdims=False)
        theirs = lax.dynamic_index_in_dim(self.got, index, 0, keepdims=False)
        return mine.astype(F32) + theirs.astype(F32)

    def start(self):
        self.got = self.line.gate(self.got)
        far = self.line.mark(self.term(self.hop).astype(BF))
        half = self.rows // 2
        self.flying = up_ring(far[:half]), down_ring(far[half:])

    def step(self):
        up, down = (part.astype(F32) for part in self.line.gate(*self.flying))
        if self.hop == H // 8:
            pad = jnp.zeros((self.rows // 2, D), F32)
            up, down = jnp.concatenate([up, pad], axis=0), jnp.concatenate([pad, down], axis=0)
        self.hop -= 1
        if not self.hop:
            return self.term(0) + up + down
        up = (up + self.term(self.hop)).astype(BF)
        down = (down + self.term(-self.hop)).astype(BF)
        self.line.mark(up, down)
        self.flying = up_ring(up), down_ring(down)


class Scatter:
    def __init__(self, line, own, other, place):
        length = H // 4
        self.line, self.place = line, place
        self.rows = own.shape[0] // length
        self.own = own.reshape(length, self.rows, D)
        self.got = across_cores(other).reshape(length, self.rows, D)
        self.hop = length // 2

    def term(self, offset):
        length = H // 4
        at = (self.place + offset) % length
        index = jnp.where(at < length // 2, 2 * at, 2 * (length - 1 - at) + 1)
        mine = lax.dynamic_index_in_dim(self.own, index, 0, keepdims=False)
        theirs = lax.dynamic_index_in_dim(self.got, index, 0, keepdims=False)
        return mine.astype(F32) + theirs.astype(F32)

    def start(self):
        self.got = self.line.gate(self.got)
        far = self.line.mark(self.term(self.hop).astype(BF))
        half = self.rows // 2
        self.flying = up_ring(far[:half]), down_ring(far[half:])

    def step(self):
        up, down = (part.astype(F32) for part in self.line.gate(*self.flying))
        if self.hop == H // 8:
            pad = jnp.zeros((self.rows // 2, D), F32)
            up, down = jnp.concatenate([up, pad], axis=0), jnp.concatenate([pad, down], axis=0)
        self.hop -= 1
        if not self.hop:
            return self.term(0) + up + down
        up = (up + self.term(self.hop)).astype(BF)
        down = (down + self.term(-self.hop)).astype(BF)
        self.line.mark(up, down)
        self.flying = up_ring(up), down_ring(down)


def settle(wholes, kept, chunks, vectors):
    rows, width = chunks[0][1].shape
    many, layers = len(chunks), 2 if vectors else 1

    def kernel(index_ref, *refs):
        blocks, rest = refs[:many], refs[many + (layers if kept else 0) :]
        outs = rest[len(vectors) : len(vectors) + layers]
        hold = rest[-1] if vectors else outs[0]
        for i, block in enumerate(blocks):

            @pl.when(pl.program_id(0) == i)
            def _(block=block):
                hold[...] = block[...]

        if vectors:
            values = hold[...].astype(F32)
            center = values - jnp.mean(values, axis=1, keepdims=True)
            scale = lax.rsqrt(jnp.mean(center * center, axis=1, keepdims=True) + 1e-05)
            normal = center * scale
            outs[0][...] = (normal * rest[0][...] + rest[1][...]).astype(BF)
            outs[1][...] = normal.astype(BF)

    whole = jax.ShapeDtypeStruct((wholes, width), BF)
    fixed = pl.BlockSpec((rows, width), lambda i, index: (0, 0))
    return pl.pallas_call(
        kernel,
        grid_spec=pltpu.PrefetchScalarGridSpec(
            num_scalar_prefetch=1,
            grid=(many,),
            in_specs=[fixed] * many
            + [pl.BlockSpec(memory_space=pl.ANY)] * (layers if kept else 0)
            + [pl.BlockSpec((1, width), lambda i, index: (0, 0))] * len(vectors),
            out_specs=[pl.BlockSpec((rows, width), lambda i, index: (index[i], 0))] * layers,
            scratch_shapes=[pltpu.VMEM((rows, width), BF)] if vectors else [],
        ),
        out_shape=[whole] * layers,
        input_output_aliases={1 + many + i: i for i in range(layers)} if kept else {},
        cost_estimate=QUICK,
        name="settle",
    )(jnp.stack([index for index, _ in chunks]), *[c for _, c in chunks], *(kept or ()), *vectors)


def turn(field, tables, sign):
    half_rot = ROT // 2
    first = pltpu.roll(field, 2 * HD - half_rot, 1)
    second = pltpu.roll(field, half_rot, 1)
    return field * tables[0] + sign * (second * tables[2] - first * tables[1])


def turn_tables(positions):
    half_rot = ROT // 2
    lane = jnp.arange(2 * HD, dtype=jnp.int32) % HD
    inverse = jnp.power(10000.0, -2.0 * (lane % half_rot).astype(F32) / ROT)
    angles = positions.astype(F32)[:, None] * inverse[None, :]
    sine = jnp.sin(angles)
    return jnp.stack(
        [
            jnp.where(lane < ROT, jnp.cos(angles), 1.0),
            jnp.where(lane < half_rot, sine, 0.0),
            jnp.where((lane >= half_rot) & (lane < ROT), sine, 0.0),
        ]
    )


def head_lanes(value, head):
    lane = lax.broadcasted_iota(jnp.int32, value.shape, 1)
    return jnp.where((lane >= HD) if head else (lane < HD), value, jnp.zeros_like(value))


def dot_of(left, right, left_dim, right_dim):
    return lax.dot_general(
        left, right, (((left_dim,), (right_dim,)), ((), ())), preferred_element_type=F32
    )


def project(values, gain_ref, shift_ref, w_ref, bias_ref, tables_ref, normed_ref, q_ref, k_ref, v_ref):
    values = values.astype(F32)
    center = values - jnp.mean(values, axis=1, keepdims=True)
    scale = lax.rsqrt(jnp.mean(center * center, axis=1, keepdims=True) + 1e-05)
    normed = (center * scale * gain_ref[...] + shift_ref[...]).astype(BF)
    normed_ref[...] = normed.reshape(normed_ref.shape)
    width = 2 * HD
    raw = dot_of(normed, w_ref[...], 1, 0) + bias_ref[...]
    tables = tables_ref[...].reshape(3, BLOCK, width)
    q_ref[...] = turn(raw[:, :width], tables, 1.0).astype(BF).reshape(q_ref.shape)
    k_ref[...] = turn(raw[:, width : 2 * width], tables, 1.0).astype(BF).reshape(k_ref.shape)
    v_ref[...] = raw[:, 2 * width :].astype(BF).reshape(v_ref.shape)


def feed(core_ref, normed_ref, att_ref, up_ref, bias_ref, down_ref, mixed_ref, slope_ref, *part_refs):
    root, cubic = 0.7978845608028654, 0.044715
    for side, part_ref in enumerate(part_refs):
        here = pl.ds(pl.multiple_of(BLOCK * ((core_ref[0] + side) % 2), BLOCK), BLOCK)
        hidden = dot_of(normed_ref[here, :], up_ref[...], 1, 0) + bias_ref[...]
        square = hidden * hidden
        bend = jnp.tanh(root * (hidden + cubic * (square * hidden)))
        active = (0.5 * hidden * (1.0 + bend)).astype(BF)
        mixed_ref[here, : 2 * HD] = att_ref[here, :]
        mixed_ref[here, 2 * HD :] = active
        slope_ref[here, :] = 0.5 * (1.0 + bend) + 0.5 * hidden * (1.0 - bend * bend) * (
            root * (1.0 + 3.0 * cubic * square)
        )
        part = dot_of(att_ref[here, :], down_ref[: 2 * HD, :], 1, 0)
        part = part + dot_of(active, down_ref[2 * HD :, :], 1, 0)
        part_ref[...] = part.astype(BF)


def feed_back(cot, down_ref, slope_ref, att_ref, hidden_ref, whole_ref, sum_ref):
    whole_ref[...] = cot.reshape(whole_ref.shape)
    mixed = dot_of(cot, down_ref[...], 1, 1)
    att_ref[...] = mixed[:, : 2 * HD].astype(BF).reshape(att_ref.shape)
    slope = slope_ref[...].reshape(BLOCK, slope_ref.shape[-1])
    hidden = (mixed[:, 2 * HD :] * slope).astype(BF)
    hidden_ref[...] = hidden.reshape(hidden_ref.shape)

    @pl.when(pl.program_id(0) == 0)
    def _():
        sum_ref[...] = jnp.zeros_like(sum_ref)

    sum_ref[...] += jnp.sum(hidden.astype(F32), axis=0, keepdims=True)


def project_back(core_ref, qkv_ref, hidden_ref, wq_ref, up_ref, normed_ref, gain_ref, shift_ref, sum_ref, *part_refs):
    @pl.when(pl.program_id(0) == 0)
    def _():
        sum_ref[...] = jnp.zeros_like(sum_ref)

    step = D // 4
    for side, part_ref in enumerate(part_refs):
        here = pl.ds(pl.multiple_of(BLOCK * ((core_ref[0] + side) % 2), BLOCK), BLOCK)
        qkv, hidden = qkv_ref[here, :], hidden_ref[here, :]
        for first in range(0, D, step):
            some = pl.ds(first, step)
            part = dot_of(qkv, wq_ref[some, :], 1, 1) + dot_of(hidden, up_ref[some, :], 1, 1)
            part_ref[:, some] = part.astype(BF)
            normal = (normed_ref[here, some].astype(F32) - shift_ref[:, some]) / gain_ref[:, some]
            sum_ref[0:1, some] += jnp.sum(part * normal, axis=0, keepdims=True)
            sum_ref[1:2, some] += jnp.sum(part, axis=0, keepdims=True)


def over_arrivals(kernel, name, arrived, core, ins, outs):
    length = H // 4
    rows, lanes = arrived[0][1].shape
    places = jnp.stack([place for place, _, _ in arrived]) % length
    y = (places >= length // 2).astype(jnp.int32)
    z = jnp.where(y == 0, places, length - 1 - places)
    lead = (length // 2, 2, 2, rows)

    def body(core_ref, z_ref, y_ref, *refs):
        blocks, rest, hold = refs[: 2 * length], refs[2 * length : -1], refs[-1]
        for step in range(length):

            @pl.when(pl.program_id(0) == step)
            def _(step=step):
                for side in range(2):
                    first = pl.multiple_of(rows * ((core_ref[0] + side) % 2), rows)
                    hold[pl.ds(first, rows), :] = blocks[2 * step + side][...]

        kernel(hold[...], *rest)

    def view(array, how):
        if how == "rows":
            return array.reshape(lead + array.shape[1:])
        return array.reshape(array.shape[:1] + lead + array.shape[2:]) if how == "tables" else array

    def spec(shape, how):
        if how == "rows":
            return pl.BlockSpec((1, 2, 1, rows, shape[-1]), lambda i, c, z, y: (z[i], 0, y[i], 0, 0))
        if how == "tables":
            return pl.BlockSpec(
                (shape[0], 1, 2, 1, rows, shape[-1]), lambda i, c, z, y: (0, z[i], 0, y[i], 0, 0)
            )
        return pl.BlockSpec(shape, lambda i, *_: (0, 0))

    once = pl.BlockSpec((rows, lanes), lambda i, *_: (0, 0), pipeline_mode=pl.Buffered(1))
    results = pl.pallas_call(
        body,
        grid_spec=pltpu.PrefetchScalarGridSpec(
            num_scalar_prefetch=3,
            grid=(length,),
            in_specs=[once] * (2 * length) + [spec(a.shape, how) for a, how in ins],
            out_specs=[spec(shape, how) for shape, _, how in outs],
            scratch_shapes=[pltpu.VMEM((2 * rows, lanes), BF)],
        ),
        out_shape=[
            jax.ShapeDtypeStruct(lead + shape[1:] if how == "rows" else shape, kind)
            for shape, kind, how in outs
        ],
        cost_estimate=QUICK,
        name=name,
    )(
        jnp.reshape(core, (1,)),
        z,
        y,
        *[block for _, mine, other in arrived for block in (mine, other)],
        *[view(a, how) for a, how in ins],
    )
    return [result.reshape(shape) for result, (shape, _, _) in zip(results, outs)]


def over_tokens(kernel, name, ins, outs, core, part=(0, 1), kept=()):
    count = ins[0][0].shape[0]
    size = 2 * BLOCK
    steps = count // size // part[1]
    first = part[0] * steps

    def spec(shape, how):
        if how in ("rows", "half"):
            rows = size if how == "rows" else size // 2
            return pl.BlockSpec((rows,) + shape[1:], lambda i, *_: (i + first, 0))
        return pl.BlockSpec(shape, lambda i, *_: (0, 0))

    def body(core_ref, *refs):
        kernel(core_ref, *refs[: len(ins)], *refs[len(ins) + len(kept) :])

    return pl.pallas_call(
        body,
        grid_spec=pltpu.PrefetchScalarGridSpec(
            num_scalar_prefetch=1,
            grid=(steps,),
            in_specs=[spec(a.shape, how) for a, how in ins]
            + [pl.BlockSpec(memory_space=pl.ANY)] * len(kept),
            out_specs=[spec(shape, how) for shape, _, how in outs],
        ),
        out_shape=[jax.ShapeDtypeStruct(shape, kind) for shape, kind, _ in outs],
        input_output_aliases={1 + len(ins) + i: i for i in range(len(kept))},
        cost_estimate=QUICK,
        name=name,
    )(jnp.reshape(core, (1,)), *[a for a, _ in ins], *kept)


def key_chunk(index):
    return pl.ds(pl.multiple_of(index * KEYS, KEYS), KEYS)


def allowed_keys(starts, chunk, block):
    keys = chunk * KEYS + lax.broadcasted_iota(jnp.int32, (KEYS, BLOCK), 0)
    queries = block * BLOCK + lax.broadcasted_iota(jnp.int32, (1, BLOCK), 1)
    return (keys >= starts) & (keys <= queries)


def fold(value, how):
    return how(value.reshape(KEYS // 8, 8, BLOCK), axis=0)


def attend_forward(first_block, kept, q_ref, k_ref, v_ref, starts_ref, *refs):
    o_ref, low_ref, lse_ref, scores_ref, acc_ref, row_ref = refs[kept:]
    block = first_block + pl.program_id(0)
    query = q_ref[...] * 0.125
    queries = [head_lanes(query, head) for head in range(2)]
    starts = starts_ref[...]
    chunks = ((block + 1) * BLOCK + KEYS - 1) // KEYS
    row_ref[...] = jnp.full_like(row_ref, NEG_FILL)

    def score(chunk, carry):
        here = key_chunk(chunk)
        keys = k_ref[here, :]
        allowed = allowed_keys(starts, chunk, block)
        for head in range(2):
            scores = jnp.where(allowed, dot_of(keys, queries[head], 1, 1), NEG_FILL)
            scores_ref[head, here, :] = scores
            row_ref[head] = jnp.maximum(row_ref[head], fold(scores, jnp.max))
        return carry

    lax.fori_loop(0, chunks, score, 0)
    tops = [jnp.max(row_ref[head], axis=0, keepdims=True) for head in range(2)]
    acc_ref[...] = jnp.zeros_like(acc_ref)
    row_ref[...] = jnp.zeros_like(row_ref)

    def mix(chunk, carry):
        here = key_chunk(chunk)
        values = v_ref[here, :]
        for head in range(2):
            weights = jnp.exp(scores_ref[head, here, :] - tops[head])
            row_ref[head] += fold(weights, jnp.sum)
            acc_ref[head] += dot_of(values, weights.astype(BF), 0, 0)
        return carry

    lax.fori_loop(0, chunks, mix, 0)
    totals = [jnp.sum(row_ref[head], axis=0, keepdims=True) for head in range(2)]
    row = lax.broadcasted_iota(jnp.int32, acc_ref.shape[1:], 0)
    out = jnp.where(row < HD, acc_ref[0] / totals[0], acc_ref[1] / totals[1]).T
    o_ref[...] = out
    low_ref[...] = out.astype(BF)
    lse_ref[...] = jnp.concatenate([tops[i] + jnp.log(totals[i]) for i in range(2)], axis=0)


def attend_backward(last_block, kept, q_ref, k_ref, v_ref, g_ref, o_ref, lse_ref, tables_ref, starts_ref, *refs):
    before, (out_ref, gk_ref, gv_ref, gq_ref) = refs[:kept], refs[kept:]
    step = pl.program_id(0)
    block = last_block - step
    width = 2 * HD

    @pl.when(step == 0)
    def _():
        gk_ref[...] = before[1][...] if kept else jnp.zeros_like(gk_ref)
        gv_ref[...] = before[2][...] if kept else jnp.zeros_like(gv_ref)

    gq_ref[...] = jnp.zeros_like(gq_ref)
    query, grad = q_ref[...] * 0.125, g_ref[...]
    product = (grad.astype(F32) * o_ref[...]).T
    dots = [jnp.sum(product[i * HD : (i + 1) * HD], axis=0, keepdims=True) for i in range(2)]
    queries = [head_lanes(query, head) for head in range(2)]
    grads = [head_lanes(grad, head) for head in range(2)]
    logs = [lse_ref[head : head + 1, :] for head in range(2)]
    starts = starts_ref[...]

    def work(chunk, carry):
        here = key_chunk(chunk)
        keys, values = k_ref[here, :], v_ref[here, :]
        allowed = allowed_keys(starts, chunk, block)
        for head in range(2):
            scores = dot_of(keys, queries[head], 1, 1)
            probs = jnp.where(allowed, jnp.exp(scores - logs[head]), 0.0)
            grad_probs = dot_of(values, grads[head], 1, 1)
            grad_scores = (probs * (grad_probs - dots[head])).astype(BF)
            gv_ref[here, :] += dot_of(probs.astype(BF), grads[head], 1, 0)
            gk_ref[here, :] += dot_of(grad_scores, queries[head], 1, 0)
            gq_ref[...] += dot_of(head_lanes(keys, head), grad_scores, 0, 0)
        return carry

    lax.fori_loop(0, ((block + 1) * BLOCK + KEYS - 1) // KEYS, work, 0)
    tables = tables_ref[...]
    here = pl.ds(pl.multiple_of(block * BLOCK, BLOCK), BLOCK)

    def back(value):
        return turn(value.astype(BF).astype(F32), tables, -1.0).astype(BF)

    out_ref[:, :width] = back(gq_ref[...].T * 0.125)
    out_ref[:, width : 2 * width] = back(gk_ref[here, :])
    out_ref[:, 2 * width :] = gv_ref[here, :].astype(BF)


def attention_forward(query, key, value, starts, first, last, kept):
    count = query.shape[0]
    width = 2 * HD
    rows = lambda i: (i + first, 0)
    block = pl.BlockSpec((BLOCK, width), rows)
    row = lambda many: pl.BlockSpec((many, BLOCK), lambda i: (0, i + first))
    full = pl.BlockSpec((count, width), lambda i: (0, 0))
    return pl.pallas_call(
        partial(attend_forward, first, len(kept)),
        grid=(last - first,),
        in_specs=[block, full, full, row(1)] + [pl.BlockSpec(memory_space=pl.ANY)] * len(kept),
        out_specs=[block] * 2 + [row(2)],
        out_shape=[
            jax.ShapeDtypeStruct((count, width), F32),
            jax.ShapeDtypeStruct((count, width), BF),
            jax.ShapeDtypeStruct((2, count), F32),
        ],
        scratch_shapes=[
            pltpu.VMEM((2, count, BLOCK), F32),
            pltpu.VMEM((2, width, BLOCK), F32),
            pltpu.VMEM((2, 8, BLOCK), F32),
        ],
        input_output_aliases={4 + i: i for i in range(len(kept))},
        cost_estimate=QUICK,
        name="attend_forward",
    )(query, key, value, starts, *kept)


def attention_backward(query, key, value, grad, out, logs, tables, starts, first, last, kept):
    count = query.shape[0]
    width = 2 * HD
    rows = lambda i: (last - 1 - i, 0)
    block = pl.BlockSpec((BLOCK, width), rows)
    full = pl.BlockSpec((count, width), lambda i: (0, 0))
    row = lambda many: pl.BlockSpec((many, BLOCK), lambda i: (0, last - 1 - i))
    return pl.pallas_call(
        partial(attend_backward, last - 1, len(kept)),
        grid=(last - first,),
        in_specs=[
            block,
            full,
            full,
            block,
            block,
            row(2),
            pl.BlockSpec((3, BLOCK, width), lambda i: (0, last - 1 - i, 0)),
            row(1),
        ]
        + [pl.BlockSpec(memory_space=pl.ANY), full, full][: len(kept)],
        out_specs=[pl.BlockSpec((BLOCK, 3 * width), rows), full, full],
        out_shape=[
            jax.ShapeDtypeStruct((count, 3 * width), BF),
            jax.ShapeDtypeStruct((count, width), F32),
            jax.ShapeDtypeStruct((count, width), F32),
        ],
        scratch_shapes=[pltpu.VMEM((width, BLOCK), F32)],
        input_output_aliases={8: 0} if kept else {},
        cost_estimate=QUICK,
        name="attend_backward",
    )(query, key, value, grad, out, logs, tables, starts, *kept)


def unpack(rows, half, parts, columns):
    many = rows.shape[0]

    def kernel(rows_ref, out_ref):
        for device in range(many):
            side = slice((device % 2) * half, (device % 2 + 1) * half)
            for part in range(parts):
                first = (part * (many // 2) + device // 2) * columns
                out_ref[side, first : first + columns] = rows_ref[
                    device, part * half : (part + 1) * half, :
                ].astype(F32)

    return pl.pallas_call(
        kernel,
        out_shape=jax.ShapeDtypeStruct((2 * half, parts * columns * many // 2), F32),
        cost_estimate=QUICK,
        name="unpack",
    )(rows)


def normalize(values):
    center = values - jnp.mean(values, axis=-1, keepdims=True)
    scale = lax.rsqrt(jnp.mean(center * center, axis=-1, keepdims=True) + 1e-05)
    return center * scale, scale


def paired_step(
    inputs,
    doc_lengths,
    ln_gain,
    ln_bias,
    w_qkv,
    b_qkv,
    w_out,
    b_out,
    w_fc1,
    b_fc1,
    w_fc2,
    b_fc2,
    cotangent,
):
    rows = inputs.shape[1]
    count = rows * H
    rank = lax.axis_index("seq") * 4 + lax.axis_index("head")
    x = rank % 2
    y, core, z = (rank // 2) % 2, (rank // 4) % 2, rank // 8
    length = H // 4
    place = jnp.where(y == 0, z, length - 1 - z)

    def split_rows(field):
        mine = lax.dynamic_slice_in_dim(field, x * rows, rows, 0)
        return mine, across_pair(lax.dynamic_slice_in_dim(field, (1 - x) * rows, rows, 0))

    def join_rows(mine, got):
        return jnp.where(x == 0, jnp.stack([mine, got]), jnp.stack([got, mine]))

    per = D // H
    per_ff = FF // H
    pairs = H // 2
    width = 2 * HD
    half = per // 2

    line = Line()
    gate, mark = line.gate, line.mark

    def pair_blocks(field):
        mine = lax.dynamic_index_in_dim(field, x, 0, keepdims=False)
        return mine, lax.dynamic_index_in_dim(field, 1 - x, 0, keepdims=False)

    def pair_rows(mine, got):
        return jnp.where(x == 0, jnp.concatenate([mine, got]), jnp.concatenate([got, mine]))

    mine_in, other_in = mark(*pair_blocks(inputs))
    got_in = across_pair(other_in)
    small = jnp.concatenate([ln_gain, ln_bias, b_out, b_fc2, b_qkv, b_fc1]).astype(BF).reshape(-1, per)
    small = jnp.pad(small, ((0, half // 2 - small.shape[0]), (0, width - per)))
    send_a = jnp.concatenate(
        [
            gate(w_qkv).astype(BF).reshape(2, half, 3, pairs, width).transpose(3, 0, 2, 1, 4).reshape(H, 3 * half, width),
            jnp.broadcast_to(small[None], (H, half // 2, width)),
        ],
        axis=1,
    )
    own_in = mark(pair_rows(mine_in, got_in))
    send_a = mark(gate(send_a))
    got_a = lax.all_to_all(send_a, AXES, 0, 0, tiled=True)
    mine_cot, other_cot = pair_blocks(gate(cotangent))
    mine_d = jnp.concatenate([gate(w_out), w_fc2], axis=0).astype(BF)
    mark(other_cot, mine_d)
    got_cot = across_pair(other_cot)
    pair_d = across_pair(mine_d)
    send_b = mark(
        gate(w_fc1)
        .astype(BF)
        .reshape(2, half, pairs, 2 * per_ff)
        .transpose(2, 0, 1, 3)
        .reshape(H, half, 2 * per_ff)
    )
    positions = gate(jnp.arange(count, dtype=jnp.int32))
    doc_ends = jnp.cumsum(lax.dynamic_index_in_dim(doc_lengths, x, 0, keepdims=False))
    starts = jnp.max(
        jnp.where(doc_ends[:, None] <= positions[None, :], doc_ends[:, None], 0), axis=0
    )[None, :]
    starts, tables = mark(*lax.optimization_barrier((starts, turn_tables(positions))))
    ring_in = Gather(line, gate(own_in), place, core)
    ring_in.send()
    ring_in.receive()
    ring_in.send()
    mine_d, pair_d = gate(mine_d, pair_d)
    low_d, high_d = jnp.where(x == 0, mine_d, pair_d), jnp.where(x == 0, pair_d, mine_d)
    down_w = mark(
        jnp.concatenate([low_d[:per], high_d[:per], low_d[per:], high_d[per:]], axis=0)
    )
    got_a = gate(got_a)
    part_a = got_a[:, : 3 * half]
    small = got_a[:, 3 * half :, :per].astype(F32)
    gain, shift, out_bias, down_bias = [small[:, i].reshape(1, D) for i in range(4)]
    member = rank // 2
    qkv_bias = small[:, 4:7].reshape(3, pairs, width)
    qkv_bias = lax.dynamic_index_in_dim(qkv_bias, member, 1, keepdims=False).reshape(1, 3 * width)
    up_bias = small[:, 7:11].reshape(pairs, 2 * per_ff)
    up_bias = lax.dynamic_index_in_dim(up_bias, member, 0)
    small = (gain, shift, qkv_bias, up_bias, out_bias, down_bias)
    part_a, *small = mark(*lax.optimization_barrier((part_a, *small)))
    gain, shift, qkv_bias, up_bias, out_bias, down_bias = small
    pair_a = across_pair(part_a)

    def join(mine, got):
        low, high = jnp.where(x == 0, mine, got), jnp.where(x == 0, got, mine)
        return jnp.stack([low, high], axis=1)

    own_cot = mark(pair_rows(*gate(mine_cot, got_cot)))
    ring_in.receive()
    ring_in.send()
    ring_in.receive()
    qkv_w = join(*gate(part_a, pair_a)).reshape(H, 2, 3, half, width)
    qkv_w = mark(qkv_w.transpose(0, 1, 3, 2, 4).reshape(D, 3 * width))
    ring_in.send()
    ring_in.receive()
    send_b = gate(send_b)
    got_b = lax.all_to_all(send_b, AXES, 0, 0, tiled=True)
    normed, query, key, value = mark(
        *over_arrivals(
            project,
            "project",
            ring_in.arrived,
            core,
            [(gate(gain), ""), (shift, ""), (qkv_w, ""), (qkv_bias, ""), (tables, "tables")],
            [((count, D), BF, "rows")] + [((count, width), BF, "rows")] * 3,
        )
    )
    blocks = count // BLOCK
    split = blocks * 5 // 8
    got_b = mark(gate(got_b))
    pair_b = across_pair(got_b)
    ring_cot = Gather(line, gate(own_cot), place, core)
    ring_cot.send()
    kept = mark(*attention_forward(gate(query), key, value, starts, 0, split, ()))
    out_full, attended, logs = mark(
        *attention_forward(gate(query), key, value, starts, split, blocks, kept)
    )
    ring_cot.receive()
    ring_cot.send()
    up_w = mark(join(*gate(got_b, pair_b)).reshape(D, 2 * per_ff))

    def fed(part, kept):
        return mark(
            *over_tokens(
                feed,
                "feed",
                [(gate(normed), "rows"), (attended, "rows"), (up_w, ""), (up_bias, ""), (down_w, "")],
                [((count, 2 * per_ff + width), BF, "rows"), ((count, 2 * per_ff), F32, "rows")]
                + [((count // 2, D), BF, "half")] * 2,
                core,
                part,
                kept,
            )
        )

    kept = fed((0, 2), ())
    ring_cot.receive()
    ring_cot.send()
    mixed, slope, own_part, other_part = fed((1, 2), kept)
    ring_cot.receive()
    ring_cot.send()
    forward = Scatter(line, own_part, gate(other_part), place)
    ring_cot.receive()
    forward.start()
    grad_att, grad_hidden, all_cot, up_sums = mark(
        *over_arrivals(
            feed_back,
            "feed_back",
            ring_cot.arrived,
            core,
            [(gate(down_w), ""), (slope, "rows")],
            [
                ((count, width), BF, "rows"),
                ((count, 2 * per_ff), BF, "rows"),
                ((count, D), BF, "rows"),
                ((1, 2 * per_ff), F32, ""),
            ],
        )
    )

    def split_pair(field, axis):
        mine = lax.dynamic_index_in_dim(field, x, axis, keepdims=False)
        other = lax.dynamic_index_in_dim(field, 1 - x, axis, keepdims=False).astype(BF)
        return mine, other

    forward.step()
    grad_hidden = fence(grad_hidden, *line.last)
    grad_up_w = mark(dot_of(normed, grad_hidden, 0, 0).astype(BF))
    mine_b, other_b = mark(*split_pair(grad_up_w.reshape(H, 2, half, 2 * per_ff), 1))
    other_b = across_pair(other_b)
    back_in = (query, key, value, grad_att, out_full, logs, tables, starts)
    kept = mark(*attention_backward(gate(query), *back_in[1:], split, blocks, ()))
    forward.step()
    grad_qkv = mark(attention_backward(gate(query), *back_in[1:], 0, split, kept)[0])
    forward.step()
    mine_b, other_b = gate(mine_b, other_b)
    send_b = mark((mine_b.astype(F32) + other_b.astype(F32)).astype(BF))
    got_b = lax.all_to_all(send_b, AXES, 0, 0, tiled=True)
    norm_sums, *back_part = mark(
        *over_tokens(
            project_back,
            "project_back",
            [(gate(grad_qkv), "rows"), (grad_hidden, "rows"), (qkv_w, ""), (up_w, ""), (normed, "rows"), (gain, ""), (shift, "")],
            [((2, D), F32, "")] + [((count // 2, D), BF, "half")] * 2,
            core,
        )
    )
    backward = Scatter(line, *back_part, place)
    backward.start()
    grad_qkv = fence(grad_qkv, *line.last)
    grad_qkv_w = mark(dot_of(normed, grad_qkv, 0, 0).astype(BF))
    mine_a, other_a = mark(*split_pair(grad_qkv_w.reshape(H, 2, half, 3 * width), 1))
    other_a = across_pair(other_a)
    got_b = mark(gate(got_b))
    backward.step()
    cot_sum = jnp.sum(own_cot.astype(F32), axis=0)
    qkv_sums = jnp.sum(gate(grad_qkv).astype(F32), axis=0).reshape(3, 1, width)
    qkv_all = lax.dynamic_update_slice(jnp.zeros((3, pairs, width), F32), qkv_sums, (0, member, 0))
    up_all = lax.dynamic_update_slice(jnp.zeros((pairs, 2 * per_ff), F32), up_sums, (member, 0))
    sums = jnp.concatenate(
        [
            norm_sums.reshape(2, H, per).transpose(1, 0, 2),
            cot_sum.reshape(H, 1, per),
            qkv_all.reshape(H, 3, per),
            up_all.reshape(H, 4, per),
        ],
        axis=1,
    )
    sums = mark(jnp.pad(sums, ((0, 0), (0, half // 2 - sums.shape[1]), (0, width - per))).astype(BF))
    mine_a, other_a = gate(mine_a, other_a)
    sum_a = (mine_a.astype(F32) + other_a.astype(F32)).astype(BF)
    sum_a = sum_a.reshape(H, half, 3, width).transpose(0, 2, 1, 3).reshape(H, 3 * half, width)
    send_a = mark(jnp.concatenate([sum_a, sums], axis=1))
    got_a = lax.all_to_all(send_a, AXES, 0, 0, tiled=True)
    forward_sum = forward.step()
    output = mark((own_in.astype(F32) + (forward_sum + (out_bias + down_bias))).astype(BF))
    output = split_rows(output)
    grad_down = mark(dot_of(fence(mixed, *line.last), all_cot, 0, 0))
    mine_o, other_o = split_pair(grad_down[: 2 * per].reshape(2, per, D), 0)
    mine_d, other_d = split_pair(grad_down[2 * per :].reshape(2, per_ff, D), 0)
    mark(other_o, other_d)
    other_o, other_d = across_pair(other_o), across_pair(other_d)
    backward.step()
    got_a = mark(gate(got_a))
    backward.step()
    grad_up_rows = mark(unpack(gate(got_b), half, 1, 2 * per_ff))
    output = mark(join_rows(*gate(*output)))
    back_sum = backward.step()
    normal, scale = normalize(own_in.astype(F32))
    scaled = back_sum * gain
    grad_in = scale * (
        scaled
        - jnp.mean(scaled, axis=-1, keepdims=True)
        - normal * jnp.mean(scaled * normal, axis=-1, keepdims=True)
    )
    grad_input = mark((own_cot.astype(F32) + grad_in).astype(BF))
    grad_input = split_rows(grad_input)
    mine_o, other_o, mine_d, other_d = gate(mine_o, other_o, mine_d, other_d)
    grad_out_rows = mine_o + other_o.astype(F32)
    grad_down_rows = mine_d + other_d.astype(F32)
    mark(grad_out_rows, grad_down_rows)
    grad_input = mark(join_rows(*gate(*grad_input)))
    grad_qkv_rows = unpack(got_a, half, 3, width)
    sums = jnp.sum(got_a[:, 3 * half : 3 * half + 10, :per].astype(F32), axis=0)
    return (
        output,
        grad_input,
        sums[0],
        sums[1],
        grad_qkv_rows,
        sums[3:6].reshape(-1),
        grad_out_rows,
        sums[2],
        grad_up_rows,
        sums[6:10].reshape(-1),
        grad_down_rows,
        sums[2],
    )


def solution(mesh):
    return jax.shard_map(
        paired_step if suits(mesh) else gathered_step,
        mesh=mesh,
        in_specs=(
            P(None, ("seq", "head"), None),
            P(),
            P(("seq", "head")),
            P(("seq", "head")),
            P(("seq", "head"), None),
            P(("seq", "head")),
            P(("seq", "head"), None),
            P(("seq", "head")),
            P(("seq", "head"), None),
            P(("seq", "head")),
            P(("seq", "head"), None),
            P(("seq", "head")),
            P(None, ("seq", "head"), None),
        ),
        out_specs=(
            P(None, ("seq", "head"), None),
            P(None, ("seq", "head"), None),
            P(("seq", "head")),
            P(("seq", "head")),
            P(("seq", "head"), None),
            P(("seq", "head")),
            P(("seq", "head"), None),
            P(("seq", "head")),
            P(("seq", "head"), None),
            P(("seq", "head")),
            P(("seq", "head"), None),
            P(("seq", "head")),
        ),
        check_vma=False,
    )
```

```python
from functools import partial

import jax
import jax.numpy as jnp
from jax import lax
from jax.experimental import pallas as pl
from jax.experimental.pallas import tpu as pltpu
from jax.sharding import PartitionSpec as P

D = 2048
H = 32
HD = 64
ROT = 32


NEG_FILL = -1e30


def from_behind(block, axis, distance):
    devices = range(lax.axis_size(axis))
    route = [(i - distance, i) for i in devices if i - distance in devices]
    return lax.ppermute(block, axis, route)


def from_behind_2(shard, axis, by):
    length = lax.axis_size(axis)
    return lax.ppermute(shard, axis, [(i, (i + by) % length) for i in range(length)])


def rotate(field, cosine, sine):
    half_rot = ROT // 2
    first_part = field[..., :half_rot]
    second_part = field[..., half_rot:ROT]
    return jnp.concatenate(
        [
            first_part * cosine - second_part * sine,
            second_part * cosine + first_part * sine,
            field[..., ROT:],
        ],
        axis=-1,
    )


def rotation_tables(positions):
    half_rot = ROT // 2
    inverse = jnp.power(10000.0, -2.0 * jnp.arange(half_rot, dtype=jnp.float32) / ROT)
    angles = positions.astype(jnp.float32)[:, None] * inverse[None, :]
    return (jnp.cos(angles)[:, None, :], jnp.sin(angles)[:, None, :])


def layer_norm(values, gain_value, shift_value):
    center = values - jnp.mean(values, axis=-1, keepdims=True)
    spread = jnp.mean(center * center, axis=-1, keepdims=True)
    return center * lax.rsqrt(spread + 1e-05) * gain_value + shift_value


def segment_ids(doc_ends, positions):
    return jnp.sum((doc_ends[:, None, :] <= positions[None, :, None]).astype(jnp.int32), axis=2)


def gelu_tanh(values):
    return jax.nn.gelu(values, approximate=True)


def allowed_pairs(query_pos, query_seg, key_pos, key_seg):
    return (key_pos[None, :] <= query_pos[:, None]) & (key_seg[None, :] == query_seg[:, None])


def masked_scores(query_seq, key_seq, allowed):
    raw_scores = (
        jnp.einsum("qhd,khd->hqk", query_seq, key_seq, preferred_element_type=jnp.float32) * 0.125
    )
    return jnp.where(allowed[None], raw_scores, NEG_FILL)


def forward_step(members, query_pos, key_pos):
    top_val, total_val, accum_val, query_seq, kv_seq, query_seg, key_seg = members
    kv_split = kv_seq.reshape(kv_seq.shape[0], 2, -1, HD)
    allowed = allowed_pairs(query_pos, query_seg, key_pos, key_seg)
    masked = masked_scores(query_seq, kv_split[:, 0], allowed)
    new_top = jnp.maximum(top_val, jnp.max(masked, axis=2))
    weights = jnp.where(allowed[None], jnp.exp(masked - new_top[:, :, None]), 0.0)
    factor = jnp.exp(top_val - new_top)
    new_total = total_val * factor + jnp.sum(weights, axis=2)
    new_accum = accum_val * factor[:, :, None] + jnp.einsum(
        "hqk,khd->hqd",
        weights.astype(jnp.bfloat16),
        kv_split[:, 1],
        preferred_element_type=jnp.float32,
    )
    return (new_top, new_total, new_accum)


def backward_step(members, query_pos, key_pos):
    grad_query, grad_kv, query_seq, kv_seq, grad_att, log_total, row_dot, query_seg, key_seg = (
        members
    )
    key_total = kv_seq.shape[0]
    kv_split = kv_seq.reshape(key_total, 2, -1, HD)
    allowed = allowed_pairs(query_pos, query_seg, key_pos, key_seg)
    masked = masked_scores(query_seq, kv_split[:, 0], allowed)
    prob_full = jnp.where(allowed[None], jnp.exp(masked - log_total[:, :, None]), 0.0)
    grad_value = jnp.einsum(
        "hqk,qhd->khd", prob_full.astype(jnp.bfloat16), grad_att, preferred_element_type=jnp.float32
    )
    grad_probs = jnp.einsum(
        "qhd,khd->hqk", grad_att, kv_split[:, 1], preferred_element_type=jnp.float32
    )
    grad_scores = (prob_full * (grad_probs - row_dot[:, :, None])).astype(jnp.bfloat16)
    grad_query = (
        grad_query
        + jnp.einsum(
            "hqk,khd->hqd", grad_scores, kv_split[:, 0], preferred_element_type=jnp.float32
        )
        * 0.125
    )
    grad_key = (
        jnp.einsum("hqk,qhd->khd", grad_scores, query_seq, preferred_element_type=jnp.float32)
        * 0.125
    )
    grad_kv = grad_kv + jnp.stack([grad_key, grad_value], axis=1).reshape(key_total, 2, -1)
    return (grad_query, grad_kv)


def gathered_step(
    inputs,
    doc_lengths,
    ln_gain,
    ln_bias,
    w_qkv,
    b_qkv,
    w_out,
    b_out,
    w_fc1,
    b_fc1,
    w_fc2,
    b_fc2,
    cotangent,
):
    seq_total = inputs.shape[0]
    row_count = inputs.shape[1]
    head_count = lax.axis_size("head")
    seq_devices = lax.axis_size("seq")
    heads_here = H // head_count
    group_width = heads_here * HD
    block_rows = row_count * head_count
    seq_rank = lax.axis_index("seq")
    head_rank = lax.axis_index("head")
    doc_ends = jnp.cumsum(doc_lengths, axis=1)
    token_pos = (seq_rank * head_count + head_rank) * row_count + jnp.arange(
        row_count, dtype=jnp.int32
    )
    query_start = seq_rank * block_rows
    query_pos = query_start + jnp.arange(block_rows, dtype=jnp.int32)
    query_seg = segment_ids(doc_ends, query_pos)
    gathered = (
        lax.all_gather(ln_gain.astype(jnp.bfloat16), ("seq", "head"), axis=0, tiled=True),
        lax.all_gather(ln_bias.astype(jnp.bfloat16), ("seq", "head"), axis=0, tiled=True),
        lax.all_gather(w_qkv.astype(jnp.bfloat16), ("seq", "head"), axis=0, tiled=True),
        lax.all_gather(b_qkv.astype(jnp.bfloat16), ("seq", "head"), axis=0, tiled=True),
        lax.all_gather(w_out.astype(jnp.bfloat16), ("seq", "head"), axis=0, tiled=True),
        lax.all_gather(b_out.astype(jnp.bfloat16), ("seq", "head"), axis=0, tiled=True),
        lax.all_gather(w_fc1.astype(jnp.bfloat16), ("seq", "head"), axis=0, tiled=True),
        lax.all_gather(b_fc1.astype(jnp.bfloat16), ("seq", "head"), axis=0, tiled=True),
        lax.all_gather(w_fc2.astype(jnp.bfloat16), ("seq", "head"), axis=0, tiled=True),
        lax.all_gather(b_fc2.astype(jnp.bfloat16), ("seq", "head"), axis=0, tiled=True),
    )
    (
        gain_full,
        shift_full,
        qkv_weight,
        qkv_bias,
        out_weight,
        out_bias,
        up_weight,
        up_bias,
        down_weight,
        down_bias,
    ) = gathered
    flat_in = inputs.reshape(seq_total * row_count, D).astype(jnp.float32)
    normed, norm_back = jax.vjp(
        layer_norm, flat_in, gain_full.astype(jnp.float32), shift_full.astype(jnp.float32)
    )
    normed_low = normed.astype(jnp.bfloat16)
    qkv_all = (
        jnp.dot(normed_low, qkv_weight, preferred_element_type=jnp.float32)
        + qkv_bias.astype(jnp.float32)
    ).reshape(seq_total, row_count, 3, H, HD)
    cosine, sine = rotation_tables(token_pos)

    def turn_field(field):
        return rotate(field, cosine, sine)

    query_rot, turn_back = jax.vjp(turn_field, qkv_all[:, :, 0])
    key_rot = turn_field(qkv_all[:, :, 1])
    stacked = (
        jnp.stack([query_rot, key_rot, qkv_all[:, :, 2]], axis=2)
        .reshape(seq_total, row_count, 3, D)
        .astype(jnp.bfloat16)
    )
    by_heads = lax.all_to_all(stacked, "head", split_axis=3, concat_axis=1, tiled=True)
    query_heads = by_heads[:, :, 0].reshape(seq_total, block_rows, heads_here, HD)
    kv_heads = by_heads[:, :, 1:3]
    start_state = (
        jnp.full((seq_total, heads_here, block_rows), NEG_FILL, jnp.float32),
        jnp.zeros((seq_total, heads_here, block_rows), jnp.float32),
        jnp.zeros((seq_total, heads_here, block_rows, HD), jnp.float32),
    )
    shard_piece = lax.all_gather(kv_heads, "seq", axis=1, tiled=True)

    def one_turn(turn_index, current):
        kv_block = lax.dynamic_slice_in_dim(shard_piece, turn_index * block_rows, block_rows, 1)
        key_start = turn_index * block_rows
        key_pos = key_start + jnp.arange(block_rows, dtype=jnp.int32)
        key_seg = segment_ids(doc_ends, key_pos)

        def one_compute(state_in):
            return lax.map(
                partial(forward_step, query_pos=query_pos, key_pos=key_pos),
                (state_in[0], state_in[1], state_in[2], query_heads, kv_block, query_seg, key_seg),
            )

        return lax.cond(
            key_start < query_start + block_rows, one_compute, lambda state_in: state_in, current
        )

    top_all, total_all, accum_all = lax.fori_loop(
        0, shard_piece.shape[1] // block_rows, one_turn, start_state
    )
    attn_full = accum_all / total_all[:, :, :, None]
    log_total = top_all + jnp.log(total_all)
    attn_low = (
        jnp.transpose(attn_full, (0, 2, 1, 3))
        .reshape(seq_total, block_rows, group_width)
        .astype(jnp.bfloat16)
    )
    attended = lax.all_to_all(attn_low, "head", split_axis=1, concat_axis=2, tiled=True).reshape(
        seq_total * row_count, D
    )
    branch = jnp.dot(attended, out_weight, preferred_element_type=jnp.float32) + out_bias.astype(
        jnp.float32
    )
    hidden = jnp.dot(normed_low, up_weight, preferred_element_type=jnp.float32) + up_bias.astype(
        jnp.float32
    )
    active, gelu_back = jax.vjp(gelu_tanh, hidden)
    active_low = active.astype(jnp.bfloat16)
    feed = jnp.dot(active_low, down_weight, preferred_element_type=jnp.float32) + down_bias.astype(
        jnp.float32
    )
    output = (flat_in + branch + feed).astype(jnp.bfloat16).reshape(inputs.shape)
    qkv_weight, out_weight, up_weight, down_weight = (
        lax.all_gather(w_qkv.astype(jnp.bfloat16), ("seq", "head"), axis=0, tiled=True),
        lax.all_gather(w_out.astype(jnp.bfloat16), ("seq", "head"), axis=0, tiled=True),
        lax.all_gather(w_fc1.astype(jnp.bfloat16), ("seq", "head"), axis=0, tiled=True),
        lax.all_gather(w_fc2.astype(jnp.bfloat16), ("seq", "head"), axis=0, tiled=True),
    )
    grad_low = cotangent.reshape(seq_total * row_count, D)
    grad_full = grad_low.astype(jnp.float32)
    cot_sum = jnp.sum(grad_full, axis=0)
    grad_down_w = jnp.einsum("nf,nd->fd", active_low, grad_low, preferred_element_type=jnp.float32)
    grad_active = jnp.einsum("nd,fd->nf", grad_low, down_weight, preferred_element_type=jnp.float32)
    grad_hidden_low = gelu_back(grad_active)[0].astype(jnp.bfloat16)
    grad_up_w = jnp.einsum(
        "nm,nf->mf", normed_low, grad_hidden_low, preferred_element_type=jnp.float32
    )
    grad_up_b = jnp.sum(grad_hidden_low.astype(jnp.float32), axis=0)
    grad_normed = jnp.einsum(
        "nf,mf->nm", grad_hidden_low, up_weight, preferred_element_type=jnp.float32
    )
    grad_out_w = jnp.einsum("nm,nd->md", attended, grad_low, preferred_element_type=jnp.float32)
    grad_att_low = jnp.einsum(
        "nd,md->nm", grad_low, out_weight, preferred_element_type=jnp.float32
    ).astype(jnp.bfloat16)
    grad_heads = lax.all_to_all(
        grad_att_low.reshape(seq_total, row_count, D),
        "head",
        split_axis=2,
        concat_axis=1,
        tiled=True,
    ).reshape(seq_total, block_rows, heads_here, HD)
    row_dot = jnp.sum(
        jnp.transpose(grad_heads.astype(jnp.float32), (0, 2, 1, 3)) * attn_full, axis=3
    )

    def back_turn(turn_index, current):
        grad_query, grad_kv, kv_now = current
        source = (seq_rank - turn_index) % seq_devices
        key_pos = source * block_rows + jnp.arange(block_rows, dtype=jnp.int32)
        key_seg = segment_ids(doc_ends, key_pos)

        def back_compute(grads_in):
            return lax.map(
                partial(backward_step, query_pos=query_pos, key_pos=key_pos),
                (
                    grads_in[0],
                    grads_in[1],
                    query_heads,
                    kv_now,
                    grad_heads,
                    log_total,
                    row_dot,
                    query_seg,
                    key_seg,
                ),
            )

        return lax.cond(
            source <= seq_rank, back_compute, lambda grads_in: grads_in, (grad_query, grad_kv)
        )

    def pass_keys(kv_now):
        return from_behind(kv_now, "seq", 1)

    def pass_grads(grad_kv):
        return from_behind_2(grad_kv.astype(jnp.bfloat16), "seq", 1).astype(grad_kv.dtype)

    def loop_turn(turn_index, current):
        grad_query, grad_kv = back_turn(turn_index, current)
        return (grad_query, pass_grads(grad_kv), pass_keys(current[2]))

    start_grads = (
        jnp.zeros((seq_total, heads_here, block_rows, HD), jnp.float32),
        jnp.zeros((seq_total, block_rows, 2, group_width), jnp.float32),
        kv_heads,
    )
    loop_state = lax.fori_loop(0, seq_devices - 1, loop_turn, start_grads)
    grad_query, grad_kv = back_turn(seq_devices - 1, loop_state)
    grad_kv = pass_grads(grad_kv)
    back_heads = jnp.concatenate(
        [
            jnp.transpose(grad_query, (0, 2, 1, 3)).reshape(seq_total, block_rows, 1, group_width),
            grad_kv,
        ],
        axis=2,
    ).astype(jnp.bfloat16)
    back_tokens = (
        lax.all_to_all(back_heads, "head", split_axis=1, concat_axis=3, tiled=True)
        .astype(jnp.float32)
        .reshape(seq_total, row_count, 3, H, HD)
    )
    grad_qkv_low = (
        jnp.stack(
            [
                turn_back(back_tokens[:, :, 0])[0],
                turn_back(back_tokens[:, :, 1])[0],
                back_tokens[:, :, 2],
            ],
            axis=2,
        )
        .reshape(seq_total * row_count, 3 * D)
        .astype(jnp.bfloat16)
    )
    grad_qkv_w = jnp.einsum(
        "nm,nk->mk", normed_low, grad_qkv_low, preferred_element_type=jnp.float32
    )
    grad_qkv_b = jnp.sum(grad_qkv_low.astype(jnp.float32), axis=0)
    grad_normed = grad_normed + jnp.einsum(
        "nk,mk->nm", grad_qkv_low, qkv_weight, preferred_element_type=jnp.float32
    )
    grad_in, grad_gain, grad_shift = norm_back(grad_normed)
    grad_input = (grad_full + grad_in).astype(jnp.bfloat16).reshape(inputs.shape)
    sums_all = (
        lax.psum_scatter(grad_gain, ("seq", "head"), scatter_dimension=0, tiled=True),
        lax.psum_scatter(grad_shift, ("seq", "head"), scatter_dimension=0, tiled=True),
        lax.psum_scatter(grad_qkv_w, ("seq", "head"), scatter_dimension=0, tiled=True),
        lax.psum_scatter(grad_qkv_b, ("seq", "head"), scatter_dimension=0, tiled=True),
        lax.psum_scatter(grad_out_w, ("seq", "head"), scatter_dimension=0, tiled=True),
        lax.psum_scatter(cot_sum, ("seq", "head"), scatter_dimension=0, tiled=True),
        lax.psum_scatter(grad_up_w, ("seq", "head"), scatter_dimension=0, tiled=True),
        lax.psum_scatter(grad_up_b, ("seq", "head"), scatter_dimension=0, tiled=True),
        lax.psum_scatter(grad_down_w, ("seq", "head"), scatter_dimension=0, tiled=True),
    )
    return (
        output,
        grad_input,
        sums_all[0],
        sums_all[1],
        sums_all[2],
        sums_all[3],
        sums_all[4],
        sums_all[5],
        sums_all[6],
        sums_all[7],
        sums_all[8],
        sums_all[5],
    )


BF = jnp.bfloat16
F32 = jnp.float32
AXES = ("seq", "head")
FF = 8192
BLOCK = 256
KEYS = 512


QUICK = pl.CostEstimate(flops=1 << 20, bytes_accessed=1 << 16, transcendentals=0)


def suits(mesh):
    return mesh.shape["seq"] * mesh.shape["head"] == H and mesh.shape["head"] == 4


def coordinates(rank):
    return rank // 8, (rank // 4) % 2, (rank // 2) % 2, rank % 2


def rank_of(z, core, y, x):
    return ((z * 2 + core) * 2 + y) * 2 + x


def route(step):
    return [(rank, rank_of(*step(*coordinates(rank)))) for rank in range(H)]


def ring_place(z, y, length):
    return z if y == 0 else length - 1 - z


def ring_point(place, length):
    place = place % length
    return (place, 0) if place < length // 2 else (length - 1 - place, 1)


def ring_route(by):
    length = H // 4

    def step(z, core, y, x):
        new_z, new_y = ring_point(ring_place(z, y, length) + by, length)
        return new_z, core, new_y, x

    return route(step)


def across_pair(value):
    return lax.ppermute(value, AXES, route(lambda z, core, y, x: (z, core, y, 1 - x)))


def across_cores(value):
    return lax.ppermute(value, AXES, route(lambda z, core, y, x: (z, 1 - core, y, x)))


def up_ring(value):
    return lax.ppermute(value, AXES, ring_route(1))


def down_ring(value):
    return lax.ppermute(value, AXES, ring_route(-1))


def block_index(place, core):
    length = H // 4
    place = place % length
    z = jnp.where(place < length // 2, place, length - 1 - place)
    y = (place >= length // 2).astype(jnp.int32)
    return (z * 2 + core) * 2 + y


def fence(value, *others):
    anywhere = pl.BlockSpec(memory_space=pl.ANY)
    return pl.pallas_call(
        lambda *refs: None,
        in_specs=[anywhere] * (1 + len(others)),
        out_specs=anywhere,
        out_shape=jax.ShapeDtypeStruct(value.shape, value.dtype),
        input_output_aliases={0: 0},
        cost_estimate=QUICK,
        name="fence",
    )(value, *others)


class Line:
    def __init__(self):
        self.last = ()

    def gate(self, *values):
        values = lax.optimization_barrier((values, self.last))[0] if self.last else values
        return values if len(values) > 1 else values[0]

    def mark(self, *values):
        self.last = values
        return values if len(values) > 1 else values[0]


class Gather:
    def __init__(self, line, own, place, core):
        self.line, self.place, self.core = line, place, core
        self.flying = (own, own)
        self.arrived, self.hop = [], 0
        self.land([(0, own)])

    def land(self, chunks):
        self.arrived += [(self.place + offset, chunk, across_cores(chunk)) for offset, chunk in chunks]
        self.hop = self.hop + 1

    def send(self):
        up, down = self.line.gate(*self.flying)
        if self.hop == H // 8:
            half = up.shape[0] // 2
            up, down = up[:half], down[half:]
        self.flying = up_ring(up), down_ring(down)

    def receive(self):
        hop = self.hop
        before = [other for _, _, other in self.arrived[-2:]]
        up, down, *before = self.line.mark(*self.line.gate(*self.flying, *before))
        for i, other in enumerate(before, len(self.arrived) - len(before)):
            self.arrived[i] = (*self.arrived[i][:2], other)
        if hop == H // 8:
            self.land([(hop, self.line.mark(jnp.concatenate([up, down], axis=0)))])
        else:
            self.flying = up, down
            self.land([(-hop, up), (hop, down)])


class Scatter:
    def __init__(self, line, own, other, place):
        length = H // 4
        self.line, self.place = line, place
        self.rows = own.shape[0] // length
        self.own = own.reshape(length, self.rows, D)
        self.got = across_cores(other).reshape(length, self.rows, D)
        self.hop = length // 2

    def term(self, offset):
        length = H // 4
        at = (self.place + offset) % length
        index = jnp.where(at < length // 2, 2 * at, 2 * (length - 1 - at) + 1)
        mine = lax.dynamic_index_in_dim(self.own, index, 0, keepdims=False)
        theirs = lax.dynamic_index_in_dim(self.got, index, 0, keepdims=False)
        return mine.astype(F32) + theirs.astype(F32)

    def start(self):
        self.got = self.line.gate(self.got)
        far = self.line.mark(self.term(self.hop).astype(BF))
        half = self.rows // 2
        self.flying = up_ring(far[:half]), down_ring(far[half:])

    def step(self):
        up, down = (part.astype(F32) for part in self.line.gate(*self.flying))
        if self.hop == H // 8:
            pad = jnp.zeros((self.rows // 2, D), F32)
            up, down = jnp.concatenate([up, pad], axis=0), jnp.concatenate([pad, down], axis=0)
        self.hop -= 1
        if not self.hop:
            return self.term(0) + up + down
        up = (up + self.term(self.hop)).astype(BF)
        down = (down + self.term(-self.hop)).astype(BF)
        self.line.mark(up, down)
        self.flying = up_ring(up), down_ring(down)


class Scatter:
    def __init__(self, line, own, other, place):
        length = H // 4
        self.line, self.place = line, place
        self.rows = own.shape[0] // length
        self.own = own.reshape(length, self.rows, D)
        self.got = across_cores(other).reshape(length, self.rows, D)
        self.hop = length // 2

    def term(self, offset):
        length = H // 4
        at = (self.place + offset) % length
        index = jnp.where(at < length // 2, 2 * at, 2 * (length - 1 - at) + 1)
        mine = lax.dynamic_index_in_dim(self.own, index, 0, keepdims=False)
        theirs = lax.dynamic_index_in_dim(self.got, index, 0, keepdims=False)
        return mine.astype(F32) + theirs.astype(F32)

    def start(self):
        self.got = self.line.gate(self.got)
        far = self.line.mark(self.term(self.hop).astype(BF))
        half = self.rows // 2
        self.flying = up_ring(far[:half]), down_ring(far[half:])

    def step(self):
        up, down = (part.astype(F32) for part in self.line.gate(*self.flying))
        if self.hop == H // 8:
            pad = jnp.zeros((self.rows // 2, D), F32)
            up, down = jnp.concatenate([up, pad], axis=0), jnp.concatenate([pad, down], axis=0)
        self.hop -= 1
        if not self.hop:
            return self.term(0) + up + down
        up = (up + self.term(self.hop)).astype(BF)
        down = (down + self.term(-self.hop)).astype(BF)
        self.line.mark(up, down)
        self.flying = up_ring(up), down_ring(down)


def settle(wholes, kept, chunks, vectors):
    rows, width = chunks[0][1].shape
    many, layers = len(chunks), 2 if vectors else 1

    def kernel(index_ref, *refs):
        blocks, rest = refs[:many], refs[many + (layers if kept else 0) :]
        outs = rest[len(vectors) : len(vectors) + layers]
        hold = rest[-1] if vectors else outs[0]
        for i, block in enumerate(blocks):

            @pl.when(pl.program_id(0) == i)
            def _(block=block):
                hold[...] = block[...]

        if vectors:
            values = hold[...].astype(F32)
            center = values - jnp.mean(values, axis=1, keepdims=True)
            scale = lax.rsqrt(jnp.mean(center * center, axis=1, keepdims=True) + 1e-05)
            normal = center * scale
            outs[0][...] = (normal * rest[0][...] + rest[1][...]).astype(BF)
            outs[1][...] = normal.astype(BF)

    whole = jax.ShapeDtypeStruct((wholes, width), BF)
    fixed = pl.BlockSpec((rows, width), lambda i, index: (0, 0))
    return pl.pallas_call(
        kernel,
        grid_spec=pltpu.PrefetchScalarGridSpec(
            num_scalar_prefetch=1,
            grid=(many,),
            in_specs=[fixed] * many
            + [pl.BlockSpec(memory_space=pl.ANY)] * (layers if kept else 0)
            + [pl.BlockSpec((1, width), lambda i, index: (0, 0))] * len(vectors),
            out_specs=[pl.BlockSpec((rows, width), lambda i, index: (index[i], 0))] * layers,
            scratch_shapes=[pltpu.VMEM((rows, width), BF)] if vectors else [],
        ),
        out_shape=[whole] * layers,
        input_output_aliases={1 + many + i: i for i in range(layers)} if kept else {},
        cost_estimate=QUICK,
        name="settle",
    )(jnp.stack([index for index, _ in chunks]), *[c for _, c in chunks], *(kept or ()), *vectors)


def turn(field, tables, sign):
    half_rot = ROT // 2
    first = pltpu.roll(field, 2 * HD - half_rot, 1)
    second = pltpu.roll(field, half_rot, 1)
    return field * tables[0] + sign * (second * tables[2] - first * tables[1])


def turn_tables(positions):
    half_rot = ROT // 2
    lane = jnp.arange(2 * HD, dtype=jnp.int32) % HD
    inverse = jnp.power(10000.0, -2.0 * (lane % half_rot).astype(F32) / ROT)
    angles = positions.astype(F32)[:, None] * inverse[None, :]
    sine = jnp.sin(angles)
    return jnp.stack(
        [
            jnp.where(lane < ROT, jnp.cos(angles), 1.0),
            jnp.where(lane < half_rot, sine, 0.0),
            jnp.where((lane >= half_rot) & (lane < ROT), sine, 0.0),
        ]
    )


def head_lanes(value, head):
    lane = lax.broadcasted_iota(jnp.int32, value.shape, 1)
    return jnp.where((lane >= HD) if head else (lane < HD), value, jnp.zeros_like(value))


def dot_of(left, right, left_dim, right_dim):
    return lax.dot_general(
        left, right, (((left_dim,), (right_dim,)), ((), ())), preferred_element_type=F32
    )


def project(values, gain_ref, shift_ref, w_ref, bias_ref, tables_ref, normed_ref, q_ref, k_ref, v_ref):
    values = values.astype(F32)
    center = values - jnp.mean(values, axis=1, keepdims=True)
    scale = lax.rsqrt(jnp.mean(center * center, axis=1, keepdims=True) + 1e-05)
    normed = (center * scale * gain_ref[...] + shift_ref[...]).astype(BF)
    normed_ref[...] = normed.reshape(normed_ref.shape)
    width = 2 * HD
    raw = dot_of(normed, w_ref[...], 1, 0) + bias_ref[...]
    tables = tables_ref[...].reshape(3, BLOCK, width)
    q_ref[...] = turn(raw[:, :width], tables, 1.0).astype(BF).reshape(q_ref.shape)
    k_ref[...] = turn(raw[:, width : 2 * width], tables, 1.0).astype(BF).reshape(k_ref.shape)
    v_ref[...] = raw[:, 2 * width :].astype(BF).reshape(v_ref.shape)


def feed(core_ref, normed_ref, att_ref, up_ref, bias_ref, down_ref, mixed_ref, slope_ref, *part_refs):
    root, cubic = 0.7978845608028654, 0.044715
    for side, part_ref in enumerate(part_refs):
        here = pl.ds(pl.multiple_of(BLOCK * ((core_ref[0] + side) % 2), BLOCK), BLOCK)
        hidden = dot_of(normed_ref[here, :], up_ref[...], 1, 0) + bias_ref[...]
        square = hidden * hidden
        bend = jnp.tanh(root * (hidden + cubic * (square * hidden)))
        active = (0.5 * hidden * (1.0 + bend)).astype(BF)
        mixed_ref[here, : 2 * HD] = att_ref[here, :]
        mixed_ref[here, 2 * HD :] = active
        slope_ref[here, :] = 0.5 * (1.0 + bend) + 0.5 * hidden * (1.0 - bend * bend) * (
            root * (1.0 + 3.0 * cubic * square)
        )
        part = dot_of(att_ref[here, :], down_ref[: 2 * HD, :], 1, 0)
        part = part + dot_of(active, down_ref[2 * HD :, :], 1, 0)
        part_ref[...] = part.astype(BF)


def feed_back(cot, down_ref, slope_ref, att_ref, hidden_ref, whole_ref, sum_ref):
    whole_ref[...] = cot.reshape(whole_ref.shape)
    mixed = dot_of(cot, down_ref[...], 1, 1)
    att_ref[...] = mixed[:, : 2 * HD].astype(BF).reshape(att_ref.shape)
    slope = slope_ref[...].reshape(BLOCK, slope_ref.shape[-1])
    hidden = (mixed[:, 2 * HD :] * slope).astype(BF)
    hidden_ref[...] = hidden.reshape(hidden_ref.shape)

    @pl.when(pl.program_id(0) == 0)
    def _():
        sum_ref[...] = jnp.zeros_like(sum_ref)

    sum_ref[...] += jnp.sum(hidden.astype(F32), axis=0, keepdims=True)


def project_back(core_ref, qkv_ref, hidden_ref, wq_ref, up_ref, normed_ref, gain_ref, shift_ref, sum_ref, *part_refs):
    @pl.when(pl.program_id(0) == 0)
    def _():
        sum_ref[...] = jnp.zeros_like(sum_ref)

    step = D // 4
    for side, part_ref in enumerate(part_refs):
        here = pl.ds(pl.multiple_of(BLOCK * ((core_ref[0] + side) % 2), BLOCK), BLOCK)
        qkv, hidden = qkv_ref[here, :], hidden_ref[here, :]
        for first in range(0, D, step):
            some = pl.ds(first, step)
            part = dot_of(qkv, wq_ref[some, :], 1, 1) + dot_of(hidden, up_ref[some, :], 1, 1)
            part_ref[:, some] = part.astype(BF)
            normal = (normed_ref[here, some].astype(F32) - shift_ref[:, some]) / gain_ref[:, some]
            sum_ref[0:1, some] += jnp.sum(part * normal, axis=0, keepdims=True)
            sum_ref[1:2, some] += jnp.sum(part, axis=0, keepdims=True)


def over_arrivals(kernel, name, arrived, core, ins, outs):
    length = H // 4
    rows, lanes = arrived[0][1].shape
    places = jnp.stack([place for place, _, _ in arrived]) % length
    y = (places >= length // 2).astype(jnp.int32)
    z = jnp.where(y == 0, places, length - 1 - places)
    lead = (length // 2, 2, 2, rows)

    def body(core_ref, z_ref, y_ref, *refs):
        blocks, rest, hold = refs[: 2 * length], refs[2 * length : -1], refs[-1]
        for step in range(length):

            @pl.when(pl.program_id(0) == step)
            def _(step=step):
                for side in range(2):
                    first = pl.multiple_of(rows * ((core_ref[0] + side) % 2), rows)
                    hold[pl.ds(first, rows), :] = blocks[2 * step + side][...]

        kernel(hold[...], *rest)

    def view(array, how):
        if how == "rows":
            return array.reshape(lead + array.shape[1:])
        return array.reshape(array.shape[:1] + lead + array.shape[2:]) if how == "tables" else array

    def spec(shape, how):
        if how == "rows":
            return pl.BlockSpec((1, 2, 1, rows, shape[-1]), lambda i, c, z, y: (z[i], 0, y[i], 0, 0))
        if how == "tables":
            return pl.BlockSpec(
                (shape[0], 1, 2, 1, rows, shape[-1]), lambda i, c, z, y: (0, z[i], 0, y[i], 0, 0)
            )
        return pl.BlockSpec(shape, lambda i, *_: (0, 0))

    once = pl.BlockSpec((rows, lanes), lambda i, *_: (0, 0), pipeline_mode=pl.Buffered(1))
    results = pl.pallas_call(
        body,
        grid_spec=pltpu.PrefetchScalarGridSpec(
            num_scalar_prefetch=3,
            grid=(length,),
            in_specs=[once] * (2 * length) + [spec(a.shape, how) for a, how in ins],
            out_specs=[spec(shape, how) for shape, _, how in outs],
            scratch_shapes=[pltpu.VMEM((2 * rows, lanes), BF)],
        ),
        out_shape=[
            jax.ShapeDtypeStruct(lead + shape[1:] if how == "rows" else shape, kind)
            for shape, kind, how in outs
        ],
        cost_estimate=QUICK,
        name=name,
    )(
        jnp.reshape(core, (1,)),
        z,
        y,
        *[block for _, mine, other in arrived for block in (mine, other)],
        *[view(a, how) for a, how in ins],
    )
    return [result.reshape(shape) for result, (shape, _, _) in zip(results, outs)]


def over_tokens(kernel, name, ins, outs, core, part=(0, 1), kept=()):
    count = ins[0][0].shape[0]
    size = 2 * BLOCK
    steps = count // size // part[1]
    first = part[0] * steps

    def spec(shape, how):
        if how in ("rows", "half"):
            rows = size if how == "rows" else size // 2
            return pl.BlockSpec((rows,) + shape[1:], lambda i, *_: (i + first, 0))
        return pl.BlockSpec(shape, lambda i, *_: (0, 0))

    def body(core_ref, *refs):
        kernel(core_ref, *refs[: len(ins)], *refs[len(ins) + len(kept) :])

    return pl.pallas_call(
        body,
        grid_spec=pltpu.PrefetchScalarGridSpec(
            num_scalar_prefetch=1,
            grid=(steps,),
            in_specs=[spec(a.shape, how) for a, how in ins]
            + [pl.BlockSpec(memory_space=pl.ANY)] * len(kept),
            out_specs=[spec(shape, how) for shape, _, how in outs],
        ),
        out_shape=[jax.ShapeDtypeStruct(shape, kind) for shape, kind, _ in outs],
        input_output_aliases={1 + len(ins) + i: i for i in range(len(kept))},
        cost_estimate=QUICK,
        name=name,
    )(jnp.reshape(core, (1,)), *[a for a, _ in ins], *kept)


def key_chunk(index):
    return pl.ds(pl.multiple_of(index * KEYS, KEYS), KEYS)


def allowed_keys(starts, chunk, block):
    keys = chunk * KEYS + lax.broadcasted_iota(jnp.int32, (KEYS, BLOCK), 0)
    queries = block * BLOCK + lax.broadcasted_iota(jnp.int32, (1, BLOCK), 1)
    return (keys >= starts) & (keys <= queries)


def fold(value, how):
    return how(value.reshape(KEYS // 8, 8, BLOCK), axis=0)


def attend_forward(first_block, kept, q_ref, k_ref, v_ref, starts_ref, *refs):
    o_ref, low_ref, lse_ref, scores_ref, acc_ref, row_ref = refs[kept:]
    block = first_block + pl.program_id(0)
    query = q_ref[...] * 0.125
    queries = [head_lanes(query, head) for head in range(2)]
    starts = starts_ref[...]
    chunks = ((block + 1) * BLOCK + KEYS - 1) // KEYS
    row_ref[...] = jnp.full_like(row_ref, NEG_FILL)

    def score(chunk, carry):
        here = key_chunk(chunk)
        keys = k_ref[here, :]
        allowed = allowed_keys(starts, chunk, block)
        for head in range(2):
            scores = jnp.where(allowed, dot_of(keys, queries[head], 1, 1), NEG_FILL)
            scores_ref[head, here, :] = scores
            row_ref[head] = jnp.maximum(row_ref[head], fold(scores, jnp.max))
        return carry

    lax.fori_loop(0, chunks, score, 0)
    tops = [jnp.max(row_ref[head], axis=0, keepdims=True) for head in range(2)]
    acc_ref[...] = jnp.zeros_like(acc_ref)
    row_ref[...] = jnp.zeros_like(row_ref)

    def mix(chunk, carry):
        here = key_chunk(chunk)
        values = v_ref[here, :]
        for head in range(2):
            weights = jnp.exp(scores_ref[head, here, :] - tops[head])
            row_ref[head] += fold(weights, jnp.sum)
            acc_ref[head] += dot_of(values, weights.astype(BF), 0, 0)
        return carry

    lax.fori_loop(0, chunks, mix, 0)
    totals = [jnp.sum(row_ref[head], axis=0, keepdims=True) for head in range(2)]
    row = lax.broadcasted_iota(jnp.int32, acc_ref.shape[1:], 0)
    out = jnp.where(row < HD, acc_ref[0] / totals[0], acc_ref[1] / totals[1]).T
    o_ref[...] = out
    low_ref[...] = out.astype(BF)
    lse_ref[...] = jnp.concatenate([tops[i] + jnp.log(totals[i]) for i in range(2)], axis=0)


def attend_backward(last_block, kept, q_ref, k_ref, v_ref, g_ref, o_ref, lse_ref, tables_ref, starts_ref, *refs):
    before, (out_ref, gk_ref, gv_ref, gq_ref) = refs[:kept], refs[kept:]
    step = pl.program_id(0)
    block = last_block - step
    width = 2 * HD

    @pl.when(step == 0)
    def _():
        gk_ref[...] = before[1][...] if kept else jnp.zeros_like(gk_ref)
        gv_ref[...] = before[2][...] if kept else jnp.zeros_like(gv_ref)

    gq_ref[...] = jnp.zeros_like(gq_ref)
    query, grad = q_ref[...] * 0.125, g_ref[...]
    product = (grad.astype(F32) * o_ref[...]).T
    dots = [jnp.sum(product[i * HD : (i + 1) * HD], axis=0, keepdims=True) for i in range(2)]
    queries = [head_lanes(query, head) for head in range(2)]
    grads = [head_lanes(grad, head) for head in range(2)]
    logs = [lse_ref[head : head + 1, :] for head in range(2)]
    starts = starts_ref[...]

    def work(chunk, carry):
        here = key_chunk(chunk)
        keys, values = k_ref[here, :], v_ref[here, :]
        allowed = allowed_keys(starts, chunk, block)
        for head in range(2):
            scores = dot_of(keys, queries[head], 1, 1)
            probs = jnp.where(allowed, jnp.exp(scores - logs[head]), 0.0)
            grad_probs = dot_of(values, grads[head], 1, 1)
            grad_scores = (probs * (grad_probs - dots[head])).astype(BF)
            gv_ref[here, :] += dot_of(probs.astype(BF), grads[head], 1, 0)
            gk_ref[here, :] += dot_of(grad_scores, queries[head], 1, 0)
            gq_ref[...] += dot_of(head_lanes(keys, head), grad_scores, 0, 0)
        return carry

    lax.fori_loop(0, ((block + 1) * BLOCK + KEYS - 1) // KEYS, work, 0)
    tables = tables_ref[...]
    here = pl.ds(pl.multiple_of(block * BLOCK, BLOCK), BLOCK)

    def back(value):
        return turn(value.astype(BF).astype(F32), tables, -1.0).astype(BF)

    out_ref[:, :width] = back(gq_ref[...].T * 0.125)
    out_ref[:, width : 2 * width] = back(gk_ref[here, :])
    out_ref[:, 2 * width :] = gv_ref[here, :].astype(BF)


def attention_forward(query, key, value, starts, first, last, kept):
    count = query.shape[0]
    width = 2 * HD
    rows = lambda i: (i + first, 0)
    block = pl.BlockSpec((BLOCK, width), rows)
    row = lambda many: pl.BlockSpec((many, BLOCK), lambda i: (0, i + first))
    full = pl.BlockSpec((count, width), lambda i: (0, 0))
    return pl.pallas_call(
        partial(attend_forward, first, len(kept)),
        grid=(last - first,),
        in_specs=[block, full, full, row(1)] + [pl.BlockSpec(memory_space=pl.ANY)] * len(kept),
        out_specs=[block] * 2 + [row(2)],
        out_shape=[
            jax.ShapeDtypeStruct((count, width), F32),
            jax.ShapeDtypeStruct((count, width), BF),
            jax.ShapeDtypeStruct((2, count), F32),
        ],
        scratch_shapes=[
            pltpu.VMEM((2, count, BLOCK), F32),
            pltpu.VMEM((2, width, BLOCK), F32),
            pltpu.VMEM((2, 8, BLOCK), F32),
        ],
        input_output_aliases={4 + i: i for i in range(len(kept))},
        cost_estimate=QUICK,
        name="attend_forward",
    )(query, key, value, starts, *kept)


def attention_backward(query, key, value, grad, out, logs, tables, starts, first, last, kept):
    count = query.shape[0]
    width = 2 * HD
    rows = lambda i: (last - 1 - i, 0)
    block = pl.BlockSpec((BLOCK, width), rows)
    full = pl.BlockSpec((count, width), lambda i: (0, 0))
    row = lambda many: pl.BlockSpec((many, BLOCK), lambda i: (0, last - 1 - i))
    return pl.pallas_call(
        partial(attend_backward, last - 1, len(kept)),
        grid=(last - first,),
        in_specs=[
            block,
            full,
            full,
            block,
            block,
            row(2),
            pl.BlockSpec((3, BLOCK, width), lambda i: (0, last - 1 - i, 0)),
            row(1),
        ]
        + [pl.BlockSpec(memory_space=pl.ANY), full, full][: len(kept)],
        out_specs=[pl.BlockSpec((BLOCK, 3 * width), rows), full, full],
        out_shape=[
            jax.ShapeDtypeStruct((count, 3 * width), BF),
            jax.ShapeDtypeStruct((count, width), F32),
            jax.ShapeDtypeStruct((count, width), F32),
        ],
        scratch_shapes=[pltpu.VMEM((width, BLOCK), F32)],
        input_output_aliases={8: 0} if kept else {},
        cost_estimate=QUICK,
        name="attend_backward",
    )(query, key, value, grad, out, logs, tables, starts, *kept)


def unpack(rows, half, parts, columns):
    many = rows.shape[0]

    def kernel(rows_ref, out_ref):
        for device in range(many):
            side = slice((device % 2) * half, (device % 2 + 1) * half)
            for part in range(parts):
                first = (part * (many // 2) + device // 2) * columns
                out_ref[side, first : first + columns] = rows_ref[
                    device, part * half : (part + 1) * half, :
                ].astype(F32)

    return pl.pallas_call(
        kernel,
        out_shape=jax.ShapeDtypeStruct((2 * half, parts * columns * many // 2), F32),
        cost_estimate=QUICK,
        name="unpack",
    )(rows)


def normalize(values):
    center = values - jnp.mean(values, axis=-1, keepdims=True)
    scale = lax.rsqrt(jnp.mean(center * center, axis=-1, keepdims=True) + 1e-05)
    return center * scale, scale


def paired_step(
    inputs,
    doc_lengths,
    ln_gain,
    ln_bias,
    w_qkv,
    b_qkv,
    w_out,
    b_out,
    w_fc1,
    b_fc1,
    w_fc2,
    b_fc2,
    cotangent,
):
    rows = inputs.shape[1]
    count = rows * H
    rank = lax.axis_index("seq") * 4 + lax.axis_index("head")
    x = rank % 2
    y, core, z = (rank // 2) % 2, (rank // 4) % 2, rank // 8
    length = H // 4
    place = jnp.where(y == 0, z, length - 1 - z)

    def split_rows(field):
        mine = lax.dynamic_slice_in_dim(field, x * rows, rows, 0)
        return mine, across_pair(lax.dynamic_slice_in_dim(field, (1 - x) * rows, rows, 0))

    def join_rows(mine, got):
        return jnp.where(x == 0, jnp.stack([mine, got]), jnp.stack([got, mine]))

    per = D // H
    per_ff = FF // H
    pairs = H // 2
    width = 2 * HD
    half = per // 2

    line = Line()
    gate, mark = line.gate, line.mark

    def pair_blocks(field):
        mine = lax.dynamic_index_in_dim(field, x, 0, keepdims=False)
        return mine, lax.dynamic_index_in_dim(field, 1 - x, 0, keepdims=False)

    def pair_rows(mine, got):
        return jnp.where(x == 0, jnp.concatenate([mine, got]), jnp.concatenate([got, mine]))

    mine_in, other_in = mark(*pair_blocks(inputs))
    got_in = across_pair(other_in)
    small = jnp.concatenate([ln_gain, ln_bias, b_out, b_fc2, b_qkv, b_fc1]).astype(BF).reshape(-1, per)
    small = jnp.pad(small, ((0, half // 2 - small.shape[0]), (0, width - per)))
    send_a = jnp.concatenate(
        [
            gate(w_qkv).astype(BF).reshape(2, half, 3, pairs, width).transpose(3, 0, 2, 1, 4).reshape(H, 3 * half, width),
            jnp.broadcast_to(small[None], (H, half // 2, width)),
        ],
        axis=1,
    )
    own_in = mark(pair_rows(mine_in, got_in))
    send_a = mark(gate(send_a))
    got_a = lax.all_to_all(send_a, AXES, 0, 0, tiled=True)
    mine_cot, other_cot = pair_blocks(gate(cotangent))
    mine_d = jnp.concatenate([gate(w_out), w_fc2], axis=0).astype(BF)
    mark(other_cot, mine_d)
    got_cot = across_pair(other_cot)
    pair_d = across_pair(mine_d)
    send_b = mark(
        gate(w_fc1)
        .astype(BF)
        .reshape(2, half, pairs, 2 * per_ff)
        .transpose(2, 0, 1, 3)
        .reshape(H, half, 2 * per_ff)
    )
    positions = gate(jnp.arange(count, dtype=jnp.int32))
    doc_ends = jnp.cumsum(lax.dynamic_index_in_dim(doc_lengths, x, 0, keepdims=False))
    starts = jnp.max(
        jnp.where(doc_ends[:, None] <= positions[None, :], doc_ends[:, None], 0), axis=0
    )[None, :]
    starts, tables = mark(*lax.optimization_barrier((starts, turn_tables(positions))))
    ring_in = Gather(line, gate(own_in), place, core)
    ring_in.send()
    ring_in.receive()
    ring_in.send()
    mine_d, pair_d = gate(mine_d, pair_d)
    low_d, high_d = jnp.where(x == 0, mine_d, pair_d), jnp.where(x == 0, pair_d, mine_d)
    down_w = mark(
        jnp.concatenate([low_d[:per], high_d[:per], low_d[per:], high_d[per:]], axis=0)
    )
    got_a = gate(got_a)
    part_a = got_a[:, : 3 * half]
    small = got_a[:, 3 * half :, :per].astype(F32)
    gain, shift, out_bias, down_bias = [small[:, i].reshape(1, D) for i in range(4)]
    member = rank // 2
    qkv_bias = small[:, 4:7].reshape(3, pairs, width)
    qkv_bias = lax.dynamic_index_in_dim(qkv_bias, member, 1, keepdims=False).reshape(1, 3 * width)
    up_bias = small[:, 7:11].reshape(pairs, 2 * per_ff)
    up_bias = lax.dynamic_index_in_dim(up_bias, member, 0)
    small = (gain, shift, qkv_bias, up_bias, out_bias, down_bias)
    part_a, *small = mark(*lax.optimization_barrier((part_a, *small)))
    gain, shift, qkv_bias, up_bias, out_bias, down_bias = small
    pair_a = across_pair(part_a)

    def join(mine, got):
        low, high = jnp.where(x == 0, mine, got), jnp.where(x == 0, got, mine)
        return jnp.stack([low, high], axis=1)

    own_cot = mark(pair_rows(*gate(mine_cot, got_cot)))
    ring_in.receive()
    ring_in.send()
    ring_in.receive()
    qkv_w = join(*gate(part_a, pair_a)).reshape(H, 2, 3, half, width)
    qkv_w = mark(qkv_w.transpose(0, 1, 3, 2, 4).reshape(D, 3 * width))
    ring_in.send()
    ring_in.receive()
    send_b = gate(send_b)
    got_b = lax.all_to_all(send_b, AXES, 0, 0, tiled=True)
    normed, query, key, value = mark(
        *over_arrivals(
            project,
            "project",
            ring_in.arrived,
            core,
            [(gate(gain), ""), (shift, ""), (qkv_w, ""), (qkv_bias, ""), (tables, "tables")],
            [((count, D), BF, "rows")] + [((count, width), BF, "rows")] * 3,
        )
    )
    blocks = count // BLOCK
    got_b = mark(gate(got_b))
    pair_b = across_pair(got_b)
    ring_cot = Gather(line, gate(own_cot), place, core)
    ring_cot.send()
    out_full, attended, logs = mark(
        *attention_forward(gate(query), key, value, starts, 0, blocks, ())
    )
    ring_cot.receive()
    ring_cot.send()
    up_w = mark(join(*gate(got_b, pair_b)).reshape(D, 2 * per_ff))

    def fed(part, kept):
        return mark(
            *over_tokens(
                feed,
                "feed",
                [(gate(normed), "rows"), (attended, "rows"), (up_w, ""), (up_bias, ""), (down_w, "")],
                [((count, 2 * per_ff + width), BF, "rows"), ((count, 2 * per_ff), F32, "rows")]
                + [((count // 2, D), BF, "half")] * 2,
                core,
                part,
                kept,
            )
        )

    kept = fed((0, 2), ())
    ring_cot.receive()
    ring_cot.send()
    mixed, slope, own_part, other_part = fed((1, 2), kept)
    ring_cot.receive()
    ring_cot.send()
    forward = Scatter(line, own_part, gate(other_part), place)
    ring_cot.receive()
    forward.start()
    grad_att, grad_hidden, all_cot, up_sums = mark(
        *over_arrivals(
            feed_back,
            "feed_back",
            ring_cot.arrived,
            core,
            [(gate(down_w), ""), (slope, "rows")],
            [
                ((count, width), BF, "rows"),
                ((count, 2 * per_ff), BF, "rows"),
                ((count, D), BF, "rows"),
                ((1, 2 * per_ff), F32, ""),
            ],
        )
    )

    def split_pair(field, axis):
        mine = lax.dynamic_index_in_dim(field, x, axis, keepdims=False)
        other = lax.dynamic_index_in_dim(field, 1 - x, axis, keepdims=False).astype(BF)
        return mine, other

    forward.step()
    grad_hidden = fence(grad_hidden, *line.last)
    grad_up_w = mark(dot_of(normed, grad_hidden, 0, 0).astype(BF))
    mine_b, other_b = mark(*split_pair(grad_up_w.reshape(H, 2, half, 2 * per_ff), 1))
    other_b = across_pair(other_b)
    back_in = (query, key, value, grad_att, out_full, logs, tables, starts)
    forward.step()
    grad_qkv = mark(attention_backward(gate(query), *back_in[1:], 0, blocks, ())[0])
    forward.step()
    mine_b, other_b = gate(mine_b, other_b)
    send_b = mark((mine_b.astype(F32) + other_b.astype(F32)).astype(BF))
    got_b = lax.all_to_all(send_b, AXES, 0, 0, tiled=True)
    norm_sums, *back_part = mark(
        *over_tokens(
            project_back,
            "project_back",
            [(gate(grad_qkv), "rows"), (grad_hidden, "rows"), (qkv_w, ""), (up_w, ""), (normed, "rows"), (gain, ""), (shift, "")],
            [((2, D), F32, "")] + [((count // 2, D), BF, "half")] * 2,
            core,
        )
    )
    backward = Scatter(line, *back_part, place)
    backward.start()
    grad_qkv = fence(grad_qkv, *line.last)
    grad_qkv_w = mark(dot_of(normed, grad_qkv, 0, 0).astype(BF))
    mine_a, other_a = mark(*split_pair(grad_qkv_w.reshape(H, 2, half, 3 * width), 1))
    other_a = across_pair(other_a)
    got_b = mark(gate(got_b))
    backward.step()
    cot_sum = jnp.sum(own_cot.astype(F32), axis=0)
    qkv_sums = jnp.sum(gate(grad_qkv).astype(F32), axis=0).reshape(3, 1, width)
    qkv_all = lax.dynamic_update_slice(jnp.zeros((3, pairs, width), F32), qkv_sums, (0, member, 0))
    up_all = lax.dynamic_update_slice(jnp.zeros((pairs, 2 * per_ff), F32), up_sums, (member, 0))
    sums = jnp.concatenate(
        [
            norm_sums.reshape(2, H, per).transpose(1, 0, 2),
            cot_sum.reshape(H, 1, per),
            qkv_all.reshape(H, 3, per),
            up_all.reshape(H, 4, per),
        ],
        axis=1,
    )
    sums = mark(jnp.pad(sums, ((0, 0), (0, half // 2 - sums.shape[1]), (0, width - per))).astype(BF))
    mine_a, other_a = gate(mine_a, other_a)
    sum_a = (mine_a.astype(F32) + other_a.astype(F32)).astype(BF)
    sum_a = sum_a.reshape(H, half, 3, width).transpose(0, 2, 1, 3).reshape(H, 3 * half, width)
    send_a = mark(jnp.concatenate([sum_a, sums], axis=1))
    got_a = lax.all_to_all(send_a, AXES, 0, 0, tiled=True)
    forward_sum = forward.step()
    output = mark((own_in.astype(F32) + (forward_sum + (out_bias + down_bias))).astype(BF))
    output = split_rows(output)
    grad_down = mark(dot_of(fence(mixed, *line.last), all_cot, 0, 0))
    mine_o, other_o = split_pair(grad_down[: 2 * per].reshape(2, per, D), 0)
    mine_d, other_d = split_pair(grad_down[2 * per :].reshape(2, per_ff, D), 0)
    mark(other_o, other_d)
    other_o, other_d = across_pair(other_o), across_pair(other_d)
    backward.step()
    got_a = mark(gate(got_a))
    backward.step()
    grad_up_rows = mark(unpack(gate(got_b), half, 1, 2 * per_ff))
    output = mark(join_rows(*gate(*output)))
    back_sum = backward.step()
    normal, scale = normalize(own_in.astype(F32))
    scaled = back_sum * gain
    grad_in = scale * (
        scaled
        - jnp.mean(scaled, axis=-1, keepdims=True)
        - normal * jnp.mean(scaled * normal, axis=-1, keepdims=True)
    )
    grad_input = mark((own_cot.astype(F32) + grad_in).astype(BF))
    grad_input = split_rows(grad_input)
    mine_o, other_o, mine_d, other_d = gate(mine_o, other_o, mine_d, other_d)
    grad_out_rows = mine_o + other_o.astype(F32)
    grad_down_rows = mine_d + other_d.astype(F32)
    mark(grad_out_rows, grad_down_rows)
    grad_input = mark(join_rows(*gate(*grad_input)))
    grad_qkv_rows = unpack(got_a, half, 3, width)
    sums = jnp.sum(got_a[:, 3 * half : 3 * half + 10, :per].astype(F32), axis=0)
    return (
        output,
        grad_input,
        sums[0],
        sums[1],
        grad_qkv_rows,
        sums[3:6].reshape(-1),
        grad_out_rows,
        sums[2],
        grad_up_rows,
        sums[6:10].reshape(-1),
        grad_down_rows,
        sums[2],
    )


def solution(mesh):
    return jax.shard_map(
        paired_step if suits(mesh) else gathered_step,
        mesh=mesh,
        in_specs=(
            P(None, ("seq", "head"), None),
            P(),
            P(("seq", "head")),
            P(("seq", "head")),
            P(("seq", "head"), None),
            P(("seq", "head")),
            P(("seq", "head"), None),
            P(("seq", "head")),
            P(("seq", "head"), None),
            P(("seq", "head")),
            P(("seq", "head"), None),
            P(("seq", "head")),
            P(None, ("seq", "head"), None),
        ),
        out_specs=(
            P(None, ("seq", "head"), None),
            P(None, ("seq", "head"), None),
            P(("seq", "head")),
            P(("seq", "head")),
            P(("seq", "head"), None),
            P(("seq", "head")),
            P(("seq", "head"), None),
            P(("seq", "head")),
            P(("seq", "head"), None),
            P(("seq", "head")),
            P(("seq", "head"), None),
            P(("seq", "head")),
        ),
        check_vma=False,
    )
```

```python
from functools import partial

import jax
import jax.numpy as jnp
from jax import lax
from jax.experimental import pallas as pl
from jax.experimental.pallas import tpu as pltpu
from jax.sharding import PartitionSpec as P

D = 2048
H = 32
HD = 64
ROT = 32


NEG_FILL = -1e30


def from_behind(block, axis, distance):
    devices = range(lax.axis_size(axis))
    route = [(i - distance, i) for i in devices if i - distance in devices]
    return lax.ppermute(block, axis, route)


def from_behind_2(shard, axis, by):
    length = lax.axis_size(axis)
    return lax.ppermute(shard, axis, [(i, (i + by) % length) for i in range(length)])


def rotate(field, cosine, sine):
    half_rot = ROT // 2
    first_part = field[..., :half_rot]
    second_part = field[..., half_rot:ROT]
    return jnp.concatenate(
        [
            first_part * cosine - second_part * sine,
            second_part * cosine + first_part * sine,
            field[..., ROT:],
        ],
        axis=-1,
    )


def rotation_tables(positions):
    half_rot = ROT // 2
    inverse = jnp.power(10000.0, -2.0 * jnp.arange(half_rot, dtype=jnp.float32) / ROT)
    angles = positions.astype(jnp.float32)[:, None] * inverse[None, :]
    return (jnp.cos(angles)[:, None, :], jnp.sin(angles)[:, None, :])


def layer_norm(values, gain_value, shift_value):
    center = values - jnp.mean(values, axis=-1, keepdims=True)
    spread = jnp.mean(center * center, axis=-1, keepdims=True)
    return center * lax.rsqrt(spread + 1e-05) * gain_value + shift_value


def segment_ids(doc_ends, positions):
    return jnp.sum((doc_ends[:, None, :] <= positions[None, :, None]).astype(jnp.int32), axis=2)


def gelu_tanh(values):
    return jax.nn.gelu(values, approximate=True)


def allowed_pairs(query_pos, query_seg, key_pos, key_seg):
    return (key_pos[None, :] <= query_pos[:, None]) & (key_seg[None, :] == query_seg[:, None])


def masked_scores(query_seq, key_seq, allowed):
    raw_scores = (
        jnp.einsum("qhd,khd->hqk", query_seq, key_seq, preferred_element_type=jnp.float32) * 0.125
    )
    return jnp.where(allowed[None], raw_scores, NEG_FILL)


def forward_step(members, query_pos, key_pos):
    top_val, total_val, accum_val, query_seq, kv_seq, query_seg, key_seg = members
    kv_split = kv_seq.reshape(kv_seq.shape[0], 2, -1, HD)
    allowed = allowed_pairs(query_pos, query_seg, key_pos, key_seg)
    masked = masked_scores(query_seq, kv_split[:, 0], allowed)
    new_top = jnp.maximum(top_val, jnp.max(masked, axis=2))
    weights = jnp.where(allowed[None], jnp.exp(masked - new_top[:, :, None]), 0.0)
    factor = jnp.exp(top_val - new_top)
    new_total = total_val * factor + jnp.sum(weights, axis=2)
    new_accum = accum_val * factor[:, :, None] + jnp.einsum(
        "hqk,khd->hqd",
        weights.astype(jnp.bfloat16),
        kv_split[:, 1],
        preferred_element_type=jnp.float32,
    )
    return (new_top, new_total, new_accum)


def backward_step(members, query_pos, key_pos):
    grad_query, grad_kv, query_seq, kv_seq, grad_att, log_total, row_dot, query_seg, key_seg = (
        members
    )
    key_total = kv_seq.shape[0]
    kv_split = kv_seq.reshape(key_total, 2, -1, HD)
    allowed = allowed_pairs(query_pos, query_seg, key_pos, key_seg)
    masked = masked_scores(query_seq, kv_split[:, 0], allowed)
    prob_full = jnp.where(allowed[None], jnp.exp(masked - log_total[:, :, None]), 0.0)
    grad_value = jnp.einsum(
        "hqk,qhd->khd", prob_full.astype(jnp.bfloat16), grad_att, preferred_element_type=jnp.float32
    )
    grad_probs = jnp.einsum(
        "qhd,khd->hqk", grad_att, kv_split[:, 1], preferred_element_type=jnp.float32
    )
    grad_scores = (prob_full * (grad_probs - row_dot[:, :, None])).astype(jnp.bfloat16)
    grad_query = (
        grad_query
        + jnp.einsum(
            "hqk,khd->hqd", grad_scores, kv_split[:, 0], preferred_element_type=jnp.float32
        )
        * 0.125
    )
    grad_key = (
        jnp.einsum("hqk,qhd->khd", grad_scores, query_seq, preferred_element_type=jnp.float32)
        * 0.125
    )
    grad_kv = grad_kv + jnp.stack([grad_key, grad_value], axis=1).reshape(key_total, 2, -1)
    return (grad_query, grad_kv)


def gathered_step(
    inputs,
    doc_lengths,
    ln_gain,
    ln_bias,
    w_qkv,
    b_qkv,
    w_out,
    b_out,
    w_fc1,
    b_fc1,
    w_fc2,
    b_fc2,
    cotangent,
):
    seq_total = inputs.shape[0]
    row_count = inputs.shape[1]
    head_count = lax.axis_size("head")
    seq_devices = lax.axis_size("seq")
    heads_here = H // head_count
    group_width = heads_here * HD
    block_rows = row_count * head_count
    seq_rank = lax.axis_index("seq")
    head_rank = lax.axis_index("head")
    doc_ends = jnp.cumsum(doc_lengths, axis=1)
    token_pos = (seq_rank * head_count + head_rank) * row_count + jnp.arange(
        row_count, dtype=jnp.int32
    )
    query_start = seq_rank * block_rows
    query_pos = query_start + jnp.arange(block_rows, dtype=jnp.int32)
    query_seg = segment_ids(doc_ends, query_pos)
    gathered = (
        lax.all_gather(ln_gain.astype(jnp.bfloat16), ("seq", "head"), axis=0, tiled=True),
        lax.all_gather(ln_bias.astype(jnp.bfloat16), ("seq", "head"), axis=0, tiled=True),
        lax.all_gather(w_qkv.astype(jnp.bfloat16), ("seq", "head"), axis=0, tiled=True),
        lax.all_gather(b_qkv.astype(jnp.bfloat16), ("seq", "head"), axis=0, tiled=True),
        lax.all_gather(w_out.astype(jnp.bfloat16), ("seq", "head"), axis=0, tiled=True),
        lax.all_gather(b_out.astype(jnp.bfloat16), ("seq", "head"), axis=0, tiled=True),
        lax.all_gather(w_fc1.astype(jnp.bfloat16), ("seq", "head"), axis=0, tiled=True),
        lax.all_gather(b_fc1.astype(jnp.bfloat16), ("seq", "head"), axis=0, tiled=True),
        lax.all_gather(w_fc2.astype(jnp.bfloat16), ("seq", "head"), axis=0, tiled=True),
        lax.all_gather(b_fc2.astype(jnp.bfloat16), ("seq", "head"), axis=0, tiled=True),
    )
    (
        gain_full,
        shift_full,
        qkv_weight,
        qkv_bias,
        out_weight,
        out_bias,
        up_weight,
        up_bias,
        down_weight,
        down_bias,
    ) = gathered
    flat_in = inputs.reshape(seq_total * row_count, D).astype(jnp.float32)
    normed, norm_back = jax.vjp(
        layer_norm, flat_in, gain_full.astype(jnp.float32), shift_full.astype(jnp.float32)
    )
    normed_low = normed.astype(jnp.bfloat16)
    qkv_all = (
        jnp.dot(normed_low, qkv_weight, preferred_element_type=jnp.float32)
        + qkv_bias.astype(jnp.float32)
    ).reshape(seq_total, row_count, 3, H, HD)
    cosine, sine = rotation_tables(token_pos)

    def turn_field(field):
        return rotate(field, cosine, sine)

    query_rot, turn_back = jax.vjp(turn_field, qkv_all[:, :, 0])
    key_rot = turn_field(qkv_all[:, :, 1])
    stacked = (
        jnp.stack([query_rot, key_rot, qkv_all[:, :, 2]], axis=2)
        .reshape(seq_total, row_count, 3, D)
        .astype(jnp.bfloat16)
    )
    by_heads = lax.all_to_all(stacked, "head", split_axis=3, concat_axis=1, tiled=True)
    query_heads = by_heads[:, :, 0].reshape(seq_total, block_rows, heads_here, HD)
    kv_heads = by_heads[:, :, 1:3]
    start_state = (
        jnp.full((seq_total, heads_here, block_rows), NEG_FILL, jnp.float32),
        jnp.zeros((seq_total, heads_here, block_rows), jnp.float32),
        jnp.zeros((seq_total, heads_here, block_rows, HD), jnp.float32),
    )
    shard_piece = lax.all_gather(kv_heads, "seq", axis=1, tiled=True)

    def one_turn(turn_index, current):
        kv_block = lax.dynamic_slice_in_dim(shard_piece, turn_index * block_rows, block_rows, 1)
        key_start = turn_index * block_rows
        key_pos = key_start + jnp.arange(block_rows, dtype=jnp.int32)
        key_seg = segment_ids(doc_ends, key_pos)

        def one_compute(state_in):
            return lax.map(
                partial(forward_step, query_pos=query_pos, key_pos=key_pos),
                (state_in[0], state_in[1], state_in[2], query_heads, kv_block, query_seg, key_seg),
            )

        return lax.cond(
            key_start < query_start + block_rows, one_compute, lambda state_in: state_in, current
        )

    top_all, total_all, accum_all = lax.fori_loop(
        0, shard_piece.shape[1] // block_rows, one_turn, start_state
    )
    attn_full = accum_all / total_all[:, :, :, None]
    log_total = top_all + jnp.log(total_all)
    attn_low = (
        jnp.transpose(attn_full, (0, 2, 1, 3))
        .reshape(seq_total, block_rows, group_width)
        .astype(jnp.bfloat16)
    )
    attended = lax.all_to_all(attn_low, "head", split_axis=1, concat_axis=2, tiled=True).reshape(
        seq_total * row_count, D
    )
    branch = jnp.dot(attended, out_weight, preferred_element_type=jnp.float32) + out_bias.astype(
        jnp.float32
    )
    hidden = jnp.dot(normed_low, up_weight, preferred_element_type=jnp.float32) + up_bias.astype(
        jnp.float32
    )
    active, gelu_back = jax.vjp(gelu_tanh, hidden)
    active_low = active.astype(jnp.bfloat16)
    feed = jnp.dot(active_low, down_weight, preferred_element_type=jnp.float32) + down_bias.astype(
        jnp.float32
    )
    output = (flat_in + branch + feed).astype(jnp.bfloat16).reshape(inputs.shape)
    qkv_weight, out_weight, up_weight, down_weight = (
        lax.all_gather(w_qkv.astype(jnp.bfloat16), ("seq", "head"), axis=0, tiled=True),
        lax.all_gather(w_out.astype(jnp.bfloat16), ("seq", "head"), axis=0, tiled=True),
        lax.all_gather(w_fc1.astype(jnp.bfloat16), ("seq", "head"), axis=0, tiled=True),
        lax.all_gather(w_fc2.astype(jnp.bfloat16), ("seq", "head"), axis=0, tiled=True),
    )
    grad_low = cotangent.reshape(seq_total * row_count, D)
    grad_full = grad_low.astype(jnp.float32)
    cot_sum = jnp.sum(grad_full, axis=0)
    grad_down_w = jnp.einsum("nf,nd->fd", active_low, grad_low, preferred_element_type=jnp.float32)
    grad_active = jnp.einsum("nd,fd->nf", grad_low, down_weight, preferred_element_type=jnp.float32)
    grad_hidden_low = gelu_back(grad_active)[0].astype(jnp.bfloat16)
    grad_up_w = jnp.einsum(
        "nm,nf->mf", normed_low, grad_hidden_low, preferred_element_type=jnp.float32
    )
    grad_up_b = jnp.sum(grad_hidden_low.astype(jnp.float32), axis=0)
    grad_normed = jnp.einsum(
        "nf,mf->nm", grad_hidden_low, up_weight, preferred_element_type=jnp.float32
    )
    grad_out_w = jnp.einsum("nm,nd->md", attended, grad_low, preferred_element_type=jnp.float32)
    grad_att_low = jnp.einsum(
        "nd,md->nm", grad_low, out_weight, preferred_element_type=jnp.float32
    ).astype(jnp.bfloat16)
    grad_heads = lax.all_to_all(
        grad_att_low.reshape(seq_total, row_count, D),
        "head",
        split_axis=2,
        concat_axis=1,
        tiled=True,
    ).reshape(seq_total, block_rows, heads_here, HD)
    row_dot = jnp.sum(
        jnp.transpose(grad_heads.astype(jnp.float32), (0, 2, 1, 3)) * attn_full, axis=3
    )

    def back_turn(turn_index, current):
        grad_query, grad_kv, kv_now = current
        source = (seq_rank - turn_index) % seq_devices
        key_pos = source * block_rows + jnp.arange(block_rows, dtype=jnp.int32)
        key_seg = segment_ids(doc_ends, key_pos)

        def back_compute(grads_in):
            return lax.map(
                partial(backward_step, query_pos=query_pos, key_pos=key_pos),
                (
                    grads_in[0],
                    grads_in[1],
                    query_heads,
                    kv_now,
                    grad_heads,
                    log_total,
                    row_dot,
                    query_seg,
                    key_seg,
                ),
            )

        return lax.cond(
            source <= seq_rank, back_compute, lambda grads_in: grads_in, (grad_query, grad_kv)
        )

    def pass_keys(kv_now):
        return from_behind(kv_now, "seq", 1)

    def pass_grads(grad_kv):
        return from_behind_2(grad_kv.astype(jnp.bfloat16), "seq", 1).astype(grad_kv.dtype)

    def loop_turn(turn_index, current):
        grad_query, grad_kv = back_turn(turn_index, current)
        return (grad_query, pass_grads(grad_kv), pass_keys(current[2]))

    start_grads = (
        jnp.zeros((seq_total, heads_here, block_rows, HD), jnp.float32),
        jnp.zeros((seq_total, block_rows, 2, group_width), jnp.float32),
        kv_heads,
    )
    loop_state = lax.fori_loop(0, seq_devices - 1, loop_turn, start_grads)
    grad_query, grad_kv = back_turn(seq_devices - 1, loop_state)
    grad_kv = pass_grads(grad_kv)
    back_heads = jnp.concatenate(
        [
            jnp.transpose(grad_query, (0, 2, 1, 3)).reshape(seq_total, block_rows, 1, group_width),
            grad_kv,
        ],
        axis=2,
    ).astype(jnp.bfloat16)
    back_tokens = (
        lax.all_to_all(back_heads, "head", split_axis=1, concat_axis=3, tiled=True)
        .astype(jnp.float32)
        .reshape(seq_total, row_count, 3, H, HD)
    )
    grad_qkv_low = (
        jnp.stack(
            [
                turn_back(back_tokens[:, :, 0])[0],
                turn_back(back_tokens[:, :, 1])[0],
                back_tokens[:, :, 2],
            ],
            axis=2,
        )
        .reshape(seq_total * row_count, 3 * D)
        .astype(jnp.bfloat16)
    )
    grad_qkv_w = jnp.einsum(
        "nm,nk->mk", normed_low, grad_qkv_low, preferred_element_type=jnp.float32
    )
    grad_qkv_b = jnp.sum(grad_qkv_low.astype(jnp.float32), axis=0)
    grad_normed = grad_normed + jnp.einsum(
        "nk,mk->nm", grad_qkv_low, qkv_weight, preferred_element_type=jnp.float32
    )
    grad_in, grad_gain, grad_shift = norm_back(grad_normed)
    grad_input = (grad_full + grad_in).astype(jnp.bfloat16).reshape(inputs.shape)
    sums_all = (
        lax.psum_scatter(grad_gain, ("seq", "head"), scatter_dimension=0, tiled=True),
        lax.psum_scatter(grad_shift, ("seq", "head"), scatter_dimension=0, tiled=True),
        lax.psum_scatter(grad_qkv_w, ("seq", "head"), scatter_dimension=0, tiled=True),
        lax.psum_scatter(grad_qkv_b, ("seq", "head"), scatter_dimension=0, tiled=True),
        lax.psum_scatter(grad_out_w, ("seq", "head"), scatter_dimension=0, tiled=True),
        lax.psum_scatter(cot_sum, ("seq", "head"), scatter_dimension=0, tiled=True),
        lax.psum_scatter(grad_up_w, ("seq", "head"), scatter_dimension=0, tiled=True),
        lax.psum_scatter(grad_up_b, ("seq", "head"), scatter_dimension=0, tiled=True),
        lax.psum_scatter(grad_down_w, ("seq", "head"), scatter_dimension=0, tiled=True),
    )
    return (
        output,
        grad_input,
        sums_all[0],
        sums_all[1],
        sums_all[2],
        sums_all[3],
        sums_all[4],
        sums_all[5],
        sums_all[6],
        sums_all[7],
        sums_all[8],
        sums_all[5],
    )


BF = jnp.bfloat16
F32 = jnp.float32
AXES = ("seq", "head")
FF = 8192
BLOCK = 256
KEYS = 512


QUICK = pl.CostEstimate(flops=1 << 20, bytes_accessed=1 << 16, transcendentals=0)


def suits(mesh):
    return mesh.shape["seq"] * mesh.shape["head"] == H and mesh.shape["head"] == 4


def coordinates(rank):
    return rank // 8, (rank // 4) % 2, (rank // 2) % 2, rank % 2


def rank_of(z, core, y, x):
    return ((z * 2 + core) * 2 + y) * 2 + x


def route(step):
    return [(rank, rank_of(*step(*coordinates(rank)))) for rank in range(H)]


def ring_place(z, y, length):
    return z if y == 0 else length - 1 - z


def ring_point(place, length):
    place = place % length
    return (place, 0) if place < length // 2 else (length - 1 - place, 1)


def ring_route(by):
    length = H // 4

    def step(z, core, y, x):
        new_z, new_y = ring_point(ring_place(z, y, length) + by, length)
        return new_z, core, new_y, x

    return route(step)


def across_pair(value):
    return lax.ppermute(value, AXES, route(lambda z, core, y, x: (z, core, y, 1 - x)))


def across_cores(value):
    return lax.ppermute(value, AXES, route(lambda z, core, y, x: (z, 1 - core, y, x)))


def up_ring(value):
    return lax.ppermute(value, AXES, ring_route(1))


def down_ring(value):
    return lax.ppermute(value, AXES, ring_route(-1))


def block_index(place, core):
    length = H // 4
    place = place % length
    z = jnp.where(place < length // 2, place, length - 1 - place)
    y = (place >= length // 2).astype(jnp.int32)
    return (z * 2 + core) * 2 + y


def fence(value, *others):
    anywhere = pl.BlockSpec(memory_space=pl.ANY)
    return pl.pallas_call(
        lambda *refs: None,
        in_specs=[anywhere] * (1 + len(others)),
        out_specs=anywhere,
        out_shape=jax.ShapeDtypeStruct(value.shape, value.dtype),
        input_output_aliases={0: 0},
        cost_estimate=QUICK,
        name="fence",
    )(value, *others)


class Line:
    def __init__(self):
        self.last = ()

    def gate(self, *values):
        values = lax.optimization_barrier((values, self.last))[0] if self.last else values
        return values if len(values) > 1 else values[0]

    def mark(self, *values):
        self.last = values
        return values if len(values) > 1 else values[0]


class Gather:
    def __init__(self, line, own, place, core):
        self.line, self.place, self.core = line, place, core
        self.flying = (own, own)
        self.arrived, self.hop = [], 0
        self.land([(0, own)])

    def land(self, chunks):
        self.arrived += [(self.place + offset, chunk, across_cores(chunk)) for offset, chunk in chunks]
        self.hop = self.hop + 1

    def send(self):
        up, down = self.line.gate(*self.flying)
        if self.hop == H // 8:
            half = up.shape[0] // 2
            up, down = up[:half], down[half:]
        self.flying = up_ring(up), down_ring(down)

    def receive(self):
        hop = self.hop
        before = [other for _, _, other in self.arrived[-2:]]
        up, down, *before = self.line.mark(*self.line.gate(*self.flying, *before))
        for i, other in enumerate(before, len(self.arrived) - len(before)):
            self.arrived[i] = (*self.arrived[i][:2], other)
        if hop == H // 8:
            self.land([(hop, self.line.mark(jnp.concatenate([up, down], axis=0)))])
        else:
            self.flying = up, down
            self.land([(-hop, up), (hop, down)])


class Scatter:
    def __init__(self, line, own, other, place):
        length = H // 4
        self.line, self.place = line, place
        self.rows = own.shape[0] // length
        self.own = own.reshape(length, self.rows, D)
        self.got = across_cores(other).reshape(length, self.rows, D)
        self.hop = length // 2

    def term(self, offset):
        length = H // 4
        at = (self.place + offset) % length
        index = jnp.where(at < length // 2, 2 * at, 2 * (length - 1 - at) + 1)
        mine = lax.dynamic_index_in_dim(self.own, index, 0, keepdims=False)
        theirs = lax.dynamic_index_in_dim(self.got, index, 0, keepdims=False)
        return mine.astype(F32) + theirs.astype(F32)

    def start(self):
        self.got = self.line.gate(self.got)
        far = self.line.mark(self.term(self.hop).astype(BF))
        half = self.rows // 2
        self.flying = up_ring(far[:half]), down_ring(far[half:])

    def step(self):
        up, down = (part.astype(F32) for part in self.line.gate(*self.flying))
        if self.hop == H // 8:
            pad = jnp.zeros((self.rows // 2, D), F32)
            up, down = jnp.concatenate([up, pad], axis=0), jnp.concatenate([pad, down], axis=0)
        self.hop -= 1
        if not self.hop:
            return self.term(0) + up + down
        up = (up + self.term(self.hop)).astype(BF)
        down = (down + self.term(-self.hop)).astype(BF)
        self.line.mark(up, down)
        self.flying = up_ring(up), down_ring(down)


class Scatter:
    def __init__(self, line, own, other, place):
        length = H // 4
        self.line, self.place = line, place
        self.rows = own.shape[0] // length
        self.own = own.reshape(length, self.rows, D)
        self.got = across_cores(other).reshape(length, self.rows, D)
        self.hop = length // 2

    def term(self, offset):
        length = H // 4
        at = (self.place + offset) % length
        index = jnp.where(at < length // 2, 2 * at, 2 * (length - 1 - at) + 1)
        mine = lax.dynamic_index_in_dim(self.own, index, 0, keepdims=False)
        theirs = lax.dynamic_index_in_dim(self.got, index, 0, keepdims=False)
        return mine.astype(F32) + theirs.astype(F32)

    def start(self):
        self.got = self.line.gate(self.got)
        far = self.line.mark(self.term(self.hop).astype(BF))
        half = self.rows // 2
        self.flying = up_ring(far[:half]), down_ring(far[half:])

    def step(self):
        up, down = (part.astype(F32) for part in self.line.gate(*self.flying))
        if self.hop == H // 8:
            pad = jnp.zeros((self.rows // 2, D), F32)
            up, down = jnp.concatenate([up, pad], axis=0), jnp.concatenate([pad, down], axis=0)
        self.hop -= 1
        if not self.hop:
            return self.term(0) + up + down
        up = (up + self.term(self.hop)).astype(BF)
        down = (down + self.term(-self.hop)).astype(BF)
        self.line.mark(up, down)
        self.flying = up_ring(up), down_ring(down)


def settle(wholes, kept, chunks, vectors):
    rows, width = chunks[0][1].shape
    many, layers = len(chunks), 2 if vectors else 1

    def kernel(index_ref, *refs):
        blocks, rest = refs[:many], refs[many + (layers if kept else 0) :]
        outs = rest[len(vectors) : len(vectors) + layers]
        hold = rest[-1] if vectors else outs[0]
        for i, block in enumerate(blocks):

            @pl.when(pl.program_id(0) == i)
            def _(block=block):
                hold[...] = block[...]

        if vectors:
            values = hold[...].astype(F32)
            center = values - jnp.mean(values, axis=1, keepdims=True)
            scale = lax.rsqrt(jnp.mean(center * center, axis=1, keepdims=True) + 1e-05)
            normal = center * scale
            outs[0][...] = (normal * rest[0][...] + rest[1][...]).astype(BF)
            outs[1][...] = normal.astype(BF)

    whole = jax.ShapeDtypeStruct((wholes, width), BF)
    fixed = pl.BlockSpec((rows, width), lambda i, index: (0, 0))
    return pl.pallas_call(
        kernel,
        grid_spec=pltpu.PrefetchScalarGridSpec(
            num_scalar_prefetch=1,
            grid=(many,),
            in_specs=[fixed] * many
            + [pl.BlockSpec(memory_space=pl.ANY)] * (layers if kept else 0)
            + [pl.BlockSpec((1, width), lambda i, index: (0, 0))] * len(vectors),
            out_specs=[pl.BlockSpec((rows, width), lambda i, index: (index[i], 0))] * layers,
            scratch_shapes=[pltpu.VMEM((rows, width), BF)] if vectors else [],
        ),
        out_shape=[whole] * layers,
        input_output_aliases={1 + many + i: i for i in range(layers)} if kept else {},
        cost_estimate=QUICK,
        name="settle",
    )(jnp.stack([index for index, _ in chunks]), *[c for _, c in chunks], *(kept or ()), *vectors)


def turn(field, tables, sign):
    half_rot = ROT // 2
    first = pltpu.roll(field, 2 * HD - half_rot, 1)
    second = pltpu.roll(field, half_rot, 1)
    return field * tables[0] + sign * (second * tables[2] - first * tables[1])


def turn_tables(positions):
    half_rot = ROT // 2
    lane = jnp.arange(2 * HD, dtype=jnp.int32) % HD
    inverse = jnp.power(10000.0, -2.0 * (lane % half_rot).astype(F32) / ROT)
    angles = positions.astype(F32)[:, None] * inverse[None, :]
    sine = jnp.sin(angles)
    return jnp.stack(
        [
            jnp.where(lane < ROT, jnp.cos(angles), 1.0),
            jnp.where(lane < half_rot, sine, 0.0),
            jnp.where((lane >= half_rot) & (lane < ROT), sine, 0.0),
        ]
    )


def head_lanes(value, head):
    lane = lax.broadcasted_iota(jnp.int32, value.shape, 1)
    return jnp.where((lane >= HD) if head else (lane < HD), value, jnp.zeros_like(value))


def dot_of(left, right, left_dim, right_dim):
    return lax.dot_general(
        left, right, (((left_dim,), (right_dim,)), ((), ())), preferred_element_type=F32
    )


def project(values, gain_ref, shift_ref, w_ref, bias_ref, tables_ref, normed_ref, q_ref, k_ref, v_ref):
    values = values.astype(F32)
    center = values - jnp.mean(values, axis=1, keepdims=True)
    scale = lax.rsqrt(jnp.mean(center * center, axis=1, keepdims=True) + 1e-05)
    normed = (center * scale * gain_ref[...] + shift_ref[...]).astype(BF)
    normed_ref[...] = normed.reshape(normed_ref.shape)
    width = 2 * HD
    raw = dot_of(normed, w_ref[...], 1, 0) + bias_ref[...]
    tables = tables_ref[...].reshape(3, BLOCK, width)
    q_ref[...] = turn(raw[:, :width], tables, 1.0).astype(BF).reshape(q_ref.shape)
    k_ref[...] = turn(raw[:, width : 2 * width], tables, 1.0).astype(BF).reshape(k_ref.shape)
    v_ref[...] = raw[:, 2 * width :].astype(BF).reshape(v_ref.shape)


def feed(core_ref, normed_ref, att_ref, up_ref, bias_ref, down_ref, mixed_ref, slope_ref, *part_refs):
    root, cubic = 0.7978845608028654, 0.044715
    for side, part_ref in enumerate(part_refs):
        here = pl.ds(pl.multiple_of(BLOCK * ((core_ref[0] + side) % 2), BLOCK), BLOCK)
        hidden = dot_of(normed_ref[here, :], up_ref[...], 1, 0) + bias_ref[...]
        square = hidden * hidden
        bend = jnp.tanh(root * (hidden + cubic * (square * hidden)))
        active = (0.5 * hidden * (1.0 + bend)).astype(BF)
        mixed_ref[here, : 2 * HD] = att_ref[here, :]
        mixed_ref[here, 2 * HD :] = active
        slope_ref[here, :] = 0.5 * (1.0 + bend) + 0.5 * hidden * (1.0 - bend * bend) * (
            root * (1.0 + 3.0 * cubic * square)
        )
        part = dot_of(att_ref[here, :], down_ref[: 2 * HD, :], 1, 0)
        part = part + dot_of(active, down_ref[2 * HD :, :], 1, 0)
        part_ref[...] = part.astype(BF)


def feed_back(cot, down_ref, slope_ref, att_ref, hidden_ref, whole_ref, sum_ref):
    whole_ref[...] = cot.reshape(whole_ref.shape)
    mixed = dot_of(cot, down_ref[...], 1, 1)
    att_ref[...] = mixed[:, : 2 * HD].astype(BF).reshape(att_ref.shape)
    slope = slope_ref[...].reshape(BLOCK, slope_ref.shape[-1])
    hidden = (mixed[:, 2 * HD :] * slope).astype(BF)
    hidden_ref[...] = hidden.reshape(hidden_ref.shape)

    @pl.when(pl.program_id(0) == 0)
    def _():
        sum_ref[...] = jnp.zeros_like(sum_ref)

    sum_ref[...] += jnp.sum(hidden.astype(F32), axis=0, keepdims=True)


def project_back(core_ref, qkv_ref, hidden_ref, wq_ref, up_ref, normed_ref, gain_ref, shift_ref, sum_ref, *part_refs):
    @pl.when(pl.program_id(0) == 0)
    def _():
        sum_ref[...] = jnp.zeros_like(sum_ref)

    step = D // 4
    for side, part_ref in enumerate(part_refs):
        here = pl.ds(pl.multiple_of(BLOCK * ((core_ref[0] + side) % 2), BLOCK), BLOCK)
        qkv, hidden = qkv_ref[here, :], hidden_ref[here, :]
        for first in range(0, D, step):
            some = pl.ds(first, step)
            part = dot_of(qkv, wq_ref[some, :], 1, 1) + dot_of(hidden, up_ref[some, :], 1, 1)
            part_ref[:, some] = part.astype(BF)
            normal = (normed_ref[here, some].astype(F32) - shift_ref[:, some]) / gain_ref[:, some]
            sum_ref[0:1, some] += jnp.sum(part * normal, axis=0, keepdims=True)
            sum_ref[1:2, some] += jnp.sum(part, axis=0, keepdims=True)


def over_arrivals(kernel, name, arrived, core, ins, outs):
    length = H // 4
    rows, lanes = arrived[0][1].shape
    places = jnp.stack([place for place, _, _ in arrived]) % length
    y = (places >= length // 2).astype(jnp.int32)
    z = jnp.where(y == 0, places, length - 1 - places)
    lead = (length // 2, 2, 2, rows)

    def body(core_ref, z_ref, y_ref, *refs):
        blocks, rest, hold = refs[: 2 * length], refs[2 * length : -1], refs[-1]
        for step in range(length):

            @pl.when(pl.program_id(0) == step)
            def _(step=step):
                for side in range(2):
                    first = pl.multiple_of(rows * ((core_ref[0] + side) % 2), rows)
                    hold[pl.ds(first, rows), :] = blocks[2 * step + side][...]

        kernel(hold[...], *rest)

    def view(array, how):
        if how == "rows":
            return array.reshape(lead + array.shape[1:])
        return array.reshape(array.shape[:1] + lead + array.shape[2:]) if how == "tables" else array

    def spec(shape, how):
        if how == "rows":
            return pl.BlockSpec((1, 2, 1, rows, shape[-1]), lambda i, c, z, y: (z[i], 0, y[i], 0, 0))
        if how == "tables":
            return pl.BlockSpec(
                (shape[0], 1, 2, 1, rows, shape[-1]), lambda i, c, z, y: (0, z[i], 0, y[i], 0, 0)
            )
        return pl.BlockSpec(shape, lambda i, *_: (0, 0))

    once = pl.BlockSpec((rows, lanes), lambda i, *_: (0, 0), pipeline_mode=pl.Buffered(1))
    results = pl.pallas_call(
        body,
        grid_spec=pltpu.PrefetchScalarGridSpec(
            num_scalar_prefetch=3,
            grid=(length,),
            in_specs=[once] * (2 * length) + [spec(a.shape, how) for a, how in ins],
            out_specs=[spec(shape, how) for shape, _, how in outs],
            scratch_shapes=[pltpu.VMEM((2 * rows, lanes), BF)],
        ),
        out_shape=[
            jax.ShapeDtypeStruct(lead + shape[1:] if how == "rows" else shape, kind)
            for shape, kind, how in outs
        ],
        cost_estimate=QUICK,
        name=name,
    )(
        jnp.reshape(core, (1,)),
        z,
        y,
        *[block for _, mine, other in arrived for block in (mine, other)],
        *[view(a, how) for a, how in ins],
    )
    return [result.reshape(shape) for result, (shape, _, _) in zip(results, outs)]


def over_tokens(kernel, name, ins, outs, core, part=(0, 1), kept=()):
    count = ins[0][0].shape[0]
    size = 2 * BLOCK
    steps = count // size // part[1]
    first = part[0] * steps

    def spec(shape, how):
        if how in ("rows", "half"):
            rows = size if how == "rows" else size // 2
            return pl.BlockSpec((rows,) + shape[1:], lambda i, *_: (i + first, 0))
        return pl.BlockSpec(shape, lambda i, *_: (0, 0))

    def body(core_ref, *refs):
        kernel(core_ref, *refs[: len(ins)], *refs[len(ins) + len(kept) :])

    return pl.pallas_call(
        body,
        grid_spec=pltpu.PrefetchScalarGridSpec(
            num_scalar_prefetch=1,
            grid=(steps,),
            in_specs=[spec(a.shape, how) for a, how in ins]
            + [pl.BlockSpec(memory_space=pl.ANY)] * len(kept),
            out_specs=[spec(shape, how) for shape, _, how in outs],
        ),
        out_shape=[jax.ShapeDtypeStruct(shape, kind) for shape, kind, _ in outs],
        input_output_aliases={1 + len(ins) + i: i for i in range(len(kept))},
        cost_estimate=QUICK,
        name=name,
    )(jnp.reshape(core, (1,)), *[a for a, _ in ins], *kept)


def key_chunk(index):
    return pl.ds(pl.multiple_of(index * KEYS, KEYS), KEYS)


def allowed_keys(starts, chunk, block):
    keys = chunk * KEYS + lax.broadcasted_iota(jnp.int32, (KEYS, BLOCK), 0)
    queries = block * BLOCK + lax.broadcasted_iota(jnp.int32, (1, BLOCK), 1)
    return (keys >= starts) & (keys <= queries)


def fold(value, how):
    return how(value.reshape(KEYS // 8, 8, BLOCK), axis=0)


def attend_forward(first_block, kept, q_ref, k_ref, v_ref, starts_ref, *refs):
    o_ref, low_ref, lse_ref, scores_ref, acc_ref, row_ref = refs[kept:]
    block = first_block + pl.program_id(0)
    query = q_ref[...] * 0.125
    queries = [head_lanes(query, head) for head in range(2)]
    starts = starts_ref[...]
    chunks = ((block + 1) * BLOCK + KEYS - 1) // KEYS
    row_ref[...] = jnp.full_like(row_ref, NEG_FILL)

    def score(chunk, carry):
        here = key_chunk(chunk)
        keys = k_ref[here, :]
        allowed = allowed_keys(starts, chunk, block)
        for head in range(2):
            scores = jnp.where(allowed, dot_of(keys, queries[head], 1, 1), NEG_FILL)
            scores_ref[head, here, :] = scores
            row_ref[head] = jnp.maximum(row_ref[head], fold(scores, jnp.max))
        return carry

    lax.fori_loop(0, chunks, score, 0)
    tops = [jnp.max(row_ref[head], axis=0, keepdims=True) for head in range(2)]
    acc_ref[...] = jnp.zeros_like(acc_ref)
    row_ref[...] = jnp.zeros_like(row_ref)

    def mix(chunk, carry):
        here = key_chunk(chunk)
        values = v_ref[here, :]
        for head in range(2):
            weights = jnp.exp(scores_ref[head, here, :] - tops[head])
            row_ref[head] += fold(weights, jnp.sum)
            acc_ref[head] += dot_of(values, weights.astype(BF), 0, 0)
        return carry

    lax.fori_loop(0, chunks, mix, 0)
    totals = [jnp.sum(row_ref[head], axis=0, keepdims=True) for head in range(2)]
    row = lax.broadcasted_iota(jnp.int32, acc_ref.shape[1:], 0)
    out = jnp.where(row < HD, acc_ref[0] / totals[0], acc_ref[1] / totals[1]).T
    o_ref[...] = out
    low_ref[...] = out.astype(BF)
    lse_ref[...] = jnp.concatenate([tops[i] + jnp.log(totals[i]) for i in range(2)], axis=0)


def attend_backward(last_block, kept, q_ref, k_ref, v_ref, g_ref, o_ref, lse_ref, tables_ref, starts_ref, *refs):
    before, (out_ref, gk_ref, gv_ref, gq_ref) = refs[:kept], refs[kept:]
    step = pl.program_id(0)
    block = last_block - step
    width = 2 * HD

    @pl.when(step == 0)
    def _():
        gk_ref[...] = before[1][...] if kept else jnp.zeros_like(gk_ref)
        gv_ref[...] = before[2][...] if kept else jnp.zeros_like(gv_ref)

    gq_ref[...] = jnp.zeros_like(gq_ref)
    query, grad = q_ref[...] * 0.125, g_ref[...]
    product = (grad.astype(F32) * o_ref[...]).T
    dots = [jnp.sum(product[i * HD : (i + 1) * HD], axis=0, keepdims=True) for i in range(2)]
    queries = [head_lanes(query, head) for head in range(2)]
    grads = [head_lanes(grad, head) for head in range(2)]
    logs = [lse_ref[head : head + 1, :] for head in range(2)]
    starts = starts_ref[...]

    def work(chunk, carry):
        here = key_chunk(chunk)
        keys, values = k_ref[here, :], v_ref[here, :]
        allowed = allowed_keys(starts, chunk, block)
        for head in range(2):
            scores = dot_of(keys, queries[head], 1, 1)
            probs = jnp.where(allowed, jnp.exp(scores - logs[head]), 0.0)
            grad_probs = dot_of(values, grads[head], 1, 1)
            grad_scores = (probs * (grad_probs - dots[head])).astype(BF)
            gv_ref[here, :] += dot_of(probs.astype(BF), grads[head], 1, 0)
            gk_ref[here, :] += dot_of(grad_scores, queries[head], 1, 0)
            gq_ref[...] += dot_of(head_lanes(keys, head), grad_scores, 0, 0)
        return carry

    lax.fori_loop(0, ((block + 1) * BLOCK + KEYS - 1) // KEYS, work, 0)
    tables = tables_ref[...]
    here = pl.ds(pl.multiple_of(block * BLOCK, BLOCK), BLOCK)

    def back(value):
        return turn(value.astype(BF).astype(F32), tables, -1.0).astype(BF)

    out_ref[:, :width] = back(gq_ref[...].T * 0.125)
    out_ref[:, width : 2 * width] = back(gk_ref[here, :])
    out_ref[:, 2 * width :] = gv_ref[here, :].astype(BF)


def attention_forward(query, key, value, starts, first, last, kept):
    count = query.shape[0]
    width = 2 * HD
    rows = lambda i: (i + first, 0)
    block = pl.BlockSpec((BLOCK, width), rows)
    row = lambda many: pl.BlockSpec((many, BLOCK), lambda i: (0, i + first))
    full = pl.BlockSpec((count, width), lambda i: (0, 0))
    return pl.pallas_call(
        partial(attend_forward, first, len(kept)),
        grid=(last - first,),
        in_specs=[block, full, full, row(1)] + [pl.BlockSpec(memory_space=pl.ANY)] * len(kept),
        out_specs=[block] * 2 + [row(2)],
        out_shape=[
            jax.ShapeDtypeStruct((count, width), F32),
            jax.ShapeDtypeStruct((count, width), BF),
            jax.ShapeDtypeStruct((2, count), F32),
        ],
        scratch_shapes=[
            pltpu.VMEM((2, count, BLOCK), F32),
            pltpu.VMEM((2, width, BLOCK), F32),
            pltpu.VMEM((2, 8, BLOCK), F32),
        ],
        input_output_aliases={4 + i: i for i in range(len(kept))},
        cost_estimate=QUICK,
        name="attend_forward",
    )(query, key, value, starts, *kept)


def attention_backward(query, key, value, grad, out, logs, tables, starts, first, last, kept):
    count = query.shape[0]
    width = 2 * HD
    rows = lambda i: (last - 1 - i, 0)
    block = pl.BlockSpec((BLOCK, width), rows)
    full = pl.BlockSpec((count, width), lambda i: (0, 0))
    row = lambda many: pl.BlockSpec((many, BLOCK), lambda i: (0, last - 1 - i))
    return pl.pallas_call(
        partial(attend_backward, last - 1, len(kept)),
        grid=(last - first,),
        in_specs=[
            block,
            full,
            full,
            block,
            block,
            row(2),
            pl.BlockSpec((3, BLOCK, width), lambda i: (0, last - 1 - i, 0)),
            row(1),
        ]
        + [pl.BlockSpec(memory_space=pl.ANY), full, full][: len(kept)],
        out_specs=[pl.BlockSpec((BLOCK, 3 * width), rows), full, full],
        out_shape=[
            jax.ShapeDtypeStruct((count, 3 * width), BF),
            jax.ShapeDtypeStruct((count, width), F32),
            jax.ShapeDtypeStruct((count, width), F32),
        ],
        scratch_shapes=[pltpu.VMEM((width, BLOCK), F32)],
        input_output_aliases={8: 0} if kept else {},
        cost_estimate=QUICK,
        name="attend_backward",
    )(query, key, value, grad, out, logs, tables, starts, *kept)


def unpack(rows, half, parts, columns):
    many = rows.shape[0]

    def kernel(rows_ref, out_ref):
        for device in range(many):
            side = slice((device % 2) * half, (device % 2 + 1) * half)
            for part in range(parts):
                first = (part * (many // 2) + device // 2) * columns
                out_ref[side, first : first + columns] = rows_ref[
                    device, part * half : (part + 1) * half, :
                ].astype(F32)

    return pl.pallas_call(
        kernel,
        out_shape=jax.ShapeDtypeStruct((2 * half, parts * columns * many // 2), F32),
        cost_estimate=QUICK,
        name="unpack",
    )(rows)


def normalize(values):
    center = values - jnp.mean(values, axis=-1, keepdims=True)
    scale = lax.rsqrt(jnp.mean(center * center, axis=-1, keepdims=True) + 1e-05)
    return center * scale, scale


def paired_step(
    inputs,
    doc_lengths,
    ln_gain,
    ln_bias,
    w_qkv,
    b_qkv,
    w_out,
    b_out,
    w_fc1,
    b_fc1,
    w_fc2,
    b_fc2,
    cotangent,
):
    rows = inputs.shape[1]
    count = rows * H
    rank = lax.axis_index("seq") * 4 + lax.axis_index("head")
    x = rank % 2
    y, core, z = (rank // 2) % 2, (rank // 4) % 2, rank // 8
    length = H // 4
    place = jnp.where(y == 0, z, length - 1 - z)

    def split_rows(field):
        mine = lax.dynamic_slice_in_dim(field, x * rows, rows, 0)
        return mine, across_pair(lax.dynamic_slice_in_dim(field, (1 - x) * rows, rows, 0))

    def join_rows(mine, got):
        return jnp.where(x == 0, jnp.stack([mine, got]), jnp.stack([got, mine]))

    per = D // H
    per_ff = FF // H
    pairs = H // 2
    width = 2 * HD
    half = per // 2

    line = Line()
    gate, mark = line.gate, line.mark

    def pair_blocks(field):
        mine = lax.dynamic_index_in_dim(field, x, 0, keepdims=False)
        return mine, lax.dynamic_index_in_dim(field, 1 - x, 0, keepdims=False)

    def pair_rows(mine, got):
        return jnp.where(x == 0, jnp.concatenate([mine, got]), jnp.concatenate([got, mine]))

    mine_in, other_in = mark(*pair_blocks(inputs))
    got_in = across_pair(other_in)
    small = jnp.concatenate([ln_gain, ln_bias, b_out, b_fc2, b_qkv, b_fc1]).astype(BF).reshape(-1, per)
    small = jnp.pad(small, ((0, half // 2 - small.shape[0]), (0, width - per)))
    send_a = jnp.concatenate(
        [
            gate(w_qkv).astype(BF).reshape(2, half, 3, pairs, width).transpose(3, 0, 2, 1, 4).reshape(H, 3 * half, width),
            jnp.broadcast_to(small[None], (H, half // 2, width)),
        ],
        axis=1,
    )
    own_in = mark(pair_rows(mine_in, got_in))
    send_a = mark(gate(send_a))
    got_a = lax.all_to_all(send_a, AXES, 0, 0, tiled=True)
    mine_cot, other_cot = pair_blocks(gate(cotangent))
    mine_d = jnp.concatenate([gate(w_out), w_fc2], axis=0).astype(BF)
    mark(other_cot, mine_d)
    got_cot = across_pair(other_cot)
    pair_d = across_pair(mine_d)
    send_b = mark(
        gate(w_fc1)
        .astype(BF)
        .reshape(2, half, pairs, 2 * per_ff)
        .transpose(2, 0, 1, 3)
        .reshape(H, half, 2 * per_ff)
    )
    positions = gate(jnp.arange(count, dtype=jnp.int32))
    doc_ends = jnp.cumsum(lax.dynamic_index_in_dim(doc_lengths, x, 0, keepdims=False))
    starts = jnp.max(
        jnp.where(doc_ends[:, None] <= positions[None, :], doc_ends[:, None], 0), axis=0
    )[None, :]
    starts, tables = mark(*lax.optimization_barrier((starts, turn_tables(positions))))
    ring_in = Gather(line, gate(own_in), place, core)
    ring_in.send()
    ring_in.receive()
    ring_in.send()
    mine_d, pair_d = gate(mine_d, pair_d)
    low_d, high_d = jnp.where(x == 0, mine_d, pair_d), jnp.where(x == 0, pair_d, mine_d)
    down_w = mark(
        jnp.concatenate([low_d[:per], high_d[:per], low_d[per:], high_d[per:]], axis=0)
    )
    got_a = gate(got_a)
    part_a = got_a[:, : 3 * half]
    small = got_a[:, 3 * half :, :per].astype(F32)
    gain, shift, out_bias, down_bias = [small[:, i].reshape(1, D) for i in range(4)]
    member = rank // 2
    qkv_bias = small[:, 4:7].reshape(3, pairs, width)
    qkv_bias = lax.dynamic_index_in_dim(qkv_bias, member, 1, keepdims=False).reshape(1, 3 * width)
    up_bias = small[:, 7:11].reshape(pairs, 2 * per_ff)
    up_bias = lax.dynamic_index_in_dim(up_bias, member, 0)
    small = (gain, shift, qkv_bias, up_bias, out_bias, down_bias)
    part_a, *small = mark(*lax.optimization_barrier((part_a, *small)))
    gain, shift, qkv_bias, up_bias, out_bias, down_bias = small
    pair_a = across_pair(part_a)

    def join(mine, got):
        low, high = jnp.where(x == 0, mine, got), jnp.where(x == 0, got, mine)
        return jnp.stack([low, high], axis=1)

    own_cot = mark(pair_rows(*gate(mine_cot, got_cot)))
    ring_in.receive()
    ring_in.send()
    ring_in.receive()
    qkv_w = join(*gate(part_a, pair_a)).reshape(H, 2, 3, half, width)
    qkv_w = mark(qkv_w.transpose(0, 1, 3, 2, 4).reshape(D, 3 * width))
    ring_in.send()
    ring_in.receive()
    send_b = gate(send_b)
    got_b = lax.all_to_all(send_b, AXES, 0, 0, tiled=True)
    normed, query, key, value = mark(
        *over_arrivals(
            project,
            "project",
            ring_in.arrived,
            core,
            [(gate(gain), ""), (shift, ""), (qkv_w, ""), (qkv_bias, ""), (tables, "tables")],
            [((count, D), BF, "rows")] + [((count, width), BF, "rows")] * 3,
        )
    )
    blocks = count // BLOCK
    got_b = mark(gate(got_b))
    pair_b = across_pair(got_b)
    ring_cot = Gather(line, gate(own_cot), place, core)
    ring_cot.send()
    out_full, attended, logs = mark(
        *attention_forward(gate(query), key, value, starts, 0, blocks, ())
    )
    ring_cot.receive()
    ring_cot.send()
    up_w = mark(join(*gate(got_b, pair_b)).reshape(D, 2 * per_ff))

    def fed(part, kept):
        return mark(
            *over_tokens(
                feed,
                "feed",
                [(gate(normed), "rows"), (attended, "rows"), (up_w, ""), (up_bias, ""), (down_w, "")],
                [((count, 2 * per_ff + width), BF, "rows"), ((count, 2 * per_ff), F32, "rows")]
                + [((count // 2, D), BF, "half")] * 2,
                core,
                part,
                kept,
            )
        )

    kept = fed((0, 2), ())
    ring_cot.receive()
    ring_cot.send()
    mixed, slope, own_part, other_part = fed((1, 2), kept)
    ring_cot.receive()
    ring_cot.send()
    forward = Scatter(line, own_part, gate(other_part), place)
    ring_cot.receive()
    forward.start()
    grad_att, grad_hidden, all_cot, up_sums = mark(
        *over_arrivals(
            feed_back,
            "feed_back",
            ring_cot.arrived,
            core,
            [(gate(down_w), ""), (slope, "rows")],
            [
                ((count, width), BF, "rows"),
                ((count, 2 * per_ff), BF, "rows"),
                ((count, D), BF, "rows"),
                ((1, 2 * per_ff), F32, ""),
            ],
        )
    )

    def split_pair(field, axis):
        mine = lax.dynamic_index_in_dim(field, x, axis, keepdims=False)
        other = lax.dynamic_index_in_dim(field, 1 - x, axis, keepdims=False).astype(BF)
        return mine, other

    forward.step()
    grad_hidden = fence(grad_hidden, *line.last)
    grad_up_w = mark(dot_of(normed, grad_hidden, 0, 0).astype(BF))
    mine_b, other_b = mark(*split_pair(grad_up_w.reshape(H, 2, half, 2 * per_ff), 1))
    other_b = across_pair(other_b)
    back_in = (query, key, value, grad_att, out_full, logs, tables, starts)
    forward.step()
    grad_qkv = mark(attention_backward(gate(query), *back_in[1:], 0, blocks, ())[0])
    forward.step()
    mine_b, other_b = gate(mine_b, other_b)
    send_b = mark((mine_b.astype(F32) + other_b.astype(F32)).astype(BF))
    got_b = lax.all_to_all(send_b, AXES, 0, 0, tiled=True)
    norm_sums, *back_part = mark(
        *over_tokens(
            project_back,
            "project_back",
            [(gate(grad_qkv), "rows"), (grad_hidden, "rows"), (qkv_w, ""), (up_w, ""), (normed, "rows"), (gain, ""), (shift, "")],
            [((2, D), F32, "")] + [((count // 2, D), BF, "half")] * 2,
            core,
        )
    )
    backward = Scatter(line, *back_part, place)
    backward.start()
    grad_qkv = fence(grad_qkv, *line.last)
    grad_qkv_w = mark(dot_of(normed, grad_qkv, 0, 0).astype(BF))
    mine_a, other_a = mark(*split_pair(grad_qkv_w.reshape(H, 2, half, 3 * width), 1))
    other_a = across_pair(other_a)
    got_b = mark(gate(got_b))
    backward.step()
    cot_sum = jnp.sum(own_cot.astype(F32), axis=0)
    qkv_sums = jnp.sum(gate(grad_qkv).astype(F32), axis=0).reshape(3, 1, width)
    qkv_all = lax.dynamic_update_slice(jnp.zeros((3, pairs, width), F32), qkv_sums, (0, member, 0))
    up_all = lax.dynamic_update_slice(jnp.zeros((pairs, 2 * per_ff), F32), up_sums, (member, 0))
    sums = jnp.concatenate(
        [
            norm_sums.reshape(2, H, per).transpose(1, 0, 2),
            cot_sum.reshape(H, 1, per),
            qkv_all.reshape(H, 3, per),
            up_all.reshape(H, 4, per),
        ],
        axis=1,
    )
    sums = mark(jnp.pad(sums, ((0, 0), (0, half // 2 - sums.shape[1]), (0, width - per))).astype(BF))
    mine_a, other_a = gate(mine_a, other_a)
    sum_a = (mine_a.astype(F32) + other_a.astype(F32)).astype(BF)
    sum_a = sum_a.reshape(H, half, 3, width).transpose(0, 2, 1, 3).reshape(H, 3 * half, width)
    send_a = mark(jnp.concatenate([sum_a, sums], axis=1))
    got_a = lax.all_to_all(send_a, AXES, 0, 0, tiled=True)
    forward_sum = forward.step()
    output = mark((own_in.astype(F32) + (forward_sum + (out_bias + down_bias))).astype(BF))
    output = split_rows(output)
    grad_down = mark(dot_of(fence(mixed, *line.last), all_cot, 0, 0))
    mine_o, other_o = split_pair(grad_down[: 2 * per].reshape(2, per, D), 0)
    mine_d, other_d = split_pair(grad_down[2 * per :].reshape(2, per_ff, D), 0)
    mark(other_o, other_d)
    other_o, other_d = across_pair(other_o), across_pair(other_d)
    backward.step()
    backward.step()
    got_a = mark(gate(got_a))
    grad_up_rows = mark(unpack(gate(got_b), half, 1, 2 * per_ff))
    output = mark(join_rows(*gate(*output)))
    back_sum = backward.step()
    normal, scale = normalize(own_in.astype(F32))
    scaled = back_sum * gain
    grad_in = scale * (
        scaled
        - jnp.mean(scaled, axis=-1, keepdims=True)
        - normal * jnp.mean(scaled * normal, axis=-1, keepdims=True)
    )
    grad_input = mark((own_cot.astype(F32) + grad_in).astype(BF))
    grad_input = split_rows(grad_input)
    mine_o, other_o, mine_d, other_d = gate(mine_o, other_o, mine_d, other_d)
    grad_out_rows = mine_o + other_o.astype(F32)
    grad_down_rows = mine_d + other_d.astype(F32)
    mark(grad_out_rows, grad_down_rows)
    grad_input = mark(join_rows(*gate(*grad_input)))
    grad_qkv_rows = unpack(got_a, half, 3, width)
    sums = jnp.sum(got_a[:, 3 * half : 3 * half + 10, :per].astype(F32), axis=0)
    return (
        output,
        grad_input,
        sums[0],
        sums[1],
        grad_qkv_rows,
        sums[3:6].reshape(-1),
        grad_out_rows,
        sums[2],
        grad_up_rows,
        sums[6:10].reshape(-1),
        grad_down_rows,
        sums[2],
    )


def solution(mesh):
    return jax.shard_map(
        paired_step if suits(mesh) else gathered_step,
        mesh=mesh,
        in_specs=(
            P(None, ("seq", "head"), None),
            P(),
            P(("seq", "head")),
            P(("seq", "head")),
            P(("seq", "head"), None),
            P(("seq", "head")),
            P(("seq", "head"), None),
            P(("seq", "head")),
            P(("seq", "head"), None),
            P(("seq", "head")),
            P(("seq", "head"), None),
            P(("seq", "head")),
            P(None, ("seq", "head"), None),
        ),
        out_specs=(
            P(None, ("seq", "head"), None),
            P(None, ("seq", "head"), None),
            P(("seq", "head")),
            P(("seq", "head")),
            P(("seq", "head"), None),
            P(("seq", "head")),
            P(("seq", "head"), None),
            P(("seq", "head")),
            P(("seq", "head"), None),
            P(("seq", "head")),
            P(("seq", "head"), None),
            P(("seq", "head")),
        ),
        check_vma=False,
    )
```
